256 devices in a mesh: head: 4 (over y_lo, core), seq: 64 (over y_hi, z, x).
Axes of the slice: x: 4, y: 4 (y_hi: 2, y_lo: 2; y = y_hi * 2 + y_lo), z: 8, core: 2. Of those that a mesh axis runs over, the one named last changes fastest.
Arguments:
- queries: bfloat16 [4, 8192, 256], P('head', 'seq'), may hold values from -6 to 6
- key_rows: bfloat16 [4, 8192, 256], P('head', 'seq'), may hold values from -6 to 6
- value_rows: bfloat16 [4, 8192, 256], P('head', 'seq'), may hold values from -6 to 6
- out_grad: bfloat16 [4, 8192, 256], P('head', 'seq'), may hold values from -6 to 6
- step_sizes: float32 [4, 8192], P('head', 'seq'), may hold values from 0.0001 to 0.0004
- norm_gain: float32 [4, 256], P('head'), may hold values from 0.1 to 1.9
- gate_init: bfloat16 [4, 256, 768], P('head', 'seq'), may hold values from -0.90625 to 0.90625
- up_init: bfloat16 [4, 256, 768], P('head', 'seq'), may hold values from -0.90625 to 0.90625
- down_init: bfloat16 [4, 256, 768], P('head', 'seq'), may hold values from -0.90625 to 0.90625
- gate_saved: bfloat16 [4, 256, 768], P('head', 'seq'), may hold values from -0.90625 to 0.90625
- up_saved: bfloat16 [4, 256, 768], P('head', 'seq'), may hold values from -0.90625 to 0.90625
- down_saved: bfloat16 [4, 256, 768], P('head', 'seq'), may hold values from -0.90625 to 0.90625
Outputs:
- grad_queries: bfloat16 [4, 8192, 256], P('head', 'seq')
- grad_keys: bfloat16 [4, 8192, 256], P('head', 'seq')
- grad_values: bfloat16 [4, 8192, 256], P('head', 'seq')
- grad_gate: float32 [4, 256, 768], P('head', 'seq')
- grad_up: float32 [4, 256, 768], P('head', 'seq')
- grad_down: float32 [4, 256, 768], P('head', 'seq')
The draws below stay inside these ranges and needn't reach their ends.
All inputs are finite; a program needn't handle non-finite values.
Results may differ from the reference program's by a relative error of at most 0.0085.
The reference program's roundings to bfloat16 on the way (of `normed`, `q_hidden`, `out_delta`, `delta_gate`, `cot_bf`, `scaled_values`, `k_hidden` and `back_proj`) count: a program that leaves them out, or rounds other values in their place, can miss the bound.
Values may be sent and summed in bfloat16 or wider, within the bound.
A program may use at most 64 MiB of HBM per device.

```python
import math
import jax
import jax.numpy as jnp
from jax import lax

HEADS = 4
HD = 256
HID = 768
TOKENS = 8192


def fast_weights(key, salt):
    row_key = jax.random.fold_in(jax.random.fold_in(key, 7), 0)
    col_key = jax.random.fold_in(jax.random.fold_in(key, 9), salt)
    base_key = jax.random.fold_in(jax.random.fold_in(key, salt), 0)
    place = jnp.arange(HD, dtype=jnp.float32) / max(HD - 1, 1)
    row_scale = 10.0 ** place[None, :, None] * jnp.exp(jax.random.uniform(row_key, (HEADS, HD, 1), minval=-0.35, maxval=0.35))
    col_scale = jnp.exp(jax.random.uniform(col_key, (HEADS, 1, HID), minval=0.0, maxval=0.3))
    base = jnp.clip(jax.random.normal(base_key, (HEADS, HD, HID)), -4.0, 4.0)
    return (base * row_scale * col_scale / (5.3 * math.sqrt(HD))).astype(jnp.bfloat16)


def draw_gate_init(key, part):
    return fast_weights(key, 11)


def draw_up_init(key, part):
    return fast_weights(key, 12)


def draw_down_init(key, part):
    return fast_weights(key, 13)


def draw_gate_saved(key, part):
    return fast_weights(key, 21)


def draw_up_saved(key, part):
    return fast_weights(key, 22)


def draw_down_saved(key, part):
    return fast_weights(key, 23)


def block_levels(rng, extent, cuts, low, top_value):
    def one(dim, blocks):
        heights = jax.random.uniform(jax.random.fold_in(jax.random.fold_in(rng, 6), dim), (blocks,), jnp.float32, low / len(cuts), top_value / len(cuts))
        return jnp.repeat(jnp.exp(heights), extent[dim] // blocks).reshape((-1,) + (1,) * (len(extent) - dim - 1))

    level = one(*cuts[0])
    for cut in cuts[1:]:
        level = level * one(*cut)
    return level


def scatter_about(stream_key, shape, scale, reach, cuts=(), kind=jnp.bfloat16):
    values = scale * jax.random.normal(stream_key, shape, jnp.float32)
    if cuts:
        values = values * block_levels(stream_key, shape, cuts, -0.22, 0.18)
    return jnp.clip(values, -reach, reach).astype(kind)


def setup_inputs(seed: int = 0) -> dict:
    key_of = jax.random.split(jax.random.key(seed), 13)
    return {
        "queries": scatter_about(key_of[0], (HEADS, TOKENS, HD), 1.0, 6.0, ((0, 4), (1, 64))),
        "key_rows": scatter_about(key_of[1], (HEADS, TOKENS, HD), 1.0, 6.0, ((0, 4), (1, 64))),
        "value_rows": scatter_about(key_of[2], (HEADS, TOKENS, HD), 1.0, 6.0, ((0, 4), (1, 64))),
        "out_grad": scatter_about(key_of[3], (HEADS, TOKENS, HD), 1.0, 6.0, ((0, 4), (1, 64))),
        "step_sizes": jnp.clip(jnp.exp(math.log(0.0004) - 1.3862944 * jax.random.uniform(key_of[4], (HEADS, TOKENS), jnp.float32) ** block_levels(key_of[4], (HEADS, TOKENS), ((0, 4), (1, 64)), -0.2, 0.2)), 0.0001, 0.0004),
        "norm_gain": jnp.clip(1.0 + 0.18 * jax.random.normal(key_of[5], (HEADS, HD), jnp.float32), 0.1, 1.9),
        "gate_init": draw_gate_init(jax.random.fold_in(key_of[12], 71), 0),
        "up_init": draw_up_init(jax.random.fold_in(key_of[12], 71), 0),
        "down_init": draw_down_init(jax.random.fold_in(key_of[12], 71), 0),
        "gate_saved": draw_gate_saved(jax.random.fold_in(key_of[12], 71), 0),
        "up_saved": draw_up_saved(jax.random.fold_in(key_of[12], 71), 0),
        "down_saved": draw_down_saved(jax.random.fold_in(key_of[12], 71), 0),
    }


def silu_parts(pre_act):
    sigmoid_val = jax.nn.sigmoid(pre_act)
    silu_val = pre_act * sigmoid_val
    silu_slope = sigmoid_val * (1.0 + pre_act * (1.0 - sigmoid_val))
    silu_bend = sigmoid_val * (1.0 - sigmoid_val) * (2.0 + pre_act * (1.0 - 2.0 * sigmoid_val))
    return (silu_val, silu_slope, silu_bend)

def column_norm(weight):
    return jnp.sqrt(lax.optimization_barrier(jnp.sum(jnp.square(weight.astype(jnp.float32)), axis=0)) + 1e-06)

def matmul_f32(left_op, right_op):
    return jnp.dot(left_op, right_op, preferred_element_type=jnp.float32)

def normed_set(inits, saveds):
    norm_init = [column_norm(weight) for weight in inits]
    norm_saved = [column_norm(weight) for weight in saveds]
    normed = [(saveds[which].astype(jnp.float32) * (norm_init[which] / norm_saved[which])).astype(jnp.bfloat16) for which in range(3)]
    return (normed, norm_init, norm_saved)

def query_forward(parts):
    queries_h, gate_i, up_i, down_i, gate_s, up_s, down_s = parts
    normed, norm_init, norm_saved = normed_set((gate_i, up_i, down_i), (gate_s, up_s, down_s))
    q_gate = matmul_f32(queries_h, normed[0])
    q_up = matmul_f32(queries_h, normed[1])
    q_hidden = (silu_parts(q_gate)[0] * q_up).astype(jnp.bfloat16)
    return matmul_f32(q_hidden, normed[2].T)

def head_backward(parts):
    queries_h, keys_h, values_h, rates_h, delta_h, gate_i, up_i, down_i, gate_s, up_s, down_s = parts
    inits = (gate_i, up_i, down_i)
    saveds = (gate_s, up_s, down_s)
    normed, norm_init, norm_saved = normed_set(inits, saveds)
    q_gate = matmul_f32(queries_h, normed[0])
    q_up = matmul_f32(queries_h, normed[1])
    gate_act, gate_slope, gate_bend = silu_parts(q_gate)
    q_hidden = (gate_act * q_up).astype(jnp.bfloat16)
    delta_hidden = matmul_f32(delta_h, normed[2])
    delta_gate = (delta_hidden * q_up * gate_slope).astype(jnp.bfloat16)
    delta_up = (delta_hidden * gate_act).astype(jnp.bfloat16)
    grad_q = (matmul_f32(delta_gate, normed[0].T) + matmul_f32(delta_up, normed[1].T)).astype(jnp.bfloat16)
    apply_grad = (matmul_f32(queries_h.T, delta_gate), matmul_f32(queries_h.T, delta_up), matmul_f32(delta_h.T, q_hidden))
    col_dot = [lax.optimization_barrier(jnp.sum(saveds[which].astype(jnp.float32) * apply_grad[which], axis=0)) for which in range(3)]
    cot = [apply_grad[which] * (norm_init[which] / norm_saved[which]) - saveds[which].astype(jnp.float32) * (col_dot[which] * norm_init[which] / norm_saved[which] ** 3) for which in range(3)]
    cot_bf = [piece.astype(jnp.bfloat16) for piece in cot]
    direct = [cot[which] + inits[which].astype(jnp.float32) * (col_dot[which] / (norm_init[which] * norm_saved[which])) for which in range(3)]
    k_gate = matmul_f32(keys_h, gate_i)
    k_up = matmul_f32(keys_h, up_i)
    k_act, k_slope, k_bend = silu_parts(k_gate)
    scaled_values = (rates_h[:, None] * values_h.astype(jnp.float32)).astype(jnp.bfloat16)
    k_proj = matmul_f32(scaled_values, down_i)
    k_hidden = (k_act * k_up).astype(jnp.bfloat16)
    rise_gate = (k_proj * k_up * k_slope).astype(jnp.bfloat16)
    rise_up = (k_proj * k_act).astype(jnp.bfloat16)
    back_gate = matmul_f32(keys_h, cot_bf[0])
    back_up = matmul_f32(keys_h, cot_bf[1])
    back_hidden = matmul_f32(scaled_values, cot_bf[2])
    back_proj = (back_gate * k_up * k_slope + back_up * k_act).astype(jnp.bfloat16)
    back_kup = (back_gate * k_proj * k_slope + back_hidden * k_act).astype(jnp.bfloat16)
    back_kgate = (back_gate * k_proj * k_up * k_bend + (back_up * k_proj + back_hidden * k_up) * k_slope).astype(jnp.bfloat16)
    grad_k = (matmul_f32(rise_gate, cot_bf[0].T) + matmul_f32(rise_up, cot_bf[1].T) + matmul_f32(back_kgate, gate_i.T) + matmul_f32(back_kup, up_i.T)).astype(jnp.bfloat16)
    grad_v = (rates_h[:, None] * (matmul_f32(k_hidden, cot_bf[2].T) + matmul_f32(back_proj, down_i.T))).astype(jnp.bfloat16)
    grad_g = direct[0] + matmul_f32(keys_h.T, back_kgate)
    grad_u = direct[1] + matmul_f32(keys_h.T, back_kup)
    grad_d = direct[2] + matmul_f32(scaled_values.T, back_proj)
    return (grad_q, grad_k, grad_v, grad_g, grad_u, grad_d)

def reference(queries, key_rows, value_rows, out_grad, step_sizes, norm_gain, gate_init, up_init, down_init, gate_saved, up_saved, down_saved):
    apply_out = lax.map(query_forward, (queries, gate_init, up_init, down_init, gate_saved, up_saved, down_saved))
    full_width = HEADS * HD
    gain_rows = norm_gain[:, None, :]
    grad_f32 = out_grad.astype(jnp.float32)
    mean_square = lax.optimization_barrier(jnp.sum(jnp.square(apply_out), axis=(0, 2))) / full_width
    gain_dot = lax.optimization_barrier(jnp.sum(apply_out * gain_rows * grad_f32, axis=(0, 2))) / full_width
    root = jnp.sqrt(mean_square + 1e-05)[None, :, None]
    out_delta = (gain_rows * grad_f32 / root - apply_out * gain_dot[None, :, None] / root ** 3).astype(jnp.bfloat16)
    results = lax.map(head_backward, (queries, key_rows, value_rows, step_sizes, out_delta, gate_init, up_init, down_init, gate_saved, up_saved, down_saved))
    return (results[0], results[1], results[2], results[3], results[4], results[5])
```

```python
import jax
import jax.numpy as jnp
from jax import lax
from jax.experimental import pallas as pl
from jax.experimental.pallas import tpu as pltpu
from jax.sharding import PartitionSpec as P

HEADS = 4
HD = 256
HID = 768
HALF = HID // 2
W3 = 3 * HALF
NX = 4
NZ = 8
TB = 128
TT = 2 * TB
SPLIT = 896
MESH = pl.DeviceIdType.MESH
F32 = jnp.float32
BF16 = jnp.bfloat16

NN = (((1,), (0,)), ((), ()))
NT = (((1,), (1,)), ((), ()))
TN = (((0,), (0,)), ((), ()))


def dot(a, b, dims=NN):
    return lax.dot_general(a, b, dims, preferred_element_type=F32)


class Sems:
    def __init__(self, ref):
        self.ref = ref
        self.next = 0

    def take(self, count):
        first = self.next
        self.next += count
        assert self.next <= self.ref.shape[0]
        return [self.ref.at[first + i] for i in range(count)]


N_SEMS = 224


def kernel(
    q_in, k_in, v_in, og_in, rate_in, gain_in,
    gi_in, ui_in, di_in, gs_in, us_in, ds_in,
    gq_out, gk_out, gv_out, gg_out, gu_out, gd_out,
    sem_ref,
    wsrc, msrc, vsrc, tq, tk, tv, to, tm,
    g_all, p1, p2, p2t, ini, sav, nrm, vecs,
    f_a, f_b, f_c, act, ups, qh, dgu,
    ap, apr, ao, ss, sr, od, agr, agb,
    s1, rxa1, rzb1, ta1, tb1, rza1, rxb1,
    s2, rxa2, rzb2, ta2, tb2, rza2, rxb2,
    cot8, c_all, cot,
    k_act, kc1, kc2, kc3, kh, rise, bk, bp,
    xq, xqr, xqo, xqi, xk, xkr, xko, xki, xv, xvr, xvo, xvi,
    fs, fr,
):
    head = lax.axis_index("head")
    seq = lax.axis_index("seq")
    c = lax.rem(head, 2)
    yl = lax.div(head, 2)
    x = lax.rem(seq, NX)
    z = lax.rem(lax.div(seq, NX), NZ)
    yh = lax.div(seq, NX * NZ)
    native = c == yh
    sems = Sems(sem_ref)
    sends = []

    def dev(yh_=None, z_=None, x_=None, yl_=None, c_=None):
        yh_ = yh if yh_ is None else yh_
        z_ = z if z_ is None else z_
        x_ = x if x_ is None else x_
        yl_ = yl if yl_ is None else yl_
        c_ = c if c_ is None else c_
        return {"head": yl_ * 2 + c_, "seq": (yh_ * NZ + z_) * NX + x_}

    def zp(j):
        return lax.rem(z + j, NZ)

    def xp(j):
        return lax.rem(x + j, NX)

    def plane(j):
        y = lax.rem(yh * 2 + yl + j, 4)
        return lax.div(y, 2), lax.rem(y, 2)

    sibling = dev(c_=1 - c)
    swapped = dev(yh_=c, c_=yh)

    def remote(src, dst, send, recv, to_dev):
        return pltpu.make_async_remote_copy(
            src_ref=src, dst_ref=dst, send_sem=send, recv_sem=recv,
            device_id=to_dev, device_id_type=MESH,
        )

    for hf in range(2):
        cols = slice(hf * HALF, (hf + 1) * HALF)
        top = jnp.concatenate([r[:, cols].astype(F32) for r in (gi_in, ui_in, di_in)], axis=1)
        low = jnp.concatenate([r[:, cols].astype(F32) for r in (gs_in, us_in, ds_in)], axis=1)
        wsrc[hf] = jnp.concatenate([top, low], axis=0).astype(BF16)

    barrier = pltpu.get_barrier_semaphore()
    partners = [dev(z_=zp(j)) for j in range(1, NZ)]
    partners += [dev(x_=xp(j)) for j in range(1, NX)]
    for j in range(1, 4):
        a, b = plane(j)
        partners.append(dev(yh_=a, yl_=b))
    partners.append(sibling)
    partners.append(dev(yh_=1 - yh, c_=1 - c))
    for p in partners:
        pl.semaphore_signal(barrier, inc=1, device_id=p, device_id_type=MESH)

    msrc[...] = jnp.zeros_like(msrc)
    msrc[0:1, :] = gain_in[...]
    msrc[1:2, 0:TB] = rate_in[...]
    eye = lax.broadcasted_iota(jnp.int32, (TB, TB), 0) == lax.broadcasted_iota(jnp.int32, (TB, TB), 1)

    def column(row):
        return jnp.sum(jnp.where(eye, jnp.broadcast_to(row, (TB, TB)), 0.0), axis=1, keepdims=True)

    def row_of(col):
        return jnp.sum(jnp.where(eye, jnp.broadcast_to(col, (TB, TB)), 0.0), axis=0, keepdims=True)

    vsrc[...] = (column(rate_in[...]) * v_in[...].astype(F32)).astype(BF16)
    pl.semaphore_wait(barrier, len(partners))

    w_send = sems.take(2)
    w_recv = sems.take(2)
    tok_send = sems.take(5)
    tok_recv = sems.take(5)
    toks = [(q_in, tq), (og_in, to), (msrc, tm), (k_in, tk), (vsrc, tv)]

    def w_copy(hf, b, to_dev):
        return remote(wsrc.at[hf], g_all.at[x, z, b], w_send[0], w_recv[0], to_dev)

    for b in range(2):

        @pl.when(native & (yh == b))
        def _(b=b):
            pltpu.make_async_copy(wsrc.at[c], g_all.at[x, z, b], w_recv[b]).start()
            remote(wsrc.at[1 - c], g_all.at[x, z, b], w_send[0], w_recv[b], sibling).start()

        @pl.when(jnp.logical_not(native) & (yh == b))
        def _(b=b):
            for hf in range(2):
                remote(
                    wsrc.at[hf], g_all.at[x, z, b], w_send[hf], w_recv[b], dev(yh_=c, c_=hf)
                ).start()

    @pl.when(native)
    def _():
        for i, (src, dst) in enumerate(toks):
            pltpu.make_async_copy(src, dst.at[c], tok_recv[i]).start()

    @pl.when(jnp.logical_not(native))
    def _():
        for i, (src, dst) in enumerate(toks):
            remote(src, dst.at[yh], tok_send[i], tok_recv[i], swapped).start()

    ri = lax.broadcasted_iota(jnp.int32, (512, 512), 0)
    ci = lax.broadcasted_iota(jnp.int32, (512, 512), 1)
    want = (
        ((ci >> 2) & 1) * 256 + ((ci >> 3) & 1) * 128 + ((ci >> 4) & 7) * 16 + (ci >> 7) * 4 + (ci & 3)
    )
    p1[...] = jnp.where(ri == want, 1.0, 0.0).astype(BF16)
    ri = lax.broadcasted_iota(jnp.int32, (256, 256), 0)
    ci = lax.broadcasted_iota(jnp.int32, (256, 256), 1)

    def natural(j):
        return ((j >> 2) & 1) * 128 + ((j >> 3) & 7) * 16 + (j >> 6) * 4 + (j & 3)

    p2[...] = jnp.where(ri == natural(ci), 1.0, 0.0).astype(BF16)
    p2t[...] = jnp.where(ci == natural(ri), 1.0, 0.0).astype(BF16)

    a_cols = pl.ds(0, SPLIT)
    b_cols = pl.ds(SPLIT, W3 - SPLIT)

    def gather(buf, own_wait):
        lead = (slice(None),) * (len(buf.shape) - 3)
        a1s, a1r = sems.take(NZ - 1), sems.take(NZ - 1)
        b1s, b1r = sems.take(NX - 1), sems.take(NX - 1)
        a2s, a2r = sems.take(NX - 1), sems.take(NX - 1)
        b2s, b2r = sems.take(NZ - 1), sems.take(NZ - 1)
        own_wait()
        own_a = buf.at[(x, z) + lead + (a_cols,)]
        own_b = buf.at[(x, z) + lead + (b_cols,)]
        b1 = [remote(own_b, own_b, b1s[j - 1], b1r[j - 1], dev(x_=xp(j))) for j in range(1, NX)]
        a1 = [remote(own_a, own_a, a1s[j - 1], a1r[j - 1], dev(z_=zp(j))) for j in range(1, NZ)]
        for cp in b1 + a1:
            cp.start()
        for cp in b1:
            cp.wait_recv()
        row_b = buf.at[(slice(None), z) + lead + (b_cols,)]
        b2 = [remote(row_b, row_b, b2s[j - 1], b2r[j - 1], dev(z_=zp(j))) for j in range(1, NZ)]
        for cp in b2:
            cp.start()
        for cp in a1:
            cp.wait_recv()
        row_a = buf.at[(x, slice(None)) + lead + (a_cols,)]
        a2 = [remote(row_a, row_a, a2s[j - 1], a2r[j - 1], dev(x_=xp(j))) for j in range(1, NX)]
        for cp in a2:
            cp.start()
        sends.extend(b1 + a1 + b2 + a2)
        return a2 + b2

    def scatter_start(buf, rxa, rzb):
        a1s, a1r = sems.take(NX - 1), sems.take(NX - 1)
        b1s, b1r = sems.take(NZ - 1), sems.take(NZ - 1)
        a1 = [
            remote(buf.at[xp(j), :, :, a_cols], rxa.at[j - 1], a1s[j - 1], a1r[j - 1], dev(x_=xp(j)))
            for j in range(1, NX)
        ]
        b1 = [
            remote(buf.at[:, zp(j), :, b_cols], rzb.at[j - 1], b1s[j - 1], b1r[j - 1], dev(z_=zp(j)))
            for j in range(1, NZ)
        ]
        for cp in a1 + b1:
            cp.start()
        sends.extend(a1 + b1)
        return a1, b1

    def scatter_mid(buf, a1, b1, rxa, rzb, ta, tb, rza, rxb):
        a2s, a2r = sems.take(NZ - 1), sems.take(NZ - 1)
        b2s, b2r = sems.take(NX - 1), sems.take(NX - 1)
        for cp in a1:
            cp.wait_recv()

        @pl.loop(0, NZ)
        def _(i):
            total = buf[x, i, :, 0:SPLIT].astype(F32)
            for j in range(NX - 1):
                total += rxa[j, i].astype(F32)
            ta[i] = total.astype(BF16)

        a2 = [remote(ta.at[zp(j)], rza.at[j - 1], a2s[j - 1], a2r[j - 1], dev(z_=zp(j))) for j in range(1, NZ)]
        for cp in a2:
            cp.start()
        for cp in b1:
            cp.wait_recv()

        @pl.loop(0, NX)
        def _(i):
            total = buf[i, z, :, SPLIT:W3].astype(F32)
            for j in range(NZ - 1):
                total += rzb[j, i].astype(F32)
            tb[i] = total.astype(BF16)

        b2 = [remote(tb.at[xp(j)], rxb.at[j - 1], b2s[j - 1], b2r[j - 1], dev(x_=xp(j))) for j in range(1, NX)]
        for cp in b2:
            cp.start()
        sends.extend(a2 + b2)
        return a2, b2

    def scatter_end(a2, b2, ta, tb, rza, rxb):
        for cp in a2:
            cp.wait_recv()
        res_a = ta[z].astype(F32)
        for j in range(NZ - 1):
            res_a += rza[j].astype(F32)
        for cp in b2:
            cp.wait_recv()
        res_b = tb[x].astype(F32)
        for j in range(NX - 1):
            res_b += rxb[j].astype(F32)
        return jnp.concatenate([res_a, res_b], axis=1)

    def w_wait():
        for b in range(2):
            pltpu.make_async_copy(wsrc.at[0], g_all.at[x, z, b], w_recv[b]).wait()

    g_done = gather(g_all, w_wait)

    sib_send = sems.take(5)
    sib_recv = sems.take(5)
    sib = []
    for i, (src, dst) in enumerate(toks):
        pltpu.make_async_copy(src, dst.at[c], tok_recv[i]).wait()
        cp = remote(dst.at[c], dst.at[c], sib_send[i], sib_recv[i], sibling)
        cp.start()
        sib.append(cp)
    for cp in sib:
        cp.wait_recv()
    sends.extend(sib)

    for cp in g_done:
        cp.wait_recv()

    g2 = g_all[...].reshape(512, W3)
    for m in range(3):
        cols = slice(m * HALF, (m + 1) * HALF)
        both = dot(p1[...], g2[:, cols]).astype(BF16)
        ini[:, cols] = both[0:HD]
        sav[:, cols] = both[HD:]

    for m in range(3):
        cols = slice(m * HALF, (m + 1) * HALF)

        def sq_step(i, carry, cols=cols):
            rows = pl.ds(pl.multiple_of(i * 16, 16), 16)
            a = ini[rows, cols].astype(F32)
            b = sav[rows, cols].astype(F32)
            return carry[0] + a * a, carry[1] + b * b

        zero = jnp.zeros((16, HALF), F32)
        sq_i, sq_s = lax.fori_loop(0, 16, sq_step, (zero, zero))
        norm_i = jnp.sqrt(jnp.sum(sq_i, axis=0, keepdims=True) + 1e-06)
        norm_s = jnp.sqrt(jnp.sum(sq_s, axis=0, keepdims=True) + 1e-06)
        ratio = norm_i / norm_s
        vecs[0:1, cols] = ratio
        vecs[1:2, cols] = norm_i / (norm_s * norm_s * norm_s)
        vecs[2:3, cols] = 1.0 / (norm_i * norm_s)

        @pl.loop(0, 16)
        def _(i, cols=cols, ratio=ratio):
            rows = pl.ds(pl.multiple_of(i * 16, 16), 16)
            nrm[rows, cols] = (sav[rows, cols].astype(F32) * ratio).astype(BF16)

    c_g, c_u, c_d = slice(0, HALF), slice(HALF, 2 * HALF), slice(2 * HALF, W3)
    c_gu = slice(0, 2 * HALF)

    q_tok = tq[...].reshape(TT, HD)
    f_a[...] = dot(q_tok, nrm[:, c_g])
    f_b[...] = dot(q_tok, nrm[:, c_u])

    @pl.loop(0, TT // 16)
    def _(i):
        rows = pl.ds(pl.multiple_of(i * 16, 16), 16)
        v = f_a[rows, :]
        up = f_b[rows, :]
        s = jax.nn.sigmoid(v)
        a = v * s
        act[rows, :] = a
        ups[rows, :] = up * (s * (1.0 + v * (1.0 - s)))
        qh[rows, :] = (a * up).astype(BF16)

    ap[...] = dot(qh[...], nrm[:, c_d], NT)
    (aps,), (aprs,) = sems.take(1), sems.take(1)
    ap_cp = remote(ap, apr, aps, aprs, sibling)
    ap_cp.start()
    sends.append(ap_cp)

    k_tok = tk[...].reshape(TT, HD)
    v_tok = tv[...].reshape(TT, HD)

    ap_cp.wait_recv()
    gains = tm[0, 0:1, :]
    for b in range(2):
        rows = slice(b * TB, (b + 1) * TB)
        out = ap[rows, :] + apr[rows, :]
        ao[rows, :] = out
        sq = jnp.sum(out * out, axis=1, keepdims=True)
        gd = jnp.sum(out * gains * to[b].astype(F32), axis=1, keepdims=True)
        ss[0:1, rows] = row_of(sq)
        ss[1:2, rows] = row_of(gd)
    sss, srs = sems.take(3), sems.take(3)
    y_cp = []
    for j in range(1, 4):
        a, b = plane(j)
        y_cp.append(remote(ss, sr.at[j - 1], sss[j - 1], srs[j - 1], dev(yh_=a, yl_=b)))
    for cp in y_cp:
        cp.start()
    sends.extend(y_cp)

    f_a[...] = dot(k_tok, ini[:, c_g])
    f_b[...] = dot(k_tok, ini[:, c_u])
    f_c[...] = dot(v_tok, ini[:, c_d])

    @pl.loop(0, TT // 16)
    def _(i):
        rows = pl.ds(pl.multiple_of(i * 16, 16), 16)
        v = f_a[rows, :]
        up = f_b[rows, :]
        proj = f_c[rows, :]
        s = jax.nn.sigmoid(v)
        a = v * s
        slope = s * (1.0 + v * (1.0 - s))
        bend = s * (1.0 - s) * (2.0 + v * (1.0 - 2.0 * s))
        k_act[rows, :] = a
        kc1[rows, :] = up * slope
        kc2[rows, :] = proj * slope
        kc3[rows, :] = proj * up * bend
        kh[rows, :] = (a * up).astype(BF16)
        rise[rows, 0:HALF] = (proj * up * slope).astype(BF16)
        rise[rows, HALF : 2 * HALF] = (proj * a).astype(BF16)

    for cp in y_cp:
        cp.wait_recv()
    tot = ss[...] + sr[0] + sr[1] + sr[2]
    full = HEADS * HD
    root_row = jnp.sqrt(tot[0:1, :] / full + 1e-05)
    inv_row = 1.0 / root_row
    fac_row = (tot[1:2, :] / full) / (root_row * root_row * root_row)
    for b in range(2):
        rows = slice(b * TB, (b + 1) * TB)
        inv = column(inv_row[:, rows])
        fac = column(fac_row[:, rows])
        od[rows, :] = (gains * to[b].astype(F32) * inv - ao[rows, :] * fac).astype(BF16)

    f_a[...] = dot(od[...], nrm[:, c_d])

    @pl.loop(0, TT // 16)
    def _(i):
        rows = pl.ds(pl.multiple_of(i * 16, 16), 16)
        dh = f_a[rows, :]
        dgu[rows, 0:HALF] = (dh * ups[rows, :]).astype(BF16)
        dgu[rows, HALF : 2 * HALF] = (dh * act[rows, :]).astype(BF16)

    agr[:, c_gu] = dot(q_tok, dgu[...], TN)
    agr[:, c_d] = dot(od[...], qh[...], TN)

    for m in range(3):
        cols = slice(m * HALF, (m + 1) * HALF)

        def cd_step(i, carry, cols=cols):
            rows = pl.ds(pl.multiple_of(i * 16, 16), 16)
            return carry + sav[rows, cols].astype(F32) * agr[rows, cols]

        part = jnp.sum(lax.fori_loop(0, 16, cd_step, jnp.zeros((16, HALF), F32)), axis=0, keepdims=True)
        ratio = vecs[0:1, cols]
        fall = part * vecs[1:2, cols]
        vecs[3:4, cols] = part * vecs[2:3, cols]

        @pl.loop(0, 16)
        def _(i, cols=cols, ratio=ratio, fall=fall):
            rows = pl.ds(pl.multiple_of(i * 16, 16), 16)
            agb[rows, cols] = (agr[rows, cols] * ratio - sav[rows, cols].astype(F32) * fall).astype(BF16)

    s1[...] = dot(p2t[...], agb[...]).astype(BF16).reshape(NX, NZ, 8, W3)
    a1, b1 = scatter_start(s1, rxa1, rzb1)

    def give_back(part, x_send, x_recv, x_out, x_in, scale):
        (s_s,), (s_r,) = sems.take(1), sems.take(1)
        x_send[...] = part.reshape(2, TB, HD)
        cp = remote(x_send.at[1 - c], x_recv, s_s, s_r, sibling)
        cp.start()
        sends.append(cp)
        (o_s,), (o_r,) = sems.take(1), sems.take(1)

        def finish():
            cp.wait_recv()
            total = x_send[c] + x_recv[...]
            if scale:
                total = total * column(tm[c, 1:2, 0:TB])
            x_out[...] = total.astype(BF16)

            @pl.when(native)
            def _():
                pltpu.make_async_copy(x_out, x_in, o_r).start()

            @pl.when(jnp.logical_not(native))
            def _():
                remote(x_out, x_in, o_s, o_r, swapped).start()

        def collect(out):
            pltpu.make_async_copy(x_out, x_in, o_r).wait()
            out[...] = x_in[...]

            @pl.when(jnp.logical_not(native))
            def _():
                remote(x_out, x_in, o_s, o_r, swapped).wait_send()

        return finish, collect

    gq_part = dot(dgu[...], nrm[:, c_gu], NT)
    q_finish, q_collect = give_back(gq_part, xq, xqr, xqo, xqi, False)
    a2, b2 = scatter_mid(s1, a1, b1, rxa1, rzb1, ta1, tb1, rza1, rxb1)
    q_finish()
    cot8[...] = scatter_end(a2, b2, ta1, tb1, rza1, rxb1)
    c_all[x, z] = cot8[...].astype(BF16)
    c_done = gather(c_all, lambda: None)
    for cp in c_done:
        cp.wait_recv()
    cot[...] = dot(p2[...], c_all[...].reshape(HD, W3)).astype(BF16)

    f_a[...] = dot(k_tok, cot[:, c_g])
    f_b[...] = dot(k_tok, cot[:, c_u])
    f_c[...] = dot(v_tok, cot[:, c_d])

    @pl.loop(0, TT // 16)
    def _(i):
        rows = pl.ds(pl.multiple_of(i * 16, 16), 16)
        bg = f_a[rows, :]
        bu = f_b[rows, :]
        bh = f_c[rows, :]
        a = k_act[rows, :]
        c1 = kc1[rows, :]
        c2 = kc2[rows, :]
        bp[rows, :] = (bg * c1 + bu * a).astype(BF16)
        bk[rows, HALF : 2 * HALF] = (bg * c2 + bh * a).astype(BF16)
        bk[rows, 0:HALF] = (bg * kc3[rows, :] + (bu * c2 + bh * c1)).astype(BF16)

    agr[:, c_gu] = dot(k_tok, bk[...], TN)
    agr[:, c_d] = dot(v_tok, bp[...], TN)
    for m in range(3):
        cols = slice(m * HALF, (m + 1) * HALF)
        extra = vecs[3:4, cols]

        @pl.loop(0, 16)
        def _(i, cols=cols, extra=extra):
            rows = pl.ds(pl.multiple_of(i * 16, 16), 16)
            agb[rows, cols] = (agr[rows, cols] + ini[rows, cols].astype(F32) * extra).astype(BF16)

    s2[...] = dot(p2t[...], agb[...]).astype(BF16).reshape(NX, NZ, 8, W3)
    a1, b1 = scatter_start(s2, rxa2, rzb2)

    gk_part = dot(rise[...], cot[:, c_gu], NT) + dot(bk[...], ini[:, c_gu], NT)
    k_finish, k_collect = give_back(gk_part, xk, xkr, xko, xki, False)
    gv_part = dot(kh[...], cot[:, c_d], NT) + dot(bp[...], ini[:, c_d], NT)
    v_finish, v_collect = give_back(gv_part, xv, xvr, xvo, xvi, True)
    k_finish()
    v_finish()
    a2, b2 = scatter_mid(s2, a1, b1, rxa2, rzb2, ta2, tb2, rza2, rxb2)
    q_collect(gq_out)
    fin = scatter_end(a2, b2, ta2, tb2, rza2, rxb2) + cot8[...]
    fs[0] = fin[0:4]
    fs[1] = fin[4:8]
    f_send = sems.take(2)
    f_recv = sems.take(2)
    for hc in range(2):

        @pl.when(c == hc)
        def _(hc=hc):
            @pl.when(native)
            def _():
                pltpu.make_async_copy(fs.at[yh], fr.at[hc], f_recv[hc]).start()

            @pl.when(jnp.logical_not(native))
            def _():
                remote(fs.at[yh], fr.at[hc], f_send[0], f_recv[hc], sibling).start()

            remote(fs.at[1 - yh], fr.at[hc], f_send[1], f_recv[hc], dev(yh_=1 - yh, c_=yh)).start()

    k_collect(gk_out)
    v_collect(gv_out)
    for hc in range(2):
        pltpu.make_async_copy(fs.at[0], fr.at[hc], f_recv[hc]).wait()
        cols = slice(hc * HALF, (hc + 1) * HALF)
        for m, out in enumerate((gg_out, gu_out, gd_out)):
            out[:, cols] = fr[hc, :, m * HALF : (m + 1) * HALF]

    for cp in sends:
        cp.wait_send()

    def sent(src, dst, sem):
        remote(src, dst, sem, f_recv[0], sibling).wait_send()

    @pl.when(native)
    def _():
        sent(wsrc.at[0], g_all.at[x, z, 0], w_send[0])

    @pl.when(jnp.logical_not(native))
    def _():
        for hf in range(2):
            sent(wsrc.at[0], g_all.at[x, z, 0], w_send[hf])
        for i, (src, dst) in enumerate(toks):
            sent(src, dst.at[0], tok_send[i])
        sent(fs.at[0], fr.at[0], f_send[0])

    sent(fs.at[0], fr.at[0], f_send[1])


def local(*args):
    (queries, key_rows, value_rows, out_grad, step_sizes, norm_gain, gate_init, up_init, down_init,
     gate_saved, up_saved, down_saved) = args
    ins = [a[0] for a in (queries, key_rows, value_rows, out_grad)]
    ins += [step_sizes, norm_gain]
    ins += [a[0] for a in (gate_init, up_init, down_init, gate_saved, up_saved, down_saved)]
    outs = [jax.ShapeDtypeStruct((TB, HD), BF16)] * 3 + [jax.ShapeDtypeStruct((4, HID), F32)] * 3

    def v(shape, dtype):
        return pltpu.VMEM(shape, dtype)

    wb = W3 - SPLIT
    rs_bufs = [
        v((NX, NZ, 8, W3), BF16),
        v((NX - 1, NZ, 8, SPLIT), BF16),
        v((NZ - 1, NX, 8, wb), BF16),
        v((NZ, 8, SPLIT), BF16),
        v((NX, 8, wb), BF16),
        v((NZ - 1, 8, SPLIT), BF16),
        v((NX - 1, 8, wb), BF16),
    ]
    ret_bufs = [v((2, TB, HD), F32), v((TB, HD), F32), v((TB, HD), BF16), v((TB, HD), BF16)]
    scratch = [
        pltpu.SemaphoreType.DMA((N_SEMS,)),
        v((2, 8, W3), BF16), v((8, HD), F32), v((TB, HD), BF16),
        v((2, TB, HD), BF16), v((2, TB, HD), BF16), v((2, TB, HD), BF16), v((2, TB, HD), BF16),
        v((2, 8, HD), F32),
        v((NX, NZ, 2, 8, W3), BF16), v((512, 512), BF16), v((256, 256), BF16), v((256, 256), BF16),
        v((HD, W3), BF16), v((HD, W3), BF16), v((HD, W3), BF16), v((8, W3), F32),
        v((TT, HALF), F32), v((TT, HALF), F32), v((TT, HALF), F32),
        v((TT, HALF), F32), v((TT, HALF), F32), v((TT, HALF), BF16), v((TT, 2 * HALF), BF16),
        v((TT, HD), F32), v((TT, HD), F32), v((TT, HD), F32), v((8, TT), F32), v((3, 8, TT), F32),
        v((TT, HD), BF16), v((HD, W3), F32), v((HD, W3), BF16),
        *rs_bufs, *rs_bufs,
        v((8, W3), F32), v((NX, NZ, 8, W3), BF16), v((HD, W3), BF16),
        v((TT, HALF), F32), v((TT, HALF), F32), v((TT, HALF), F32), v((TT, HALF), F32),
        v((TT, HALF), BF16), v((TT, 2 * HALF), BF16), v((TT, 2 * HALF), BF16), v((TT, HALF), BF16),
        *ret_bufs, *ret_bufs, *ret_bufs,
        v((2, 4, W3), F32), v((2, 4, W3), F32),
    ]
    vm = pl.BlockSpec(memory_space=pltpu.VMEM)
    res = pl.pallas_call(
        kernel,
        out_shape=outs,
        in_specs=[vm] * len(ins),
        out_specs=[vm] * len(outs),
        scratch_shapes=scratch,
        compiler_params=pltpu.CompilerParams(
            collective_id=0, has_side_effects=True, vmem_limit_bytes=60 * 1024 * 1024
        ),
    )(*ins)
    return tuple(r[None] for r in res)


def solution(mesh):
    three = P("head", "seq", None)
    return jax.shard_map(
        local,
        mesh=mesh,
        in_specs=(three, three, three, three, P("head", "seq"), P("head", None)) + (three,) * 6,
        out_specs=(three,) * 6,
        check_vma=False,
    )
```

```python
import jax
import jax.numpy as jnp
from jax import lax
from jax.experimental import pallas as pl
from jax.experimental.pallas import tpu as pltpu
from jax.sharding import PartitionSpec as P

HEADS = 4
HD = 256
HID = 768
HALF = HID // 2
W3 = 3 * HALF
NX = 4
NZ = 8
TB = 128
TT = 2 * TB
MESH = pl.DeviceIdType.MESH
F32 = jnp.float32
BF16 = jnp.bfloat16

NN = (((1,), (0,)), ((), ()))
NT = (((1,), (1,)), ((), ()))
TN = (((0,), (0,)), ((), ()))

GATE = (0, 384, "z")
UP = (384, 384, "z")
DOWN_A = (768, 128, "z")
DOWN_B = (896, 256, "x")
STREAMS = (GATE, UP, DOWN_A, DOWN_B)
N_SEMS = 224


def dot(a, b, dims=NN):
    return lax.dot_general(a, b, dims, preferred_element_type=F32)


class Sems:
    def __init__(self, ref):
        self.ref = ref
        self.next = 0

    def take(self):
        self.next += 1
        assert self.next <= self.ref.shape[0]
        return self.ref.at[self.next - 1]

    def many(self, count):
        return [self.take() for _ in range(count)]


def wait_for(ref, sem):
    pltpu.make_async_copy(ref, ref, sem).wait()


def loop16(body):
    @pl.loop(0, 16)
    def _(i):
        body(i, pl.ds(pl.multiple_of(i * 16, 16), 16))


def block(buf, i, cols):
    v = buf[lax.div(i, 4), pl.ds(lax.rem(i, 4) * 2, 2), :, cols]
    return v.astype(F32).reshape(16, v.shape[-1])


def set_block(buf, i, cols, value):
    buf[lax.div(i, 4), pl.ds(lax.rem(i, 4) * 2, 2), :, cols] = value.reshape(2, 8, value.shape[-1]).astype(BF16)


def kernel(*refs):
    refs = list(refs)

    def grab(n):
        out = refs[:n]
        del refs[:n]
        return out

    in_hbm = grab(12)
    gq_out, gk_out, gv_out, gg_out, gu_out, gd_out = grab(6)
    (sem_ref,) = grab(1)
    q_in, k_in, v_in, og_in, rate_in, gain_in = in_vmem = grab(6)
    w_in = grab(6)
    in_vmem = in_vmem + w_in
    wsrc, stage, msrc, vsrc = grab(4)
    tq, tk, tv, to, tm = grab(5)
    qp, kp, vp, op, gp = grab(5)
    sv_all, in_all, c_all = grab(3)
    sq_z, sq_x, p2, ini, nrm, vecs, cot = grab(7)
    f_a, f_b, f_c, act, ups, qh, dgu = grab(7)
    ap, apr, ao, ss, sr, od, agr = grab(7)
    s1, s2 = grab(2)
    rs1 = [grab(3) for _ in STREAMS]
    rs2 = [grab(3) for _ in STREAMS]
    k_act, kc1, kc2, kc3, kh, rise, bk, bp = grab(8)
    rets = [grab(4) for _ in range(3)]
    fs, fr = grab(2)
    assert not refs

    head = lax.axis_index("head")
    seq = lax.axis_index("seq")
    c = lax.rem(head, 2)
    yl = lax.div(head, 2)
    x = lax.rem(seq, NX)
    z = lax.rem(lax.div(seq, NX), NZ)
    yh = lax.div(seq, NX * NZ)
    native = c == yh
    foreign = jnp.logical_not(native)
    sems = Sems(sem_ref)
    at_end = []

    def dev(yh_=None, z_=None, x_=None, yl_=None, c_=None):
        yh_ = yh if yh_ is None else yh_
        z_ = z if z_ is None else z_
        x_ = x if x_ is None else x_
        yl_ = yl if yl_ is None else yl_
        c_ = c if c_ is None else c_
        return {"head": yl_ * 2 + c_, "seq": (yh_ * NZ + z_) * NX + x_}

    def zp(j):
        return lax.rem(z + j, NZ)

    def xp(j):
        return lax.rem(x + j, NX)

    def plane(j):
        y = lax.rem(yh * 2 + yl + j, 4)
        return lax.div(y, 2), lax.rem(y, 2)

    sibling = dev(c_=1 - c)
    swapped = dev(yh_=c, c_=yh)

    def send(src, dst, s_sem, r_sem, to_dev):
        pltpu.make_async_remote_copy(
            src_ref=src, dst_ref=dst, send_sem=s_sem, recv_sem=r_sem,
            device_id=to_dev, device_id_type=MESH,
        ).start()

    def keep(src, dst, sem):
        pltpu.make_async_copy(src, dst, sem).start()

    in_sems = sems.many(12)
    for i in (6, 7, 8, 9, 10, 11, 4, 5, 2, 0, 3, 1):
        keep(in_hbm[i], in_vmem[i], in_sems[i])

    def in_ready(*which):
        for i in which:
            wait_for(in_vmem[i], in_sems[i])

    barrier = pltpu.get_barrier_semaphore()
    partners = [dev(z_=zp(j)) for j in range(1, NZ)]
    partners += [dev(x_=xp(j)) for j in range(1, NX)]
    for j in range(1, 4):
        a, b = plane(j)
        partners.append(dev(yh_=a, yl_=b))
    partners.append(sibling)
    partners.append(dev(yh_=1 - yh, c_=1 - c))
    for p in partners:
        pl.semaphore_signal(barrier, inc=1, device_id=p, device_id_type=MESH)
    with jax.named_scope("w_in"):
        in_ready(6, 7, 8, 9, 10, 11)
    for hf in range(2):
        cols = slice(hf * HALF, (hf + 1) * HALF)
        top = jnp.concatenate([r[:, cols].astype(F32) for r in w_in[:3]], axis=1)
        low = jnp.concatenate([r[:, cols].astype(F32) for r in w_in[3:]], axis=1)
        wsrc[hf] = jnp.concatenate([top, low], axis=0).astype(BF16)

    eye = lax.broadcasted_iota(jnp.int32, (TB, TB), 0) == lax.broadcasted_iota(jnp.int32, (TB, TB), 1)

    def column(row):
        return jnp.sum(jnp.where(eye, jnp.broadcast_to(row, (TB, TB)), 0.0), axis=1, keepdims=True)

    def row_of(col):
        return jnp.sum(jnp.where(eye, jnp.broadcast_to(col, (TB, TB)), 0.0), axis=0, keepdims=True)

    in_ready(4, 5, 2, 0, 3, 1)
    msrc[...] = jnp.zeros_like(msrc)
    msrc[0:1, :] = gain_in[...]
    msrc[1:2, 0:TB] = rate_in[...]
    vsrc[...] = (column(rate_in[...]) * v_in[...].astype(F32)).astype(BF16)
    ri = lax.broadcasted_iota(jnp.int32, (HD, HD), 0)
    ci = lax.broadcasted_iota(jnp.int32, (HD, HD), 1)
    natural = ((ci >> 2) & 1) * 128 + ((ci >> 3) & 7) * 16 + (ci >> 6) * 4 + (ci & 3)
    p2[...] = jnp.where(ri == natural, 1.0, 0.0).astype(BF16)
    with jax.named_scope("barrier"):
        pl.semaphore_wait(barrier, len(partners))

    w_send = sems.many(2)
    w_recv = sems.many(2)
    tok_send = sems.many(5)
    tok_recv = sems.many(5)
    toks = [(q_in, tq), (msrc, tm), (og_in, to), (k_in, tk), (vsrc, tv)]
    for b in range(2):

        @pl.when(native & (yh == b))
        def _(b=b):
            keep(wsrc.at[c], stage.at[b], w_recv[b])
            send(wsrc.at[1 - c], stage.at[b], w_send[0], w_recv[b], sibling)

        @pl.when(foreign & (yh == b))
        def _(b=b):
            for hf in range(2):
                send(wsrc.at[hf], stage.at[b], w_send[hf], w_recv[b], dev(yh_=c, c_=hf))

    @pl.when(native)
    def _():
        for i, (src, dst) in enumerate(toks):
            keep(src, dst.at[c], tok_recv[i])

    @pl.when(foreign)
    def _():
        for i, (src, dst) in enumerate(toks):
            send(src, dst.at[yh], tok_send[i], tok_recv[i], swapped)

    sib_send = sems.many(5)
    sib_recv = sems.many(5)

    def tok_forward(i):
        src, dst = toks[i]
        wait_for(dst.at[0], tok_recv[i])
        send(dst.at[c], dst.at[c], sib_send[i], sib_recv[i], sibling)
        at_end.append((dst.at[0], sib_send[i]))

    def tok_ready(i):
        wait_for(toks[i][1].at[0], sib_recv[i])

    class Gather:
        def __init__(self, buf, stream):
            first, n, axis = stream
            self.buf, self.cols, self.axis = buf, pl.ds(first, n), axis
            self.s1, self.r1, self.s2, self.r2 = sems.many(4)

        def start(self):
            own = self.buf.at[x, z, :, self.cols]
            if self.axis == "z":
                for j in range(1, NZ):
                    send(own, own, self.s1, self.r1, dev(z_=zp(j)))
                self.all1 = self.buf.at[0, 0 : NZ - 1, :, self.cols]
            else:
                for j in range(1, NX):
                    send(own, own, self.s1, self.r1, dev(x_=xp(j)))
                self.all1 = self.buf.at[0, 0 : NX - 1, :, self.cols]
            at_end.append((self.all1, self.s1))

        def mid(self):
            wait_for(self.all1, self.r1)
            if self.axis == "z":
                part = self.buf.at[x, :, :, self.cols]
                for j in range(1, NX):
                    send(part, part, self.s2, self.r2, dev(x_=xp(j)))
                self.all2 = self.buf.at[0 : NX - 1, :, :, self.cols]
            else:
                part = self.buf.at[:, z, :, self.cols]
                for j in range(1, NZ):
                    send(part, part, self.s2, self.r2, dev(z_=zp(j)))
                self.all2 = self.buf.at[:, 0 : NZ - 1, :, self.cols]
            at_end.append((self.all2, self.s2))

        def end(self):
            wait_for(self.all2, self.r2)

    class Scatter:
        def __init__(self, buf, stream, bufs, owners=False):
            first, n, axis = stream
            self.buf, self.cols, self.axis, self.owners = buf, slice(first, first + n), axis, owners
            self.got1, self.mine, self.got2 = bufs
            self.s1, self.r1, self.s2, self.r2 = sems.many(4)
            if owners:
                self.l2 = sems.take()

        def start(self):
            cols = pl.ds(self.cols.start, self.cols.stop - self.cols.start)
            if self.axis == "z":
                for j in range(1, NX):
                    send(self.buf.at[xp(j), :, :, cols], self.got1.at[j - 1], self.s1, self.r1, dev(x_=xp(j)))
            else:
                for j in range(1, NZ):
                    send(self.buf.at[:, zp(j), :, cols], self.got1.at[j - 1], self.s1, self.r1, dev(z_=zp(j)))
            at_end.append((self.got1, self.s1))

        def mid(self):
            wait_for(self.got1, self.r1)
            count = NZ if self.axis == "z" else NX

            @pl.loop(0, count)
            def _(i):
                if self.axis == "z":
                    total = self.buf[x, i, :, self.cols].astype(F32)
                else:
                    total = self.buf[i, z, :, self.cols].astype(F32)
                for j in range(self.got1.shape[0]):
                    total += self.got1[j, i].astype(F32)
                if self.owners:
                    self.mine[i, 0] = total[0:4].astype(BF16)
                    self.mine[i, 1] = total[4:8].astype(BF16)
                else:
                    self.mine[i] = total.astype(BF16)

            if not self.owners:
                for j in range(1, count):
                    if self.axis == "z":
                        send(self.mine.at[zp(j)], self.got2.at[j - 1], self.s2, self.r2, dev(z_=zp(j)))
                    else:
                        send(self.mine.at[xp(j)], self.got2.at[j - 1], self.s2, self.r2, dev(x_=xp(j)))
                at_end.append((self.got2, self.s2))
                return
            for j in range(count):
                for b in range(2):
                    if self.axis == "z":
                        src, to_dev = self.mine.at[zp(j), b], dev(yh_=b, z_=zp(j), c_=yh)
                    else:
                        src, to_dev = self.mine.at[xp(j), b], dev(yh_=b, x_=xp(j), c_=yh)
                    if j > 0:
                        send(src, self.got2.at[c, j], self.s2, self.r2, to_dev)
                        continue
                    here = native & (yh == b)

                    @pl.when(here)
                    def _(src=src, j=j):
                        keep(src, self.got2.at[c, j], self.r2)

                    @pl.when(jnp.logical_not(here))
                    def _(src=src, j=j, to_dev=to_dev):
                        send(src, self.got2.at[c, j], self.s2, self.r2, to_dev)

        def end(self):
            wait_for(self.got2, self.r2)
            if self.owners:
                for hc in range(2):
                    total = fr[hc, :, self.cols]
                    for j in range(self.got2.shape[1]):
                        total += self.got2[hc, j].astype(F32)
                    first = self.cols.start
                    m = first // HALF
                    lo = first - m * HALF + hc * HALF
                    (gg_out, gu_out, gd_out)[m][:, lo : lo + self.cols.stop - first] = total
                return None
            total = self.mine[z if self.axis == "z" else x].astype(F32)
            for j in range(self.got2.shape[0]):
                total += self.got2[j].astype(F32)
            return total

        def sent(self):
            count = NZ if self.axis == "z" else NX

            @pl.when(native)
            def _():
                wait_for(self.got2.at[0, 0 : count - 1], self.s2)

            @pl.when(foreign)
            def _():
                wait_for(self.got2.at[0, 0:1], self.s2)
                wait_for(self.got2.at[0, 0 : count - 1], self.s2)

            wait_for(self.got2.at[0, 0:count], self.s2)

    sv_g = {s: Gather(sv_all, s) for s in STREAMS}
    in_g = {s: Gather(in_all, s) for s in STREAMS}
    c_g = {s: Gather(c_all, s) for s in STREAMS}
    sc1 = {s: Scatter(s1, s, rs1[i]) for i, s in enumerate(STREAMS)}
    sc2 = {s: Scatter(s2, s, rs2[i], True) for i, s in enumerate(STREAMS)}

    with jax.named_scope("w_rows"):
        for b in range(2):
            wait_for(stage.at[0], w_recv[b])
    got = [stage[b].astype(F32) for b in range(2)]
    sv_all[x, z] = jnp.concatenate([got[0][4:8], got[1][4:8]], axis=0).astype(BF16)
    order_g = (GATE, UP, DOWN_B, DOWN_A)
    for s in order_g:
        sv_g[s].start()
    init8 = jnp.concatenate([got[0][0:4], got[1][0:4]], axis=0)
    in_all[x, z] = init8.astype(BF16)
    sq_z[z] = jnp.sum(init8 * init8, axis=0, keepdims=True)
    sq_s1, sq_r1, sq_s2, sq_r2 = sems.many(4)
    for j in range(1, NZ):
        send(sq_z.at[z], sq_z.at[z], sq_s1, sq_r1, dev(z_=zp(j)))
    at_end.append((sq_z.at[0 : NZ - 1], sq_s1))

    with jax.named_scope("w_tok1"):
        for i in range(3):
            tok_forward(i)
    with jax.named_scope("w_sv_mid"):
        for s in order_g:
            sv_g[s].mid()
            if s is GATE:
                wait_for(sq_z.at[0 : NZ - 1], sq_r1)
                total = sq_z[0]
                for j in range(1, NZ):
                    total += sq_z[j]
                sq_x[x] = total
                for j in range(1, NX):
                    send(sq_x.at[x], sq_x.at[x], sq_s2, sq_r2, dev(x_=xp(j)))
                at_end.append((sq_x.at[0 : NX - 1], sq_s2))
    for s in STREAMS:
        in_g[s].start()

    def permuted(src, dst):
        dst[...] = dot(src[...].reshape(TT, HD), p2[...]).astype(BF16)

    with jax.named_scope("w_tok2"):
        for i in range(3):
            tok_ready(i)
    permuted(tq, qp)
    permuted(to, op)
    gains_nat = tm[0, 0:1, :]
    gcol = jnp.concatenate([column(gains_nat[:, 0:TB]), column(gains_nat[:, TB:])], axis=0)
    gp[...] = jnp.sum(p2[...].astype(F32) * gcol, axis=0, keepdims=True)
    with jax.named_scope("w_tok3"):
        for i in range(3, 5):
            tok_forward(i)

    with jax.named_scope("w_sq"):
        wait_for(sq_x.at[0 : NX - 1], sq_r2)
    sq_init = sq_x[0] + sq_x[1] + sq_x[2] + sq_x[3]
    norm_init = jnp.sqrt(sq_init + 1e-06)

    def normalize(m):
        cols = slice(m * HALF, (m + 1) * HALF)

        def step(i, carry):
            a = block(sv_all, i, cols)
            return carry + a * a

        sq = jnp.sum(lax.fori_loop(0, 16, step, jnp.zeros((16, HALF), F32)), axis=0, keepdims=True)
        norm_i = norm_init[:, cols]
        norm_s = jnp.sqrt(sq + 1e-06)
        ratio = norm_i / norm_s
        vecs[0:1, cols] = ratio
        vecs[1:2, cols] = norm_i / (norm_s * norm_s * norm_s)
        vecs[2:3, cols] = 1.0 / (norm_i * norm_s)

        def body(i, rows):
            nrm[rows, cols] = (block(sv_all, i, cols) * ratio).astype(BF16)

        loop16(body)

    c_0, c_1, c_2 = (slice(m * HALF, (m + 1) * HALF) for m in range(3))
    c_01 = slice(0, 2 * HALF)

    with jax.named_scope("w_sv_gate"):
        sv_g[GATE].end()
    normalize(0)
    f_a[...] = dot(qp[...], nrm[:, c_0])
    with jax.named_scope("w_sv_up"):
        sv_g[UP].end()
    normalize(1)
    f_b[...] = dot(qp[...], nrm[:, c_1])

    def q_body(i, rows):
        v = f_a[rows, :]
        up = f_b[rows, :]
        s = jax.nn.sigmoid(v)
        a = v * s
        act[rows, :] = a
        ups[rows, :] = up * (s * (1.0 + v * (1.0 - s)))
        qh[rows, :] = (a * up).astype(BF16)

    loop16(q_body)
    with jax.named_scope("w_sv_down"):
        sv_g[DOWN_A].end()
        sv_g[DOWN_B].end()
    normalize(2)
    ap[...] = dot(qh[...], nrm[:, c_2], NT)
    aps, aprs = sems.many(2)
    send(ap, apr, aps, aprs, sibling)
    at_end.append((ap, aps))
    with jax.named_scope("w_in_mid"):
        for s in STREAMS:
            in_g[s].mid()

    gains = gp[...]
    with jax.named_scope("w_ap"):
        wait_for(apr, aprs)
    for b in range(2):
        rows = slice(b * TB, (b + 1) * TB)
        out = ap[rows, :] + apr[rows, :]
        ao[rows, :] = out
        ss[0:1, rows] = row_of(jnp.sum(out * out, axis=1, keepdims=True))
        ss[1:2, rows] = row_of(jnp.sum(out * gains * op[rows, :].astype(F32), axis=1, keepdims=True))
    ss_s, ss_r = sems.many(2)
    for j in range(1, 4):
        a, b = plane(j)
        send(ss, sr.at[j - 1], ss_s, ss_r, dev(yh_=a, yl_=b))
    at_end.append((sr, ss_s))
    with jax.named_scope("w_tok4"):
        for i in range(3, 5):
            tok_ready(i)
    permuted(tk, kp)
    permuted(tv, vp)

    with jax.named_scope("w_sums"):
        wait_for(sr, ss_r)
    tot = ss[...] + sr[0] + sr[1] + sr[2]
    full = HEADS * HD
    root_row = jnp.sqrt(tot[0:1, :] / full + 1e-05)
    inv_row = 1.0 / root_row
    fac_row = (tot[1:2, :] / full) / (root_row * root_row * root_row)
    for b in range(2):
        rows = slice(b * TB, (b + 1) * TB)
        inv = column(inv_row[:, rows])
        fac = column(fac_row[:, rows])
        od[rows, :] = (gains * op[rows, :].astype(F32) * inv - ao[rows, :] * fac).astype(BF16)

    def project(m, grad):
        cols = slice(m * HALF, (m + 1) * HALF)
        agr[...] = grad

        def step(i, carry):
            return carry + block(sv_all, i, cols) * agr[pl.ds(pl.multiple_of(i * 16, 16), 16), :]

        part = jnp.sum(lax.fori_loop(0, 16, step, jnp.zeros((16, HALF), F32)), axis=0, keepdims=True)
        ratio = vecs[0:1, cols]
        fall = part * vecs[1:2, cols]
        vecs[3:4, cols] = part * vecs[2:3, cols]

        def body(i, rows):
            set_block(s1, i, cols, agr[rows, :] * ratio - block(sv_all, i, cols) * fall)

        loop16(body)

    project(2, dot(od[...], qh[...], TN))
    sc1[DOWN_A].start()
    sc1[DOWN_B].start()
    f_a[...] = dot(od[...], nrm[:, c_2])

    def d_body(i, rows):
        dh = f_a[rows, :]
        dgu[rows, 0:HALF] = (dh * ups[rows, :]).astype(BF16)
        dgu[rows, HALF : 2 * HALF] = (dh * act[rows, :]).astype(BF16)

    loop16(d_body)
    project(0, dot(qp[...], dgu[:, 0:HALF], TN))
    sc1[GATE].start()
    project(1, dot(qp[...], dgu[:, HALF : 2 * HALF], TN))
    sc1[UP].start()

    class Give:
        def __init__(self, bufs, scale):
            self.part, self.got, self.out, self.back = bufs
            self.scale = scale
            self.s1, self.r1, self.s2, self.r2 = sems.many(4)

        def start(self, part):
            self.part[...] = part.reshape(2, TB, HD)
            send(self.part.at[1 - c], self.got, self.s1, self.r1, sibling)
            at_end.append((self.got, self.s1))

        def finish(self):
            wait_for(self.got, self.r1)
            total = self.part[c] + self.got[...]
            if self.scale:
                total = total * column(tm[c, 1:2, 0:TB])
            self.out[...] = dot(total.astype(BF16), p2[...], NT).astype(BF16)

            @pl.when(native)
            def _():
                keep(self.out, self.back, self.r2)

            @pl.when(foreign)
            def _():
                send(self.out, self.back, self.s2, self.r2, swapped)

        def collect(self, out):
            wait_for(self.back, self.r2)
            out[...] = self.back[...]

        def sent(self):
            wait_for(self.back, self.s2)

    give_q, give_k, give_v = (Give(rets[i], i == 2) for i in range(3))
    give_q.start(dot(dgu[...], nrm[:, c_01], NT))
    with jax.named_scope("w_in_end"):
        for s in STREAMS:
            in_g[s].end()
    ini[...] = in_all[...].reshape(HD, W3)
    f_a[...] = dot(kp[...], ini[:, c_0])
    f_b[...] = dot(kp[...], ini[:, c_1])
    f_c[...] = dot(vp[...], ini[:, c_2])

    def k_body(i, rows):
        v = f_a[rows, :]
        up = f_b[rows, :]
        proj = f_c[rows, :]
        s = jax.nn.sigmoid(v)
        a = v * s
        slope = s * (1.0 + v * (1.0 - s))
        bend = s * (1.0 - s) * (2.0 + v * (1.0 - 2.0 * s))
        k_act[rows, :] = a
        kc1[rows, :] = up * slope
        kc2[rows, :] = proj * slope
        kc3[rows, :] = proj * up * bend
        kh[rows, :] = (a * up).astype(BF16)
        rise[rows, 0:HALF] = (proj * up * slope).astype(BF16)
        rise[rows, HALF : 2 * HALF] = (proj * a).astype(BF16)

    loop16(k_body)
    with jax.named_scope("w_sc1_mid"):
        for s in (DOWN_A, DOWN_B, GATE, UP):
            sc1[s].mid()
    give_q.finish()
    for s in (DOWN_A, DOWN_B, GATE, UP):
        with jax.named_scope("w_sc1_end"):
            res = sc1[s].end()
        cols = slice(s[0], s[0] + s[1])
        c_all[x, z, :, cols] = res.astype(BF16)
        c_g[s].start()
        fs[0, :, cols] = res[0:4]
        fs[1, :, cols] = res[4:8]

    f_send = sems.many(2)
    f_recv = sems.many(2)
    for hc in range(2):

        @pl.when(c == hc)
        def _(hc=hc):
            @pl.when(native)
            def _():
                keep(fs.at[yh], fr.at[hc], f_recv[hc])

            @pl.when(foreign)
            def _():
                send(fs.at[yh], fr.at[hc], f_send[0], f_recv[hc], sibling)

            send(fs.at[1 - yh], fr.at[hc], f_send[1], f_recv[hc], dev(yh_=1 - yh, c_=yh))

    with jax.named_scope("w_c_mid"):
        for s in (DOWN_B, DOWN_A, GATE, UP):
            c_g[s].mid()

    def cot_of(m):
        cols = slice(m * HALF, (m + 1) * HALF)
        cot[:, cols] = c_all[:, :, :, cols].reshape(HD, HALF)
        return cot[:, cols]

    with jax.named_scope("w_c_down"):
        c_g[DOWN_A].end()
        c_g[DOWN_B].end()
    f_c[...] = dot(vp[...], cot_of(2))
    with jax.named_scope("w_c_gate"):
        c_g[GATE].end()
    f_a[...] = dot(kp[...], cot_of(0))
    with jax.named_scope("w_c_up"):
        c_g[UP].end()
    f_b[...] = dot(kp[...], cot_of(1))

    def b_body(i, rows):
        bg = f_a[rows, :]
        bu = f_b[rows, :]
        bh = f_c[rows, :]
        a = k_act[rows, :]
        c1 = kc1[rows, :]
        c2 = kc2[rows, :]
        bp[rows, :] = (bg * c1 + bu * a).astype(BF16)
        bk[rows, HALF : 2 * HALF] = (bg * c2 + bh * a).astype(BF16)
        bk[rows, 0:HALF] = (bg * kc3[rows, :] + (bu * c2 + bh * c1)).astype(BF16)

    loop16(b_body)

    def inner(m, grad):
        cols = slice(m * HALF, (m + 1) * HALF)
        extra = vecs[3:4, cols]
        agr[...] = grad

        def body(i, rows):
            set_block(s2, i, cols, agr[rows, :] + ini[rows, cols].astype(F32) * extra)

        loop16(body)

    inner(2, dot(vp[...], bp[...], TN))
    sc2[DOWN_B].start()
    sc2[DOWN_A].start()
    inner(0, dot(kp[...], bk[:, 0:HALF], TN))
    sc2[GATE].start()
    inner(1, dot(kp[...], bk[:, HALF : 2 * HALF], TN))
    sc2[UP].start()
    give_k.start(dot(rise[...], cot[:, c_01], NT) + dot(bk[...], ini[:, c_01], NT))
    give_v.start(dot(kh[...], cot[:, c_2], NT) + dot(bp[...], ini[:, c_2], NT))
    give_k.finish()
    give_v.finish()
    with jax.named_scope("w_sc2_mid"):
        for s in (DOWN_A, DOWN_B, GATE, UP):
            sc2[s].mid()
    with jax.named_scope("w_collect"):
        give_q.collect(gq_out)
        give_k.collect(gk_out)
        give_v.collect(gv_out)
        for hc in range(2):
            wait_for(fr.at[0], f_recv[hc])
    with jax.named_scope("w_sc2_end"):
        for s in (DOWN_A, DOWN_B, GATE, UP):
            sc2[s].end()

    with jax.named_scope("w_sent"):
        for ref, sem in at_end:
            wait_for(ref, sem)
        for s in STREAMS:
            sc2[s].sent()

        @pl.when(native)
        def _():
            wait_for(stage.at[0], w_send[0])

        @pl.when(foreign)
        def _():
            for hf in range(2):
                wait_for(stage.at[0], w_send[hf])
            for i, (src, dst) in enumerate(toks):
                wait_for(dst.at[0], tok_send[i])
            wait_for(fr.at[0], f_send[0])
            for give in (give_q, give_k, give_v):
                give.sent()

        wait_for(fr.at[0], f_send[1])


def write_out(*refs):
    sem = refs[-1]
    half = (len(refs) - 1) // 2
    copies = [pltpu.make_async_copy(refs[i], refs[half + i], sem.at[i]) for i in range(half)]
    for cp in copies:
        cp.start()
    for cp in copies:
        cp.wait()


def local(*args):
    (queries, key_rows, value_rows, out_grad, step_sizes, norm_gain, gate_init, up_init, down_init,
     gate_saved, up_saved, down_saved) = args
    ins = [a[0] for a in (queries, key_rows, value_rows, out_grad)]
    ins += [step_sizes, norm_gain]
    ins += [a[0] for a in (gate_init, up_init, down_init, gate_saved, up_saved, down_saved)]
    shapes = [((TB, HD), BF16)] * 3 + [((4, HID), F32)] * 3

    def v(dtype, *shape):
        return pltpu.VMEM(shape, dtype)

    def rs_bufs(owners):
        out = []
        for _, n, axis in STREAMS:
            if axis == "z":
                first, count = v(BF16, NX - 1, NZ, 8, n), NZ
            else:
                first, count = v(BF16, NZ - 1, NX, 8, n), NX
            if owners:
                out += [first, v(BF16, count, 2, 4, n), v(BF16, 2, count, 4, n)]
            else:
                out += [first, v(BF16, count, 8, n), v(BF16, count - 1, 8, n)]
        return out

    ret = [v(F32, 2, TB, HD), v(F32, TB, HD), v(BF16, TB, HD), v(BF16, TB, HD)]
    scratch = [
        pltpu.SemaphoreType.DMA((N_SEMS,)),
        *[v(a.dtype, *a.shape) for a in ins],
        v(BF16, 2, 8, W3), v(BF16, 2, 8, W3), v(F32, 8, HD), v(BF16, TB, HD),
        *[v(BF16, 2, TB, HD)] * 4, v(F32, 2, 8, HD),
        *[v(BF16, TT, HD)] * 4, v(F32, 1, HD),
        *[v(BF16, NX, NZ, 8, W3)] * 3,
        v(F32, NZ, 1, W3), v(F32, NX, 1, W3), v(BF16, HD, HD),
        v(BF16, HD, W3), v(BF16, HD, W3), v(F32, 8, W3), v(BF16, HD, W3),
        *[v(F32, TT, HALF)] * 5, v(BF16, TT, HALF), v(BF16, TT, 2 * HALF),
        *[v(F32, TT, HD)] * 3, v(F32, 8, TT), v(F32, 3, 8, TT), v(BF16, TT, HD), v(F32, HD, HALF),
        *[v(BF16, NX, NZ, 8, W3)] * 2,
        *rs_bufs(False), *rs_bufs(True),
        *[v(F32, TT, HALF)] * 4, v(BF16, TT, HALF), v(BF16, TT, 2 * HALF), v(BF16, TT, 2 * HALF), v(BF16, TT, HALF),
        *ret * 3,
        v(F32, 2, 4, W3), v(F32, 2, 4, W3),
    ]
    vm = pl.BlockSpec(memory_space=pltpu.VMEM)
    res = pl.pallas_call(
        kernel,
        out_shape=[pltpu.VMEM(s, d) for s, d in shapes],
        in_specs=[pl.BlockSpec(memory_space=pltpu.HBM)] * len(ins),
        out_specs=[vm] * len(shapes),
        scratch_shapes=scratch,
        compiler_params=pltpu.CompilerParams(
            collective_id=0, has_side_effects=True, vmem_limit_bytes=60 * 1024 * 1024
        ),
    )(*[pltpu.with_memory_space_constraint(a, pltpu.HBM) for a in ins])
    res = pl.pallas_call(
        write_out,
        out_shape=[jax.ShapeDtypeStruct(s, d) for s, d in shapes],
        in_specs=[vm] * len(shapes),
        out_specs=[pl.BlockSpec(memory_space=pl.ANY)] * len(shapes),
        scratch_shapes=[pltpu.SemaphoreType.DMA((len(shapes),))],
    )(*[pltpu.with_memory_space_constraint(r, pltpu.VMEM) for r in res])
    return tuple(r[None] for r in res)


def solution(mesh):
    three = P("head", "seq", None)
    return jax.shard_map(
        local,
        mesh=mesh,
        in_specs=(three, three, three, three, P("head", "seq"), P("head", None)) + (three,) * 6,
        out_specs=(three,) * 6,
        check_vma=False,
    )
```

```python
import math

import jax
import jax.numpy as jnp
from jax import lax
from jax.experimental import pallas as pl
from jax.experimental.pallas import tpu as pltpu
from jax.sharding import PartitionSpec as P

HEADS = 4
HD = 256
HID = 768
HALF = HID // 2
W3 = 3 * HALF
NX = 4
NZ = 8
TB = 128
TT = 2 * TB
MESH = pl.DeviceIdType.MESH
F32 = jnp.float32
BF16 = jnp.bfloat16

NN = (((1,), (0,)), ((), ()))
NT = (((1,), (1,)), ((), ()))
TN = (((0,), (0,)), ((), ()))

GATE_A, GATE_B = (0, 256, "z"), (256, 128, "x")
UP_A, UP_B = (384, 256, "z"), (640, 128, "x")
DOWN_A, DOWN_B = (768, 256, "z"), (1024, 128, "x")
STREAMS = (GATE_A, GATE_B, UP_A, UP_B, DOWN_A, DOWN_B)
BY_MATRIX = ((GATE_A, GATE_B), (UP_A, UP_B), (DOWN_A, DOWN_B))
N_SEMS = 68
SENT_ROWS = 7232


def dot(a, b, dims=NN):
    return lax.dot_general(a, b, dims, preferred_element_type=F32)


class Sems:
    def __init__(self, ref):
        self.ref = ref
        self.next = 0

    def take(self):
        self.next += 1
        assert self.next <= self.ref.shape[0]
        return self.ref.at[self.next - 1]

    def many(self, count):
        return [self.take() for _ in range(count)]


def wait_for(ref, sem):
    pltpu.make_async_copy(ref, ref, sem).wait()


def loop16(body):
    @pl.loop(0, 16)
    def _(i):
        body(i, pl.ds(pl.multiple_of(i * 16, 16), 16))


def block(buf, i, cols):
    v = buf[lax.div(i, 4), pl.ds(lax.rem(i, 4) * 2, 2), :, cols]
    return v.astype(F32).reshape(16, v.shape[-1])


def set_block(buf, i, cols, value):
    buf[lax.div(i, 4), pl.ds(lax.rem(i, 4) * 2, 2), :, cols] = value.reshape(2, 8, value.shape[-1]).astype(BF16)


def kernel(*refs):
    refs = list(refs)

    def grab(n):
        out = refs[:n]
        del refs[:n]
        return out

    in_hbm = grab(12)
    gq_out, gk_out, gv_out, gg_out, gu_out, gd_out = grab(6)
    (sem_ref,) = grab(1)
    q_in, k_in, v_in, og_in, rate_in, gain_in = in_vmem = grab(6)
    stage, msrc, vsrc = grab(3)
    tq, tk, tv, to, tm = grab(5)
    qp, kp, vp, op, gp = grab(5)
    sv_all, in_all, c_all = grab(3)
    sq_z, sq_x, p2, ini, nrm, vecs, cot = grab(7)
    f_a, f_b, f_c, act, ups, qh, dgu = grab(7)
    ap, apr, ao, ss, sr, od, agr = grab(7)
    s1, s2 = grab(2)
    rs1 = [grab(3) for _ in STREAMS]
    rs2 = [grab(3) for _ in STREAMS]
    k_act, kc1, kc2, kc3, kh, rise, bk, bp = grab(8)
    rets = [grab(4) for _ in range(3)]
    fs, fr, sent, x1_ref, own_bytes = grab(5)
    assert not refs

    head = lax.axis_index("head")
    seq = lax.axis_index("seq")
    c = lax.rem(head, 2)
    yl = lax.div(head, 2)
    x = lax.rem(seq, NX)
    z = lax.rem(lax.div(seq, NX), NZ)
    yh = lax.div(seq, NX * NZ)
    native = c == yh
    foreign = jnp.logical_not(native)
    sems = Sems(sem_ref)
    at_end = []

    def dev(yh_=None, z_=None, x_=None, yl_=None, c_=None):
        yh_ = yh if yh_ is None else yh_
        z_ = z if z_ is None else z_
        x_ = x if x_ is None else x_
        yl_ = yl if yl_ is None else yl_
        c_ = c if c_ is None else c_
        return {"head": yl_ * 2 + c_, "seq": (yh_ * NZ + z_) * NX + x_}

    def zp(j):
        return lax.rem(z + j, NZ)

    def xp(j):
        return lax.rem(x + j, NX)

    def plane(j):
        y = lax.rem(yh * 2 + yl + j, 4)
        return lax.div(y, 2), lax.rem(y, 2)

    sibling = dev(c_=1 - c)
    swapped = dev(yh_=c, c_=yh)

    shared_sem = sems.take()
    sent_bytes = []

    def share(src, dst, r_sem, to_dev):
        sent_bytes.append(math.prod(src.shape) * jnp.dtype(src.dtype).itemsize)
        send(src, dst, shared_sem, r_sem, to_dev)

    def send(src, dst, s_sem, r_sem, to_dev):
        pltpu.make_async_remote_copy(
            src_ref=src, dst_ref=dst, send_sem=s_sem, recv_sem=r_sem,
            device_id=to_dev, device_id_type=MESH,
        ).start()

    def keep(src, dst, sem):
        pltpu.make_async_copy(src, dst, sem).start()

    def wait_bytes(count, sem):
        assert count % 4096 == 0
        wait_for(sent.at[0 : count // 512], sem)

    barrier = pltpu.get_barrier_semaphore()
    partners = [dev(z_=zp(j)) for j in range(1, NZ)]
    partners += [dev(x_=xp(j)) for j in range(1, NX)]
    for j in range(1, 4):
        a, b = plane(j)
        partners.append(dev(yh_=a, yl_=b))
    partners.append(sibling)
    partners.append(dev(yh_=1 - yh, c_=1 - c))
    for p in partners:
        pl.semaphore_signal(barrier, inc=1, device_id=p, device_id_type=MESH)
    tok_in, rate_sem, gain_sem = sems.many(3)
    for i in (2, 0, 3, 1):
        keep(in_hbm[i], in_vmem[i], tok_in)
    keep(in_hbm[4], rate_in, rate_sem)
    keep(in_hbm[5], gain_in, gain_sem)
    with jax.named_scope("barrier"):
        pl.semaphore_wait(barrier, len(partners))

    w_send = sems.take()
    w_recv = sems.many(2)

    def rows_of(m, half):
        return in_hbm[6 + m].at[:, pl.ds(half * HALF, HALF)]

    @pl.when(native)
    def _():
        for b in range(2):
            for hf in range(2):

                @pl.when((yh == b) & (c == hf))
                def _(b=b, hf=hf):
                    for m in (3, 4, 5, 0, 1, 2):
                        send(rows_of(m, 1 - hf), stage.at[b, m], w_send, w_recv[b], sibling)
                    for m in (3, 4, 5, 0, 1, 2):
                        keep(rows_of(m, hf), stage.at[b, m], w_recv[b])

    @pl.when(foreign)
    def _():
        for b in range(2):

            @pl.when(yh == b)
            def _(b=b):
                for m in (3, 4, 5, 0, 1, 2):
                    for hf in range(2):
                        send(rows_of(m, hf), stage.at[b, m], w_send, w_recv[b], dev(yh_=c, c_=hf))

    eye = lax.broadcasted_iota(jnp.int32, (TB, TB), 0) == lax.broadcasted_iota(jnp.int32, (TB, TB), 1)

    def column(row):
        return jnp.sum(jnp.where(eye, jnp.broadcast_to(row, (TB, TB)), 0.0), axis=1, keepdims=True)

    def row_of(col):
        return jnp.sum(jnp.where(eye, jnp.broadcast_to(col, (TB, TB)), 0.0), axis=0, keepdims=True)

    wait_bytes(4 * TB * HD * 2, tok_in)
    wait_for(rate_in, rate_sem)
    wait_for(gain_in, gain_sem)
    msrc[...] = jnp.zeros_like(msrc)
    msrc[0:1, :] = gain_in[...]
    msrc[1:2, 0:TB] = rate_in[...]
    vsrc[...] = (column(rate_in[...]) * v_in[...].astype(F32)).astype(BF16)
    ri = lax.broadcasted_iota(jnp.int32, (HD, HD), 0)
    ci = lax.broadcasted_iota(jnp.int32, (HD, HD), 1)
    natural = ((ci >> 2) & 1) * 128 + ((ci >> 3) & 7) * 16 + (ci >> 6) * 4 + (ci & 3)
    p2[...] = jnp.where(ri == natural, 1.0, 0.0).astype(BF16)
    tok_send = sems.take()
    tok_recv = sems.many(3)
    toks = [(q_in, tq), (msrc, tm), (og_in, to), (k_in, tk), (vsrc, tv)]
    groups = ((0,), (1, 2), (3, 4))
    group_bytes = (TB * HD * 2, TB * HD * 2 + 8 * HD * 4, TB * HD * 4)

    @pl.when(native)
    def _():
        for g, which in enumerate(groups):
            for i in which:
                keep(toks[i][0], toks[i][1].at[c], tok_recv[g])

    @pl.when(foreign)
    def _():
        for g, which in enumerate(groups):
            for i in which:
                send(toks[i][0], toks[i][1].at[yh], tok_send, tok_recv[g], swapped)

    sib_recv = sems.many(3)

    def tok_forward(g):
        wait_bytes(group_bytes[g], tok_recv[g])
        for i in groups[g]:
            dst = toks[i][1]
            share(dst.at[c], dst.at[c], sib_recv[g], sibling)

    def tok_ready(g):
        wait_bytes(group_bytes[g], sib_recv[g])

    class Gather:
        def __init__(self, buf, stream, r1, r2):
            first, n, axis = stream
            self.buf, self.cols, self.axis = buf, pl.ds(first, n), axis
            self.r1, self.r2 = r1, r2

        def start(self):
            own = self.buf.at[x, z, :, self.cols]
            if self.axis == "z":
                for j in range(1, NZ):
                    share(own, own, self.r1, dev(z_=zp(j)))
                self.all1 = self.buf.at[0, 0 : NZ - 1, :, self.cols]
            else:
                for j in range(1, NX):
                    share(own, own, self.r1, dev(x_=xp(j)))
                self.all1 = self.buf.at[0, 0 : NX - 1, :, self.cols]

        def mid(self, waited=False):
            if not waited:
                wait_for(self.all1, self.r1)
            if self.axis == "z":
                part = self.buf.at[x, :, :, self.cols]
                for j in range(1, NX):
                    share(part, part, self.r2, dev(x_=xp(j)))
            else:
                part = self.buf.at[:, z, :, self.cols]
                for j in range(1, NZ):
                    share(part, part, self.r2, dev(z_=zp(j)))

    class Scatter:
        def __init__(self, buf, stream, bufs, owners=None):
            first, n, axis = stream
            self.buf, self.cols, self.axis, self.owners = buf, slice(first, first + n), axis, owners
            self.got1, self.mine, self.got2 = bufs
            self.r1 = sems.take()
            self.s2, self.r2 = owners if owners else (None, sems.take())

        def start(self):
            cols = pl.ds(self.cols.start, self.cols.stop - self.cols.start)
            if self.axis == "z":
                for j in range(1, NX):
                    share(self.buf.at[xp(j), :, :, cols], self.got1.at[j - 1], self.r1, dev(x_=xp(j)))
            else:
                for j in range(1, NZ):
                    share(self.buf.at[:, zp(j), :, cols], self.got1.at[j - 1], self.r1, dev(z_=zp(j)))

        def mid(self):
            wait_for(self.got1, self.r1)
            count = NZ if self.axis == "z" else NX

            @pl.loop(0, count)
            def _(i):
                if self.axis == "z":
                    total = self.buf[x, i, :, self.cols].astype(F32)
                else:
                    total = self.buf[i, z, :, self.cols].astype(F32)
                for j in range(self.got1.shape[0]):
                    total += self.got1[j, i].astype(F32)
                if self.owners:
                    self.mine[i, 0] = total[0:4].astype(BF16)
                    self.mine[i, 1] = total[4:8].astype(BF16)
                else:
                    self.mine[i] = total.astype(BF16)

            if not self.owners:
                for j in range(1, count):
                    if self.axis == "z":
                        share(self.mine.at[zp(j)], self.got2.at[j - 1], self.r2, dev(z_=zp(j)))
                    else:
                        share(self.mine.at[xp(j)], self.got2.at[j - 1], self.r2, dev(x_=xp(j)))
                return
            for j in range(count):
                for b in range(2):
                    if self.axis == "z":
                        src, to_dev = self.mine.at[zp(j), b], dev(yh_=b, z_=zp(j), c_=yh)
                    else:
                        src, to_dev = self.mine.at[xp(j), b], dev(yh_=b, x_=xp(j), c_=yh)
                    if j > 0:
                        send(src, self.got2.at[c, j], self.s2, self.r2, to_dev)
                        continue
                    here = native & (yh == b)

                    @pl.when(here)
                    def _(src=src, j=j):
                        keep(src, self.got2.at[c, j], self.r2)

                    @pl.when(jnp.logical_not(here))
                    def _(src=src, j=j, to_dev=to_dev):
                        send(src, self.got2.at[c, j], self.s2, self.r2, to_dev)

        def end(self):
            if not self.owners:
                wait_for(self.got2, self.r2)
            if self.owners:
                for hc in range(2):
                    total = fr[hc, :, self.cols]
                    for j in range(self.got2.shape[1]):
                        total += self.got2[hc, j].astype(F32)
                    first = self.cols.start
                    m = first // HALF
                    lo = first - m * HALF + hc * HALF
                    (gg_out, gu_out, gd_out)[m][:, lo : lo + self.cols.stop - first] = total
                return None
            total = self.mine[z if self.axis == "z" else x].astype(F32)
            for j in range(self.got2.shape[0]):
                total += self.got2[j].astype(F32)
            return total

    assert 3 * (NX - 1) * 8 * 128 == 8 * W3
    z1_bytes = 3 * (NZ - 1) * 8 * 256 * 2
    matrix_bytes = (NX - 1) * NZ * 8 * 256 * 2 + (NZ - 1) * NX * 8 * 128 * 2

    def gathers(buf, x1_shared, z1_shared, all2_shared):
        x1 = sems.take() if x1_shared else None
        z1 = sems.take() if z1_shared else None
        r2 = sems.take() if all2_shared else None
        out, ends = {}, []
        for pair in BY_MATRIX:
            mine = r2 if all2_shared else sems.take()
            ends.append(mine)
            for s in pair:
                one = z1 if s[2] == "z" else x1
                out[s] = Gather(buf, s, sems.take() if one is None else one, mine)
        return out, x1, z1, ends

    def end_matrix(ends, m):
        wait_bytes(matrix_bytes, ends[m])

    sv_g, sv_x1, _, sv_ends = gathers(sv_all, True, False, False)
    in_g, in_x1, in_z1, in_ends = gathers(in_all, True, True, True)
    c_g, _, _, c_ends = gathers(c_all, False, False, False)
    sc1 = {s: Scatter(s1, s, rs1[i]) for i, s in enumerate(STREAMS)}
    own_send = sems.take()
    own_recv = {s: sem for pair, sem in zip(BY_MATRIX, sems.many(3)) for s in pair}
    sc2 = {s: Scatter(s2, s, rs2[i], (own_send, own_recv[s])) for i, s in enumerate(STREAMS)}

    with jax.named_scope("w_rows"):
        for b in range(2):
            wait_for(stage.at[0], w_recv[b])

    def eight(first):
        return jnp.concatenate(
            [jnp.concatenate([stage[b, m].astype(F32) for m in range(first, first + 3)], axis=1) for b in range(2)],
            axis=0,
        )

    sv_all[x, z] = eight(3).astype(BF16)
    for s in STREAMS:
        sv_g[s].start()
    init8 = eight(0)
    in_all[x, z] = init8.astype(BF16)
    sq_z[z] = jnp.sum(init8 * init8, axis=0, keepdims=True)
    sq_s1, sq_r1, sq_s2, sq_r2 = sems.many(4)
    for j in range(1, NZ):
        send(sq_z.at[z], sq_z.at[z], sq_s1, sq_r1, dev(z_=zp(j)))
    at_end.append((sq_z.at[0 : NZ - 1], sq_s1))

    with jax.named_scope("w_tok1"):
        tok_forward(0)
        tok_forward(1)
    with jax.named_scope("w_sv_mid"):
        wait_for(x1_ref, sv_x1)
        for s in (GATE_B, UP_B, DOWN_B, GATE_A, UP_A, DOWN_A):
            sv_g[s].mid(s[2] == "x")
            if s is DOWN_B:
                wait_for(sq_z.at[0 : NZ - 1], sq_r1)
                total = sq_z[0]
                for j in range(1, NZ):
                    total += sq_z[j]
                sq_x[x] = total
                for j in range(1, NX):
                    send(sq_x.at[x], sq_x.at[x], sq_s2, sq_r2, dev(x_=xp(j)))
                at_end.append((sq_x.at[0 : NX - 1], sq_s2))
    for s in STREAMS:
        in_g[s].start()

    def permuted(src, dst):
        dst[...] = dot(src[...].reshape(TT, HD), p2[...]).astype(BF16)

    with jax.named_scope("w_tok2"):
        tok_ready(0)
        tok_ready(1)
    permuted(tq, qp)
    permuted(to, op)
    gains_nat = tm[0, 0:1, :]
    gcol = jnp.concatenate([column(gains_nat[:, 0:TB]), column(gains_nat[:, TB:])], axis=0)
    gp[...] = jnp.sum(p2[...].astype(F32) * gcol, axis=0, keepdims=True)
    with jax.named_scope("w_tok3"):
        tok_forward(2)

    with jax.named_scope("w_sq"):
        wait_for(sq_x.at[0 : NX - 1], sq_r2)
    sq_init = sq_x[0] + sq_x[1] + sq_x[2] + sq_x[3]
    norm_init = jnp.sqrt(sq_init + 1e-06)

    def normalize(m):
        cols = slice(m * HALF, (m + 1) * HALF)

        def step(i, carry):
            a = block(sv_all, i, cols)
            return carry + a * a

        sq = jnp.sum(lax.fori_loop(0, 16, step, jnp.zeros((16, HALF), F32)), axis=0, keepdims=True)
        norm_i = norm_init[:, cols]
        norm_s = jnp.sqrt(sq + 1e-06)
        ratio = norm_i / norm_s
        vecs[0:1, cols] = ratio
        vecs[1:2, cols] = norm_i / (norm_s * norm_s * norm_s)
        vecs[2:3, cols] = 1.0 / (norm_i * norm_s)

        def body(i, rows):
            nrm[rows, cols] = (block(sv_all, i, cols) * ratio).astype(BF16)

        loop16(body)

    c_0, c_1, c_2 = (slice(m * HALF, (m + 1) * HALF) for m in range(3))
    c_01 = slice(0, 2 * HALF)

    with jax.named_scope("w_sv_gate"):
        end_matrix(sv_ends, 0)
    normalize(0)
    f_a[...] = dot(qp[...], nrm[:, c_0])
    with jax.named_scope("w_sv_up"):
        end_matrix(sv_ends, 1)
    normalize(1)
    f_b[...] = dot(qp[...], nrm[:, c_1])

    def q_body(i, rows):
        v = f_a[rows, :]
        up = f_b[rows, :]
        s = jax.nn.sigmoid(v)
        a = v * s
        act[rows, :] = a
        ups[rows, :] = up * (s * (1.0 + v * (1.0 - s)))
        qh[rows, :] = (a * up).astype(BF16)

    loop16(q_body)
    with jax.named_scope("w_sv_down"):
        end_matrix(sv_ends, 2)
    normalize(2)
    ap[...] = dot(qh[...], nrm[:, c_2], NT)
    aprs = sems.take()
    share(ap, apr, aprs, sibling)

    gains = gp[...]
    with jax.named_scope("w_ap"):
        wait_for(apr, aprs)
    for b in range(2):
        rows = slice(b * TB, (b + 1) * TB)
        out = ap[rows, :] + apr[rows, :]
        ao[rows, :] = out
        ss[0:1, rows] = row_of(jnp.sum(out * out, axis=1, keepdims=True))
        ss[1:2, rows] = row_of(jnp.sum(out * gains * op[rows, :].astype(F32), axis=1, keepdims=True))
    ss_r = sems.take()
    for j in range(1, 4):
        a, b = plane(j)
        share(ss, sr.at[j - 1], ss_r, dev(yh_=a, yl_=b))
    with jax.named_scope("w_in_mid"):
        wait_for(x1_ref, in_x1)
        wait_bytes(z1_bytes, in_z1)
        for s in STREAMS:
            in_g[s].mid(True)
    with jax.named_scope("w_tok4"):
        tok_ready(2)
    permuted(tk, kp)
    permuted(tv, vp)

    with jax.named_scope("w_sums"):
        wait_for(sr, ss_r)
    tot = ss[...] + sr[0] + sr[1] + sr[2]
    full = HEADS * HD
    root_row = jnp.sqrt(tot[0:1, :] / full + 1e-05)
    inv_row = 1.0 / root_row
    fac_row = (tot[1:2, :] / full) / (root_row * root_row * root_row)
    for b in range(2):
        rows = slice(b * TB, (b + 1) * TB)
        inv = column(inv_row[:, rows])
        fac = column(fac_row[:, rows])
        od[rows, :] = (gains * op[rows, :].astype(F32) * inv - ao[rows, :] * fac).astype(BF16)

    def project(m, grad):
        cols = slice(m * HALF, (m + 1) * HALF)
        agr[...] = grad

        def step(i, carry):
            return carry + block(sv_all, i, cols) * agr[pl.ds(pl.multiple_of(i * 16, 16), 16), :]

        part = jnp.sum(lax.fori_loop(0, 16, step, jnp.zeros((16, HALF), F32)), axis=0, keepdims=True)
        ratio = vecs[0:1, cols]
        fall = part * vecs[1:2, cols]
        vecs[3:4, cols] = part * vecs[2:3, cols]

        def body(i, rows):
            set_block(s1, i, cols, agr[rows, :] * ratio - block(sv_all, i, cols) * fall)

        loop16(body)

    project(2, dot(od[...], qh[...], TN))
    for s in BY_MATRIX[2]:
        sc1[s].start()
    f_a[...] = dot(od[...], nrm[:, c_2])

    def d_body(i, rows):
        dh = f_a[rows, :]
        dgu[rows, 0:HALF] = (dh * ups[rows, :]).astype(BF16)
        dgu[rows, HALF : 2 * HALF] = (dh * act[rows, :]).astype(BF16)

    loop16(d_body)
    project(0, dot(qp[...], dgu[:, 0:HALF], TN))
    for s in BY_MATRIX[0]:
        sc1[s].start()
    project(1, dot(qp[...], dgu[:, HALF : 2 * HALF], TN))
    for s in BY_MATRIX[1]:
        sc1[s].start()

    give_send, give_recv = sems.many(2)

    class Give:
        def __init__(self, bufs, scale):
            self.part, self.got, self.out, self.back = bufs
            self.scale = scale
            self.r1 = sems.take()
            self.s2, self.r2 = give_send, give_recv

        def start(self, part):
            self.part[...] = part.reshape(2, TB, HD)
            share(self.part.at[1 - c], self.got, self.r1, sibling)

        def finish(self):
            wait_for(self.got, self.r1)
            total = self.part[c] + self.got[...]
            if self.scale:
                total = total * column(tm[c, 1:2, 0:TB])
            self.out[...] = dot(total.astype(BF16), p2[...], NT).astype(BF16)

            @pl.when(native)
            def _():
                keep(self.out, self.back, self.r2)

            @pl.when(foreign)
            def _():
                send(self.out, self.back, self.s2, self.r2, swapped)

    give_q, give_k, give_v = (Give(rets[i], i == 2) for i in range(3))
    give_q.start(dot(dgu[...], nrm[:, c_01], NT))
    with jax.named_scope("w_sc1_mid"):
        for s in (DOWN_A, GATE_A, DOWN_B, UP_A, GATE_B, UP_B):
            sc1[s].mid()
    with jax.named_scope("w_in_end"):
        wait_bytes(3 * matrix_bytes, in_ends[0])
    ini[...] = in_all[...].reshape(HD, W3)
    f_a[...] = dot(kp[...], ini[:, c_0])
    f_b[...] = dot(kp[...], ini[:, c_1])
    f_c[...] = dot(vp[...], ini[:, c_2])

    def k_body(i, rows):
        v = f_a[rows, :]
        up = f_b[rows, :]
        proj = f_c[rows, :]
        s = jax.nn.sigmoid(v)
        a = v * s
        slope = s * (1.0 + v * (1.0 - s))
        bend = s * (1.0 - s) * (2.0 + v * (1.0 - 2.0 * s))
        k_act[rows, :] = a
        kc1[rows, :] = up * slope
        kc2[rows, :] = proj * slope
        kc3[rows, :] = proj * up * bend
        kh[rows, :] = (a * up).astype(BF16)
        rise[rows, 0:HALF] = (proj * up * slope).astype(BF16)
        rise[rows, HALF : 2 * HALF] = (proj * a).astype(BF16)

    loop16(k_body)
    for s in (DOWN_A, DOWN_B, GATE_B, GATE_A, UP_B, UP_A):
        with jax.named_scope("w_sc1_end"):
            res = sc1[s].end()
        cols = slice(s[0], s[0] + s[1])
        c_all[x, z, :, cols] = res.astype(BF16)
        c_g[s].start()
        fs[0, :, cols] = res[0:4]
        fs[1, :, cols] = res[4:8]

    f_send, f_recv = sems.many(2)
    for hc in range(2):

        @pl.when(c == hc)
        def _(hc=hc):
            @pl.when(native)
            def _():
                keep(fs.at[yh], fr.at[hc], f_recv)

            @pl.when(foreign)
            def _():
                send(fs.at[yh], fr.at[hc], f_send, f_recv, sibling)

            send(fs.at[1 - yh], fr.at[hc], f_send, f_recv, dev(yh_=1 - yh, c_=yh))

    give_q.finish()
    with jax.named_scope("w_c_mid"):
        for s in (DOWN_B, GATE_B, DOWN_A, UP_B, GATE_A, UP_A):
            c_g[s].mid()

    def cot_of(m):
        cols = slice(m * HALF, (m + 1) * HALF)
        cot[:, cols] = c_all[:, :, :, cols].reshape(HD, HALF)
        return cot[:, cols]

    with jax.named_scope("w_c_down"):
        end_matrix(c_ends, 2)
    f_c[...] = dot(vp[...], cot_of(2))
    with jax.named_scope("w_c_gate"):
        end_matrix(c_ends, 0)
    f_a[...] = dot(kp[...], cot_of(0))
    def up_body(i, rows):
        bk[rows, HALF : 2 * HALF] = (f_a[rows, :] * kc2[rows, :] + f_c[rows, :] * k_act[rows, :]).astype(BF16)

    loop16(up_body)

    def inner(m, grad):
        cols = slice(m * HALF, (m + 1) * HALF)
        extra = vecs[3:4, cols]
        agr[...] = grad

        def body(i, rows):
            set_block(s2, i, cols, agr[rows, :] + ini[rows, cols].astype(F32) * extra)

        loop16(body)

    inner(1, dot(kp[...], bk[:, HALF : 2 * HALF], TN))
    for s in BY_MATRIX[1]:
        sc2[s].start()
    with jax.named_scope("w_c_up"):
        end_matrix(c_ends, 1)
    f_b[...] = dot(kp[...], cot_of(1))

    def b_body(i, rows):
        bg = f_a[rows, :]
        bu = f_b[rows, :]
        c1 = kc1[rows, :]
        bp[rows, :] = (bg * c1 + bu * k_act[rows, :]).astype(BF16)
        bk[rows, 0:HALF] = (bg * kc3[rows, :] + (bu * kc2[rows, :] + f_c[rows, :] * c1)).astype(BF16)

    loop16(b_body)
    inner(2, dot(vp[...], bp[...], TN))
    for s in BY_MATRIX[2]:
        sc2[s].start()
    inner(0, dot(kp[...], bk[:, 0:HALF], TN))
    for s in BY_MATRIX[0]:
        sc2[s].start()
    give_k.start(dot(rise[...], cot[:, c_01], NT) + dot(bk[...], ini[:, c_01], NT))
    give_v.start(dot(kh[...], cot[:, c_2], NT) + dot(bp[...], ini[:, c_2], NT))
    with jax.named_scope("w_sc2_mid"):
        sc2[UP_A].mid()
    with jax.named_scope("w_give_k"):
        give_k.finish()
    with jax.named_scope("w_give_v"):
        give_v.finish()
    with jax.named_scope("w_sc2_mid"):
        for s in (DOWN_A, UP_B, GATE_A, DOWN_B, GATE_B):
            sc2[s].mid()
    with jax.named_scope("w_collect"):
        wait_bytes(3 * TB * HD * 2, give_recv)
        for give, out in ((give_q, gq_out), (give_k, gk_out), (give_v, gv_out)):
            out[...] = give.back[...]
        wait_for(fr, f_recv)
    with jax.named_scope("w_sc2_end"):
        for m in (1, 2, 0):
            wait_bytes(2 * (NZ * 4 * 256 * 2 + NX * 4 * 128 * 2), own_recv[BY_MATRIX[m][0]])
            for s in BY_MATRIX[m]:
                sc2[s].end()

    assert sum(sent_bytes) % 4096 == 0 and sum(sent_bytes) // 512 <= SENT_ROWS
    with jax.named_scope("w_sent"):
        wait_for(sent.at[0 : sum(sent_bytes) // 512], shared_sem)
        for ref, sem in at_end:
            wait_for(ref, sem)

        @pl.when(native)
        def _():
            wait_for(stage.at[0], w_send)
            wait_for(fr.at[0], f_send)
            wait_for(own_bytes, own_send)

        @pl.when(foreign)
        def _():
            wait_bytes(2 * 6 * 4 * HALF * 2, w_send)
            wait_bytes(sum(group_bytes), tok_send)
            wait_for(fr, f_send)
            wait_bytes(3 * TB * HD * 2, give_send)
            wait_bytes(3 * 2 * (NZ * 4 * 256 * 2 + NX * 4 * 128 * 2), own_send)


def write_out(*refs):
    sem = refs[-1]
    half = (len(refs) - 1) // 2
    copies = [pltpu.make_async_copy(refs[i], refs[half + i], sem.at[i]) for i in range(half)]
    for cp in copies:
        cp.start()
    for cp in copies:
        cp.wait()


def local(*args):
    (queries, key_rows, value_rows, out_grad, step_sizes, norm_gain, gate_init, up_init, down_init,
     gate_saved, up_saved, down_saved) = args
    ins = [a[0] for a in (queries, key_rows, value_rows, out_grad)]
    ins += [step_sizes, norm_gain]
    ins += [a[0] for a in (gate_init, up_init, down_init, gate_saved, up_saved, down_saved)]
    shapes = [((TB, HD), BF16)] * 3 + [((4, HID), F32)] * 3

    def v(dtype, *shape):
        return pltpu.VMEM(shape, dtype)

    def rs_bufs(owners):
        out = []
        for _, n, axis in STREAMS:
            if axis == "z":
                first, count = v(BF16, NX - 1, NZ, 8, n), NZ
            else:
                first, count = v(BF16, NZ - 1, NX, 8, n), NX
            if owners:
                out += [first, v(BF16, count, 2, 4, n), v(BF16, 2, count, 4, n)]
            else:
                out += [first, v(BF16, count, 8, n), v(BF16, count - 1, 8, n)]
        return out

    ret = [v(F32, 2, TB, HD), v(F32, TB, HD), v(BF16, TB, HD), v(BF16, TB, HD)]
    scratch = [
        pltpu.SemaphoreType.DMA((N_SEMS,)),
        *[v(a.dtype, *a.shape) for a in ins[:6]],
        v(BF16, 2, 6, 4, HALF), v(F32, 8, HD), v(BF16, TB, HD),
        *[v(BF16, 2, TB, HD)] * 4, v(F32, 2, 8, HD),
        *[v(BF16, TT, HD)] * 4, v(F32, 1, HD),
        *[v(BF16, NX, NZ, 8, W3)] * 3,
        v(F32, NZ, 1, W3), v(F32, NX, 1, W3), v(BF16, HD, HD),
        v(BF16, HD, W3), v(BF16, HD, W3), v(F32, 8, W3), v(BF16, HD, W3),
        *[v(F32, TT, HALF)] * 5, v(BF16, TT, HALF), v(BF16, TT, 2 * HALF),
        *[v(F32, TT, HD)] * 3, v(F32, 8, TT), v(F32, 3, 8, TT), v(BF16, TT, HD), v(F32, HD, HALF),
        *[v(BF16, NX, NZ, 8, W3)] * 2,
        *rs_bufs(False), *rs_bufs(True),
        *[v(F32, TT, HALF)] * 4, v(BF16, TT, HALF), v(BF16, TT, 2 * HALF), v(BF16, TT, 2 * HALF), v(BF16, TT, HALF),
        *ret * 3,
        v(F32, 2, 4, W3), v(F32, 2, 4, W3), v(F32, SENT_ROWS, 128),
        v(BF16, 8, W3), v(F32, 111, 2, 128),
    ]
    vm = pl.BlockSpec(memory_space=pltpu.VMEM)
    res = pl.pallas_call(
        kernel,
        out_shape=[pltpu.VMEM(s, d) for s, d in shapes],
        in_specs=[pl.BlockSpec(memory_space=pltpu.HBM)] * len(ins),
        out_specs=[vm] * len(shapes),
        scratch_shapes=scratch,
        compiler_params=pltpu.CompilerParams(
            collective_id=0, has_side_effects=True, vmem_limit_bytes=60 * 1024 * 1024
        ),
    )(*[pltpu.with_memory_space_constraint(a, pltpu.HBM) for a in ins])
    res = pl.pallas_call(
        write_out,
        out_shape=[jax.ShapeDtypeStruct(s, d) for s, d in shapes],
        in_specs=[vm] * len(shapes),
        out_specs=[pl.BlockSpec(memory_space=pl.ANY)] * len(shapes),
        scratch_shapes=[pltpu.SemaphoreType.DMA((len(shapes),))],
    )(*[pltpu.with_memory_space_constraint(r, pltpu.VMEM) for r in res])
    return tuple(r[None] for r in res)


def solution(mesh):
    three = P("head", "seq", None)
    return jax.shard_map(
        local,
        mesh=mesh,
        in_specs=(three, three, three, three, P("head", "seq"), P("head", None)) + (three,) * 6,
        out_specs=(three,) * 6,
        check_vma=False,
    )
```

```python
import math

import jax
import jax.numpy as jnp
from jax import lax
from jax.experimental import pallas as pl
from jax.experimental.pallas import tpu as pltpu
from jax.sharding import PartitionSpec as P

HEADS = 4
HD = 256
HID = 768
HALF = HID // 2
W3 = 3 * HALF
NX = 4
NZ = 8
TB = 128
TT = 2 * TB
MESH = pl.DeviceIdType.MESH
F32 = jnp.float32
BF16 = jnp.bfloat16

NN = (((1,), (0,)), ((), ()))
NT = (((1,), (1,)), ((), ()))
TN = (((0,), (0,)), ((), ()))

def streams_of(pieces):
    out = []
    for m in range(3):
        first, mine = m * HALF, []
        for n, axis in pieces:
            mine.append((first, n, axis))
            first += n
        out.append(tuple(mine))
    return tuple(out)


FINE = streams_of(((128, "z"), (128, "z"), (128, "x")))
COARSE = streams_of(((256, "z"), (128, "x")))
(GATE_1, GATE_2, GATE_X), (UP_1, UP_2, UP_X), (DOWN_1, DOWN_2, DOWN_X) = FINE
STREAMS = sum(FINE, ())
N_SEMS = 83
SENT_ROWS = 7232


def dot(a, b, dims=NN):
    return lax.dot_general(a, b, dims, preferred_element_type=F32)


class Sems:
    def __init__(self, ref):
        self.ref = ref
        self.next = 0

    def take(self):
        self.next += 1
        assert self.next <= self.ref.shape[0]
        return self.ref.at[self.next - 1]

    def many(self, count):
        return [self.take() for _ in range(count)]


def wait_for(ref, sem):
    pltpu.make_async_copy(ref, ref, sem).wait()


def loop16(body):
    @pl.loop(0, 16)
    def _(i):
        body(i, pl.ds(pl.multiple_of(i * 16, 16), 16))


def block(buf, i, cols):
    v = buf[lax.div(i, 4), pl.ds(lax.rem(i, 4) * 2, 2), :, cols]
    return v.astype(F32).reshape(16, v.shape[-1])


def set_block(buf, i, cols, value):
    buf[lax.div(i, 4), pl.ds(lax.rem(i, 4) * 2, 2), :, cols] = value.reshape(2, 8, value.shape[-1]).astype(BF16)


def kernel(*refs):
    refs = list(refs)

    def grab(n):
        out = refs[:n]
        del refs[:n]
        return out

    in_hbm = grab(12)
    gq_out, gk_out, gv_out, gg_out, gu_out, gd_out = grab(6)
    (sem_ref,) = grab(1)
    q_in, k_in, v_in, og_in, rate_in, gain_in = in_vmem = grab(6)
    w_in = grab(6)
    stage, msrc, vsrc = grab(3)
    tq, tk, tv, to, tm = grab(5)
    qp, kp, vp, op, gp = grab(5)
    sv_all, in_all, c_all = grab(3)
    sq_z, sq_x, p2, ini, nrm, vecs, cot = grab(7)
    f_a, f_b, f_c, act, ups, qh, dgu = grab(7)
    ap, apr, ao, ss, sr, od, agr = grab(7)
    s1, s2 = grab(2)
    rs1 = [grab(3) for _ in STREAMS]
    rs2 = [grab(3) for _ in STREAMS]
    k_act, kc1, kc2, kc3, kh, rise, bk, bp = grab(8)
    rets = [grab(4) for _ in range(3)]
    fs, fr, sent, x1_ref, own_bytes = grab(5)
    assert not refs

    head = lax.axis_index("head")
    seq = lax.axis_index("seq")
    c = lax.rem(head, 2)
    yl = lax.div(head, 2)
    x = lax.rem(seq, NX)
    z = lax.rem(lax.div(seq, NX), NZ)
    yh = lax.div(seq, NX * NZ)
    native = c == yh
    foreign = jnp.logical_not(native)
    sems = Sems(sem_ref)
    at_end = []

    def dev(yh_=None, z_=None, x_=None, yl_=None, c_=None):
        yh_ = yh if yh_ is None else yh_
        z_ = z if z_ is None else z_
        x_ = x if x_ is None else x_
        yl_ = yl if yl_ is None else yl_
        c_ = c if c_ is None else c_
        return {"head": yl_ * 2 + c_, "seq": (yh_ * NZ + z_) * NX + x_}

    def zp(j):
        return lax.rem(z + j, NZ)

    def xp(j):
        return lax.rem(x + j, NX)

    def plane(j):
        y = lax.rem(yh * 2 + yl + j, 4)
        return lax.div(y, 2), lax.rem(y, 2)

    sibling = dev(c_=1 - c)
    swapped = dev(yh_=c, c_=yh)

    shared_sem = sems.take()
    sent_bytes = []

    def share(src, dst, r_sem, to_dev):
        sent_bytes.append(math.prod(src.shape) * jnp.dtype(src.dtype).itemsize)
        send(src, dst, shared_sem, r_sem, to_dev)

    def send(src, dst, s_sem, r_sem, to_dev):
        pltpu.make_async_remote_copy(
            src_ref=src, dst_ref=dst, send_sem=s_sem, recv_sem=r_sem,
            device_id=to_dev, device_id_type=MESH,
        ).start()

    def keep(src, dst, sem):
        pltpu.make_async_copy(src, dst, sem).start()

    def wait_bytes(count, sem):
        assert count % 4096 == 0
        wait_for(sent.at[0 : count // 512], sem)

    barrier = pltpu.get_barrier_semaphore()
    partners = [dev(z_=zp(j)) for j in range(1, NZ)]
    partners += [dev(x_=xp(j)) for j in range(1, NX)]
    for j in range(1, 4):
        a, b = plane(j)
        partners.append(dev(yh_=a, yl_=b))
    partners.append(sibling)
    partners.append(dev(yh_=1 - yh, c_=1 - c))
    for p in partners:
        pl.semaphore_signal(barrier, inc=1, device_id=p, device_id_type=MESH)
    rows_in, tok_in, rate_sem, gain_sem = sems.many(4)
    for m in range(6):
        keep(in_hbm[6 + m], w_in[m], rows_in)
    for i in (2, 0, 3, 1):
        keep(in_hbm[i], in_vmem[i], tok_in)
    keep(in_hbm[4], rate_in, rate_sem)
    keep(in_hbm[5], gain_in, gain_sem)
    with jax.named_scope("barrier"):
        pl.semaphore_wait(barrier, len(partners))

    w_send = sems.take()
    w_recv = (sems.many(2), sems.many(2))
    wait_bytes(6 * 4 * HID * 2, rows_in)

    def rows_of(m, half):
        return w_in[m].at[:, pl.ds(half * HALF, HALF)]

    @pl.when(native)
    def _():
        for b in range(2):
            for hf in range(2):

                @pl.when((yh == b) & (c == hf))
                def _(b=b, hf=hf):
                    for m in (3, 4, 5, 0, 1, 2):
                        send(rows_of(m, 1 - hf), stage.at[b, m], w_send, w_recv[m // 3][b], sibling)
                    for m in (3, 4, 5, 0, 1, 2):
                        keep(rows_of(m, hf), stage.at[b, m], w_recv[m // 3][b])

    @pl.when(foreign)
    def _():
        for b in range(2):

            @pl.when(yh == b)
            def _(b=b):
                for m in (3, 4, 5, 0, 1, 2):
                    for hf in range(2):
                        send(rows_of(m, hf), stage.at[b, m], w_send, w_recv[m // 3][b], dev(yh_=c, c_=hf))

    eye = lax.broadcasted_iota(jnp.int32, (TB, TB), 0) == lax.broadcasted_iota(jnp.int32, (TB, TB), 1)

    def column(row):
        return jnp.sum(jnp.where(eye, jnp.broadcast_to(row, (TB, TB)), 0.0), axis=1, keepdims=True)

    def row_of(col):
        return jnp.sum(jnp.where(eye, jnp.broadcast_to(col, (TB, TB)), 0.0), axis=0, keepdims=True)

    wait_bytes(4 * TB * HD * 2, tok_in)
    wait_for(rate_in, rate_sem)
    wait_for(gain_in, gain_sem)
    msrc[...] = jnp.zeros_like(msrc)
    msrc[0:1, :] = gain_in[...]
    msrc[1:2, 0:TB] = rate_in[...]
    vsrc[...] = (column(rate_in[...]) * v_in[...].astype(F32)).astype(BF16)
    ri = lax.broadcasted_iota(jnp.int32, (HD, HD), 0)
    ci = lax.broadcasted_iota(jnp.int32, (HD, HD), 1)
    natural = ((ci >> 2) & 1) * 128 + ((ci >> 3) & 7) * 16 + (ci >> 6) * 4 + (ci & 3)
    p2[...] = jnp.where(ri == natural, 1.0, 0.0).astype(BF16)
    tok_send = sems.take()
    tok_recv = sems.many(3)
    toks = [(q_in, tq), (msrc, tm), (og_in, to), (k_in, tk), (vsrc, tv)]
    groups = ((0,), (1, 2), (3, 4))
    group_bytes = (TB * HD * 2, TB * HD * 2 + 8 * HD * 4, TB * HD * 4)

    @pl.when(native)
    def _():
        for g, which in enumerate(groups):
            for i in which:
                keep(toks[i][0], toks[i][1].at[c], tok_recv[g])

    @pl.when(foreign)
    def _():
        for g, which in enumerate(groups):
            for i in which:
                send(toks[i][0], toks[i][1].at[yh], tok_send, tok_recv[g], swapped)

    sib_recv = sems.many(3)

    def tok_forward(g):
        wait_bytes(group_bytes[g], tok_recv[g])
        for i in groups[g]:
            dst = toks[i][1]
            share(dst.at[c], dst.at[c], sib_recv[g], sibling)

    def tok_ready(g):
        wait_bytes(group_bytes[g], sib_recv[g])

    class Gather:
        def __init__(self, buf, stream, r1, r2):
            first, n, axis = stream
            self.buf, self.cols, self.axis = buf, pl.ds(first, n), axis
            self.r1, self.r2 = r1, r2

        def start(self):
            own = self.buf.at[x, z, :, self.cols]
            if self.axis == "z":
                for j in range(1, NZ):
                    share(own, own, self.r1, dev(z_=zp(j)))
                self.all1 = self.buf.at[0, 0 : NZ - 1, :, self.cols]
            else:
                for j in range(1, NX):
                    share(own, own, self.r1, dev(x_=xp(j)))
                self.all1 = self.buf.at[0, 0 : NX - 1, :, self.cols]

        def mid(self, waited=False):
            if not waited:
                wait_for(self.all1, self.r1)
            if self.axis == "z":
                part = self.buf.at[x, :, :, self.cols]
                for j in range(1, NX):
                    share(part, part, self.r2, dev(x_=xp(j)))
            else:
                part = self.buf.at[:, z, :, self.cols]
                for j in range(1, NZ):
                    share(part, part, self.r2, dev(z_=zp(j)))

    class Scatter:
        def __init__(self, buf, stream, bufs, owners=None):
            first, n, axis = stream
            self.buf, self.cols, self.axis, self.owners = buf, slice(first, first + n), axis, owners
            self.got1, self.mine, self.got2 = bufs
            self.r1 = sems.take()
            self.s2, self.r2 = owners if owners else (None, sems.take())

        def start(self):
            cols = pl.ds(self.cols.start, self.cols.stop - self.cols.start)
            if self.axis == "z":
                for j in range(1, NX):
                    share(self.buf.at[xp(j), :, :, cols], self.got1.at[j - 1], self.r1, dev(x_=xp(j)))
            else:
                for j in range(1, NZ):
                    share(self.buf.at[:, zp(j), :, cols], self.got1.at[j - 1], self.r1, dev(z_=zp(j)))

        def mid(self):
            wait_for(self.got1, self.r1)
            count = NZ if self.axis == "z" else NX

            @pl.loop(0, count)
            def _(i):
                if self.axis == "z":
                    total = self.buf[x, i, :, self.cols].astype(F32)
                else:
                    total = self.buf[i, z, :, self.cols].astype(F32)
                for j in range(self.got1.shape[0]):
                    total += self.got1[j, i].astype(F32)
                if self.owners:
                    self.mine[i, 0] = total[0:4].astype(BF16)
                    self.mine[i, 1] = total[4:8].astype(BF16)
                else:
                    self.mine[i] = total.astype(BF16)

            if not self.owners:
                for j in range(1, count):
                    if self.axis == "z":
                        share(self.mine.at[zp(j)], self.got2.at[j - 1], self.r2, dev(z_=zp(j)))
                    else:
                        share(self.mine.at[xp(j)], self.got2.at[j - 1], self.r2, dev(x_=xp(j)))
                return
            for j in range(count):
                for b in range(2):
                    if self.axis == "z":
                        src, to_dev = self.mine.at[zp(j), b], dev(yh_=b, z_=zp(j), c_=yh)
                    else:
                        src, to_dev = self.mine.at[xp(j), b], dev(yh_=b, x_=xp(j), c_=yh)
                    if j > 0:
                        send(src, self.got2.at[c, j], self.s2, self.r2, to_dev)
                        continue
                    here = native & (yh == b)

                    @pl.when(here)
                    def _(src=src, j=j):
                        keep(src, self.got2.at[c, j], self.r2)

                    @pl.when(jnp.logical_not(here))
                    def _(src=src, j=j, to_dev=to_dev):
                        send(src, self.got2.at[c, j], self.s2, self.r2, to_dev)

        def end(self):
            if not self.owners:
                wait_for(self.got2, self.r2)
            if self.owners:
                for hc in range(2):
                    total = fr[hc, :, self.cols]
                    for j in range(self.got2.shape[1]):
                        total += self.got2[hc, j].astype(F32)
                    first = self.cols.start
                    m = first // HALF
                    lo = first - m * HALF + hc * HALF
                    (gg_out, gu_out, gd_out)[m][:, lo : lo + self.cols.stop - first] = total
                return None
            total = self.mine[z if self.axis == "z" else x].astype(F32)
            for j in range(self.got2.shape[0]):
                total += self.got2[j].astype(F32)
            return total

    assert 3 * (NX - 1) * 8 * 128 == 8 * W3
    z1_bytes = 3 * (NZ - 1) * 8 * 256 * 2
    matrix_bytes = (NX - 1) * NZ * 8 * 256 * 2 + (NZ - 1) * NX * 8 * 128 * 2

    def gathers(buf, matrices, x1_shared, z1_shared, all2_shared):
        x1 = sems.take() if x1_shared else None
        z1 = sems.take() if z1_shared else None
        r2 = sems.take() if all2_shared else None
        out, ends = {}, []
        for pair in matrices:
            mine = r2 if all2_shared else sems.take()
            ends.append(mine)
            for s in pair:
                one = z1 if s[2] == "z" else x1
                out[s] = Gather(buf, s, sems.take() if one is None else one, mine)
        return out, x1, z1, ends

    def end_matrix(ends, m):
        wait_bytes(matrix_bytes, ends[m])

    sv_g, sv_x1, _, sv_ends = gathers(sv_all, COARSE, True, False, False)
    in_g, in_x1, in_z1, in_ends = gathers(in_all, COARSE, True, True, True)
    c_g, _, _, c_ends = gathers(c_all, FINE, False, False, False)
    sc1 = {s: Scatter(s1, s, rs1[i]) for i, s in enumerate(STREAMS)}
    own_send = sems.take()
    own_recv = {s: sem for pair, sem in zip(FINE, sems.many(3)) for s in pair}
    sc2 = {s: Scatter(s2, s, rs2[i], (own_send, own_recv[s])) for i, s in enumerate(STREAMS)}

    with jax.named_scope("w_rows"):
        for b in range(2):
            wait_for(stage.at[0, 3:6], w_recv[1][b])

    def eight(first):
        return jnp.concatenate(
            [jnp.concatenate([stage[b, m].astype(F32) for m in range(first, first + 3)], axis=1) for b in range(2)],
            axis=0,
        )

    saved8 = eight(3)
    sv_all[x, z] = saved8.astype(BF16)
    for s in sum(COARSE, ()):
        sv_g[s].start()
    for b in range(2):
        wait_for(stage.at[0, 0:3], w_recv[0][b])
    init8 = eight(0)
    in_all[x, z] = init8.astype(BF16)
    sq_x[x, :, 0:W3] = jnp.sum(init8 * init8, axis=0, keepdims=True)
    sq_x[x, :, W3:] = jnp.sum(saved8 * saved8, axis=0, keepdims=True)
    sq_s1, sq_r1, sq_s2, sq_r2 = sems.many(4)
    for j in range(1, NX):
        send(sq_x.at[x], sq_x.at[x], sq_s1, sq_r1, dev(x_=xp(j)))
    at_end.append((sq_x.at[0 : NX - 1], sq_s1))

    with jax.named_scope("w_tok1"):
        tok_forward(0)
        tok_forward(1)
    with jax.named_scope("w_sv_mid"):
        wait_for(sq_x.at[0 : NX - 1], sq_r1)
        sq_z[z] = sq_x[0] + sq_x[1] + sq_x[2] + sq_x[3]
        for j in range(1, NZ):
            send(sq_z.at[z], sq_z.at[z], sq_s2, sq_r2, dev(z_=zp(j)))
        at_end.append((sq_z.at[0 : NZ - 1], sq_s2))
        wait_for(x1_ref, sv_x1)
        for s in [pair[1] for pair in COARSE] + [pair[0] for pair in COARSE]:
            sv_g[s].mid(s[2] == "x")

    def permuted(src, dst):
        dst[...] = dot(src[...].reshape(TT, HD), p2[...]).astype(BF16)

    with jax.named_scope("w_tok2"):
        tok_ready(0)
        tok_ready(1)
    permuted(tq, qp)
    permuted(to, op)
    gains_nat = tm[0, 0:1, :]
    gcol = jnp.concatenate([column(gains_nat[:, 0:TB]), column(gains_nat[:, TB:])], axis=0)
    gp[...] = jnp.sum(p2[...].astype(F32) * gcol, axis=0, keepdims=True)
    with jax.named_scope("w_tok3"):
        tok_forward(2)

    with jax.named_scope("w_sq"):
        wait_for(sq_z.at[0 : NZ - 1], sq_r2)
    total = sq_z[0]
    for j in range(1, NZ):
        total += sq_z[j]
    norms = jnp.sqrt(total + 1e-06)
    norm_i, norm_s = norms[:, 0:W3], norms[:, W3:]
    vecs[0:1, :] = norm_i / norm_s
    vecs[1:2, :] = norm_i / (norm_s * norm_s * norm_s)
    vecs[2:3, :] = 1.0 / (norm_i * norm_s)

    def normalize(m):
        cols = slice(m * HALF, (m + 1) * HALF)
        ratio = vecs[0:1, cols]

        def body(i, rows):
            nrm[rows, cols] = (block(sv_all, i, cols) * ratio).astype(BF16)

        loop16(body)

    c_0, c_1, c_2 = (slice(m * HALF, (m + 1) * HALF) for m in range(3))
    c_01 = slice(0, 2 * HALF)

    with jax.named_scope("w_sv_gate"):
        end_matrix(sv_ends, 0)
    for s in sum(COARSE, ()):
        in_g[s].start()
    normalize(0)
    f_a[...] = dot(qp[...], nrm[:, c_0])
    with jax.named_scope("w_sv_up"):
        end_matrix(sv_ends, 1)
    normalize(1)
    f_b[...] = dot(qp[...], nrm[:, c_1])

    def q_body(i, rows):
        v = f_a[rows, :]
        up = f_b[rows, :]
        s = jax.nn.sigmoid(v)
        a = v * s
        act[rows, :] = a
        ups[rows, :] = up * (s * (1.0 + v * (1.0 - s)))
        qh[rows, :] = (a * up).astype(BF16)

    loop16(q_body)
    with jax.named_scope("w_sv_down"):
        end_matrix(sv_ends, 2)
    normalize(2)
    ap[...] = dot(qh[...], nrm[:, c_2], NT)
    aprs = sems.take()
    share(ap, apr, aprs, sibling)

    gains = gp[...]
    with jax.named_scope("w_ap"):
        wait_for(apr, aprs)
    for b in range(2):
        rows = slice(b * TB, (b + 1) * TB)
        out = ap[rows, :] + apr[rows, :]
        ao[rows, :] = out
        ss[0:1, rows] = row_of(jnp.sum(out * out, axis=1, keepdims=True))
        ss[1:2, rows] = row_of(jnp.sum(out * gains * op[rows, :].astype(F32), axis=1, keepdims=True))
    ss_r = sems.take()
    for j in range(1, 4):
        a, b = plane(j)
        share(ss, sr.at[j - 1], ss_r, dev(yh_=a, yl_=b))
    with jax.named_scope("w_in_mid"):
        wait_for(x1_ref, in_x1)
        wait_bytes(z1_bytes, in_z1)
        for s in sum(COARSE, ()):
            in_g[s].mid(True)
    with jax.named_scope("w_tok4"):
        tok_ready(2)
    permuted(tk, kp)
    permuted(tv, vp)

    with jax.named_scope("w_sums"):
        wait_for(sr, ss_r)
    tot = ss[...] + sr[0] + sr[1] + sr[2]
    full = HEADS * HD
    root_row = jnp.sqrt(tot[0:1, :] / full + 1e-05)
    inv_row = 1.0 / root_row
    fac_row = (tot[1:2, :] / full) / (root_row * root_row * root_row)
    for b in range(2):
        rows = slice(b * TB, (b + 1) * TB)
        inv = column(inv_row[:, rows])
        fac = column(fac_row[:, rows])
        od[rows, :] = (gains * op[rows, :].astype(F32) * inv - ao[rows, :] * fac).astype(BF16)

    def project(m, grad):
        cols = slice(m * HALF, (m + 1) * HALF)
        agr[...] = grad

        def step(i, carry):
            return carry + block(sv_all, i, cols) * agr[pl.ds(pl.multiple_of(i * 16, 16), 16), :]

        part = jnp.sum(lax.fori_loop(0, 16, step, jnp.zeros((16, HALF), F32)), axis=0, keepdims=True)
        ratio = vecs[0:1, cols]
        fall = part * vecs[1:2, cols]
        vecs[3:4, cols] = part * vecs[2:3, cols]

        def body(i, rows):
            set_block(s1, i, cols, agr[rows, :] * ratio - block(sv_all, i, cols) * fall)

        loop16(body)

    project(2, dot(od[...], qh[...], TN))
    for s in FINE[2]:
        sc1[s].start()
    f_a[...] = dot(od[...], nrm[:, c_2])

    def d_body(i, rows):
        dh = f_a[rows, :]
        dgu[rows, 0:HALF] = (dh * ups[rows, :]).astype(BF16)
        dgu[rows, HALF : 2 * HALF] = (dh * act[rows, :]).astype(BF16)

    loop16(d_body)
    project(0, dot(qp[...], dgu[:, 0:HALF], TN))
    for s in FINE[0]:
        sc1[s].start()
    project(1, dot(qp[...], dgu[:, HALF : 2 * HALF], TN))
    for s in FINE[1]:
        sc1[s].start()

    give_send, give_recv = sems.many(2)

    class Give:
        def __init__(self, bufs, scale):
            self.part, self.got, self.out, self.back = bufs
            self.scale = scale
            self.r1 = sems.take()
            self.s2, self.r2 = give_send, give_recv

        def first(self, part):
            self.part[...] = part.reshape(2, TB, HD)

        def start(self, part, more=False):
            part = part.reshape(2, TB, HD)
            self.part[...] = self.part[...] + part if more else part
            share(self.part.at[1 - c], self.got, self.r1, sibling)

        def finish(self):
            wait_for(self.got, self.r1)
            total = self.part[c] + self.got[...]
            if self.scale:
                total = total * column(tm[c, 1:2, 0:TB])
            self.out[...] = dot(total.astype(BF16), p2[...], NT).astype(BF16)

            @pl.when(native)
            def _():
                keep(self.out, self.back, self.r2)

            @pl.when(foreign)
            def _():
                send(self.out, self.back, self.s2, self.r2, swapped)

    give_q, give_k, give_v = (Give(rets[i], i == 2) for i in range(3))
    give_q.start(dot(dgu[...], nrm[:, c_01], NT))
    with jax.named_scope("w_sc1_mid"):
        for s in (DOWN_1, DOWN_2, GATE_1, GATE_2, DOWN_X, UP_1, UP_2, GATE_X, UP_X):
            sc1[s].mid()
    with jax.named_scope("w_in_end"):
        wait_bytes(3 * matrix_bytes, in_ends[0])
    ini[...] = in_all[...].reshape(HD, W3)
    f_a[...] = dot(kp[...], ini[:, c_0])
    f_b[...] = dot(kp[...], ini[:, c_1])
    f_c[...] = dot(vp[...], ini[:, c_2])

    def k_body(i, rows):
        v = f_a[rows, :]
        up = f_b[rows, :]
        proj = f_c[rows, :]
        s = jax.nn.sigmoid(v)
        a = v * s
        slope = s * (1.0 + v * (1.0 - s))
        bend = s * (1.0 - s) * (2.0 + v * (1.0 - 2.0 * s))
        k_act[rows, :] = a
        kc1[rows, :] = up * slope
        kc2[rows, :] = proj * slope
        kc3[rows, :] = proj * up * bend
        kh[rows, :] = (a * up).astype(BF16)
        rise[rows, 0:HALF] = (proj * up * slope).astype(BF16)
        rise[rows, HALF : 2 * HALF] = (proj * a).astype(BF16)

    loop16(k_body)
    for s in (DOWN_X, DOWN_1, DOWN_2, GATE_1, GATE_X, GATE_2, UP_1, UP_2, UP_X):
        with jax.named_scope("w_sc1_end"):
            res = sc1[s].end()
        cols = slice(s[0], s[0] + s[1])
        c_all[x, z, :, cols] = res.astype(BF16)
        c_g[s].start()
        fs[0, :, cols] = res[0:4]
        fs[1, :, cols] = res[4:8]

    f_send, f_recv = sems.many(2)
    for hc in range(2):

        @pl.when(c == hc)
        def _(hc=hc):
            @pl.when(native)
            def _():
                keep(fs.at[yh], fr.at[hc], f_recv)

            @pl.when(foreign)
            def _():
                send(fs.at[yh], fr.at[hc], f_send, f_recv, sibling)

            send(fs.at[1 - yh], fr.at[hc], f_send, f_recv, dev(yh_=1 - yh, c_=yh))

    give_q.finish()
    with jax.named_scope("w_c_mid"):
        for s in (DOWN_X, GATE_X, DOWN_1, DOWN_2, UP_X, GATE_1, GATE_2, UP_1, UP_2):
            c_g[s].mid()

    def cot_of(m):
        cols = slice(m * HALF, (m + 1) * HALF)
        cot[:, cols] = c_all[:, :, :, cols].reshape(HD, HALF)
        return cot[:, cols]

    with jax.named_scope("w_c_down"):
        end_matrix(c_ends, 2)
    f_c[...] = dot(vp[...], cot_of(2))
    give_v.first(dot(kh[...], cot[:, c_2], NT))
    with jax.named_scope("w_c_gate"):
        end_matrix(c_ends, 0)
    f_a[...] = dot(kp[...], cot_of(0))
    def up_body(i, rows):
        bk[rows, HALF : 2 * HALF] = (f_a[rows, :] * kc2[rows, :] + f_c[rows, :] * k_act[rows, :]).astype(BF16)

    loop16(up_body)

    def inner(m, grad):
        cols = slice(m * HALF, (m + 1) * HALF)
        extra = vecs[3:4, cols]
        agr[...] = grad

        def body(i, rows):
            set_block(s2, i, cols, agr[rows, :] + ini[rows, cols].astype(F32) * extra)

        loop16(body)

    inner(1, dot(kp[...], bk[:, HALF : 2 * HALF], TN))
    for s in FINE[1]:
        sc2[s].start()
    give_k.first(dot(rise[:, 0:HALF], cot[:, c_0], NT))
    with jax.named_scope("w_c_up"):
        end_matrix(c_ends, 1)
    f_b[...] = dot(kp[...], cot_of(1))

    def b_body(i, rows):
        bg = f_a[rows, :]
        bu = f_b[rows, :]
        c1 = kc1[rows, :]
        bp[rows, :] = (bg * c1 + bu * k_act[rows, :]).astype(BF16)
        bk[rows, 0:HALF] = (bg * kc3[rows, :] + (bu * kc2[rows, :] + f_c[rows, :] * c1)).astype(BF16)

    loop16(b_body)
    inner(2, dot(vp[...], bp[...], TN))
    for s in FINE[2]:
        sc2[s].start()
    inner(0, dot(kp[...], bk[:, 0:HALF], TN))
    for s in FINE[0]:
        sc2[s].start()
    give_v.start(dot(bp[...], ini[:, c_2], NT), True)
    give_k.start(dot(rise[:, HALF:], cot[:, c_1], NT) + dot(bk[...], ini[:, c_01], NT), True)
    with jax.named_scope("w_give_v"):
        give_v.finish()
    with jax.named_scope("w_give_k"):
        give_k.finish()
    with jax.named_scope("w_sc2_mid"):
        for s in (UP_1, UP_2, DOWN_1, DOWN_2, UP_X, GATE_1, GATE_2, DOWN_X, GATE_X):
            sc2[s].mid()
    wait_for(fr, f_recv)

    def rows_out(m):
        wait_bytes(2 * (NZ * 4 * 256 * 2 + NX * 4 * 128 * 2), own_recv[FINE[m][0]])
        for s in FINE[m]:
            sc2[s].end()

    with jax.named_scope("w_sc2_end"):
        rows_out(1)
        rows_out(2)
    with jax.named_scope("w_collect"):
        wait_bytes(3 * TB * HD * 2, give_recv)
        for give, out in ((give_q, gq_out), (give_k, gk_out), (give_v, gv_out)):
            out[...] = give.back[...]
    with jax.named_scope("w_sc2_end"):
        rows_out(0)

    assert sum(sent_bytes) % 4096 == 0 and sum(sent_bytes) // 512 <= SENT_ROWS
    with jax.named_scope("w_sent"):
        wait_for(sent.at[0 : sum(sent_bytes) // 512], shared_sem)
        for ref, sem in at_end:
            wait_for(ref, sem)

        @pl.when(native)
        def _():
            wait_for(stage.at[0], w_send)
            wait_for(fr.at[0], f_send)
            wait_for(own_bytes, own_send)

        @pl.when(foreign)
        def _():
            wait_bytes(2 * 6 * 4 * HALF * 2, w_send)
            wait_bytes(sum(group_bytes), tok_send)
            wait_for(fr, f_send)
            wait_bytes(3 * TB * HD * 2, give_send)
            wait_bytes(3 * 2 * (NZ * 4 * 256 * 2 + NX * 4 * 128 * 2), own_send)


def write_out(*refs):
    sem = refs[-1]
    half = (len(refs) - 1) // 2
    copies = [pltpu.make_async_copy(refs[i], refs[half + i], sem.at[i]) for i in range(half)]
    for cp in copies:
        cp.start()
    for cp in copies:
        cp.wait()


def local(*args):
    (queries, key_rows, value_rows, out_grad, step_sizes, norm_gain, gate_init, up_init, down_init,
     gate_saved, up_saved, down_saved) = args
    ins = [a[0] for a in (queries, key_rows, value_rows, out_grad)]
    ins += [step_sizes, norm_gain]
    ins += [a[0] for a in (gate_init, up_init, down_init, gate_saved, up_saved, down_saved)]
    shapes = [((TB, HD), BF16)] * 3 + [((4, HID), F32)] * 3

    def v(dtype, *shape):
        return pltpu.VMEM(shape, dtype)

    def rs_bufs(owners):
        out = []
        for _, n, axis in STREAMS:
            if axis == "z":
                first, count = v(BF16, NX - 1, NZ, 8, n), NZ
            else:
                first, count = v(BF16, NZ - 1, NX, 8, n), NX
            if owners:
                out += [first, v(BF16, count, 2, 4, n), v(BF16, 2, count, 4, n)]
            else:
                out += [first, v(BF16, count, 8, n), v(BF16, count - 1, 8, n)]
        return out

    ret = [v(F32, 2, TB, HD), v(F32, TB, HD), v(BF16, TB, HD), v(BF16, TB, HD)]
    scratch = [
        pltpu.SemaphoreType.DMA((N_SEMS,)),
        *[v(a.dtype, *a.shape) for a in ins[:6]],
        *[v(BF16, 4, HID)] * 6,
        v(BF16, 2, 6, 4, HALF), v(F32, 8, HD), v(BF16, TB, HD),
        *[v(BF16, 2, TB, HD)] * 4, v(F32, 2, 8, HD),
        *[v(BF16, TT, HD)] * 4, v(F32, 1, HD),
        *[v(BF16, NX, NZ, 8, W3)] * 3,
        v(F32, NZ, 1, 2 * W3), v(F32, NX, 1, 2 * W3), v(BF16, HD, HD),
        v(BF16, HD, W3), v(BF16, HD, W3), v(F32, 8, W3), v(BF16, HD, W3),
        *[v(F32, TT, HALF)] * 5, v(BF16, TT, HALF), v(BF16, TT, 2 * HALF),
        *[v(F32, TT, HD)] * 3, v(F32, 8, TT), v(F32, 3, 8, TT), v(BF16, TT, HD), v(F32, HD, HALF),
        *[v(BF16, NX, NZ, 8, W3)] * 2,
        *rs_bufs(False), *rs_bufs(True),
        *[v(F32, TT, HALF)] * 4, v(BF16, TT, HALF), v(BF16, TT, 2 * HALF), v(BF16, TT, 2 * HALF), v(BF16, TT, HALF),
        *ret * 3,
        v(F32, 2, 4, W3), v(F32, 2, 4, W3), v(F32, SENT_ROWS, 128),
        v(BF16, 8, W3), v(F32, 111, 2, 128),
    ]
    vm = pl.BlockSpec(memory_space=pltpu.VMEM)
    res = pl.pallas_call(
        kernel,
        out_shape=[pltpu.VMEM(s, d) for s, d in shapes],
        in_specs=[pl.BlockSpec(memory_space=pltpu.HBM)] * len(ins),
        out_specs=[vm] * len(shapes),
        scratch_shapes=scratch,
        compiler_params=pltpu.CompilerParams(
            collective_id=0, has_side_effects=True, vmem_limit_bytes=60 * 1024 * 1024
        ),
    )(*[pltpu.with_memory_space_constraint(a, pltpu.HBM) for a in ins])
    res = pl.pallas_call(
        write_out,
        out_shape=[jax.ShapeDtypeStruct(s, d) for s, d in shapes],
        in_specs=[vm] * len(shapes),
        out_specs=[pl.BlockSpec(memory_space=pl.ANY)] * len(shapes),
        scratch_shapes=[pltpu.SemaphoreType.DMA((len(shapes),))],
    )(*[pltpu.with_memory_space_constraint(r, pltpu.VMEM) for r in res])
    return tuple(r[None] for r in res)


def solution(mesh):
    three = P("head", "seq", None)
    return jax.shard_map(
        local,
        mesh=mesh,
        in_specs=(three, three, three, three, P("head", "seq"), P("head", None)) + (three,) * 6,
        out_specs=(three,) * 6,
        check_vma=False,
    )
```

```python
import math

import jax
import jax.numpy as jnp
from jax import lax
from jax.experimental import pallas as pl
from jax.experimental.pallas import tpu as pltpu
from jax.sharding import PartitionSpec as P

HEADS = 4
HD = 256
HID = 768
HALF = HID // 2
W3 = 3 * HALF
NX = 4
NZ = 8
FAR_X = (2, 1, 3)
FAR_Z = (4, 3, 5, 2, 6, 1, 7)
TB = 128
TT = 2 * TB
MESH = pl.DeviceIdType.MESH
F32 = jnp.float32
BF16 = jnp.bfloat16

NN = (((1,), (0,)), ((), ()))
NT = (((1,), (1,)), ((), ()))
TN = (((0,), (0,)), ((), ()))

def streams_of(pieces):
    out = []
    for m in range(3):
        first, mine = m * HALF, []
        for n, axis in pieces:
            mine.append((first, n, axis))
            first += n
        out.append(tuple(mine))
    return tuple(out)


FINE = streams_of(((256, "z"), (128, "x")))
COARSE = streams_of(((256, "z"), (128, "x")))
(GATE_1, GATE_X), (UP_1, UP_X), (DOWN_1, DOWN_X) = FINE
STREAMS = sum(FINE, ())
N_SEMS = 71
SENT_ROWS = 7232


def dot(a, b, dims=NN):
    return lax.dot_general(a, b, dims, preferred_element_type=F32)


class Sems:
    def __init__(self, ref):
        self.ref = ref
        self.next = 0

    def take(self):
        self.next += 1
        assert self.next <= self.ref.shape[0]
        return self.ref.at[self.next - 1]

    def many(self, count):
        return [self.take() for _ in range(count)]


def wait_for(ref, sem):
    pltpu.make_async_copy(ref, ref, sem).wait()


def loop16(body):
    @pl.loop(0, 16, unroll=4)
    def _(i):
        body(i, pl.ds(pl.multiple_of(i * 16, 16), 16))


def block(buf, i, cols):
    v = buf[lax.div(i, 4), pl.ds(lax.rem(i, 4) * 2, 2), :, cols]
    return v.astype(F32).reshape(16, v.shape[-1])


def set_block(buf, i, cols, value):
    buf[lax.div(i, 4), pl.ds(lax.rem(i, 4) * 2, 2), :, cols] = value.reshape(2, 8, value.shape[-1]).astype(BF16)


def kernel(*refs):
    refs = list(refs)

    def grab(n):
        out = refs[:n]
        del refs[:n]
        return out

    in_hbm = grab(12)
    gq_out, gk_out, gv_out, gg_out, gu_out, gd_out = grab(6)
    (sem_ref,) = grab(1)
    q_in, k_in, v_in, og_in, rate_in, gain_in = in_vmem = grab(6)
    w_in = grab(6)
    stage, msrc, vsrc = grab(3)
    tq, tk, tv, to, tm = grab(5)
    qp, kp, vp, op, gp = grab(5)
    sv_all, in_all, c_all = grab(3)
    sq_z, sq_x, p2, ini, nrm, vecs, cot = grab(7)
    f_a, f_b, f_c, act, ups, qh, dgu = grab(7)
    ap, apr, ao, ss, sr, od, agr = grab(7)
    s1, s2 = grab(2)
    rs1 = [grab(3) for _ in STREAMS]
    rs2 = [grab(3) for _ in STREAMS]
    k_act, kc1, kc2, kc3, kh, rise, bk, bp = grab(8)
    rets = [grab(4) for _ in range(3)]
    fs, fr, sent, x1_ref, own_bytes = grab(5)
    assert not refs

    head = lax.axis_index("head")
    seq = lax.axis_index("seq")
    c = lax.rem(head, 2)
    yl = lax.div(head, 2)
    x = lax.rem(seq, NX)
    z = lax.rem(lax.div(seq, NX), NZ)
    yh = lax.div(seq, NX * NZ)
    native = c == yh
    foreign = jnp.logical_not(native)
    sems = Sems(sem_ref)
    at_end = []

    def dev(yh_=None, z_=None, x_=None, yl_=None, c_=None):
        yh_ = yh if yh_ is None else yh_
        z_ = z if z_ is None else z_
        x_ = x if x_ is None else x_
        yl_ = yl if yl_ is None else yl_
        c_ = c if c_ is None else c_
        return {"head": yl_ * 2 + c_, "seq": (yh_ * NZ + z_) * NX + x_}

    def zp(j):
        return lax.rem(z + j, NZ)

    def xp(j):
        return lax.rem(x + j, NX)

    def plane(j):
        y = lax.rem(yh * 2 + yl + j, 4)
        return lax.div(y, 2), lax.rem(y, 2)

    sibling = dev(c_=1 - c)
    swapped = dev(yh_=c, c_=yh)

    shared_sem = sems.take()
    sent_bytes = []

    def share(src, dst, r_sem, to_dev):
        sent_bytes.append(math.prod(src.shape) * jnp.dtype(src.dtype).itemsize)
        send(src, dst, shared_sem, r_sem, to_dev)

    def send(src, dst, s_sem, r_sem, to_dev):
        pltpu.make_async_remote_copy(
            src_ref=src, dst_ref=dst, send_sem=s_sem, recv_sem=r_sem,
            device_id=to_dev, device_id_type=MESH,
        ).start()

    def keep(src, dst, sem):
        pltpu.make_async_copy(src, dst, sem).start()

    def wait_bytes(count, sem):
        assert count % 4096 == 0
        wait_for(sent.at[0 : count // 512], sem)

    barrier = pltpu.get_barrier_semaphore()
    partners = [dev(z_=zp(j)) for j in range(1, NZ)]
    partners += [dev(x_=xp(j)) for j in range(1, NX)]
    for j in range(1, 4):
        a, b = plane(j)
        partners.append(dev(yh_=a, yl_=b))
    partners.append(sibling)
    partners.append(dev(yh_=1 - yh, c_=1 - c))
    for p in partners:
        pl.semaphore_signal(barrier, inc=1, device_id=p, device_id_type=MESH)
    rows_in, tok_in, rate_sem, gain_sem = sems.many(4)
    for m in range(6):
        keep(in_hbm[6 + m], w_in[m], rows_in)
    for i in (2, 0, 3, 1):
        keep(in_hbm[i], in_vmem[i], tok_in)
    keep(in_hbm[4], rate_in, rate_sem)
    keep(in_hbm[5], gain_in, gain_sem)
    with jax.named_scope("barrier"):
        pl.semaphore_wait(barrier, len(partners))

    w_send = sems.take()
    w_recv = (sems.many(2), sems.many(2))
    wait_bytes(6 * 4 * HID * 2, rows_in)

    def rows_of(m, half):
        return w_in[m].at[:, pl.ds(half * HALF, HALF)]

    @pl.when(native)
    def _():
        for b in range(2):
            for hf in range(2):

                @pl.when((yh == b) & (c == hf))
                def _(b=b, hf=hf):
                    for m in (3, 4, 5, 0, 1, 2):
                        send(rows_of(m, 1 - hf), stage.at[b, m], w_send, w_recv[m // 3][b], sibling)
                    for m in (3, 4, 5, 0, 1, 2):
                        keep(rows_of(m, hf), stage.at[b, m], w_recv[m // 3][b])

    @pl.when(foreign)
    def _():
        for b in range(2):

            @pl.when(yh == b)
            def _(b=b):
                for m in (3, 4, 5, 0, 1, 2):
                    for hf in range(2):
                        send(rows_of(m, hf), stage.at[b, m], w_send, w_recv[m // 3][b], dev(yh_=c, c_=hf))

    eye = lax.broadcasted_iota(jnp.int32, (TB, TB), 0) == lax.broadcasted_iota(jnp.int32, (TB, TB), 1)

    def column(row):
        return jnp.sum(jnp.where(eye, jnp.broadcast_to(row, (TB, TB)), 0.0), axis=1, keepdims=True)

    def row_of(col):
        return jnp.sum(jnp.where(eye, jnp.broadcast_to(col, (TB, TB)), 0.0), axis=0, keepdims=True)

    wait_bytes(4 * TB * HD * 2, tok_in)
    wait_for(rate_in, rate_sem)
    wait_for(gain_in, gain_sem)
    msrc[...] = jnp.zeros_like(msrc)
    msrc[0:1, :] = gain_in[...]
    msrc[1:2, 0:TB] = rate_in[...]
    vsrc[...] = (column(rate_in[...]) * v_in[...].astype(F32)).astype(BF16)
    ri = lax.broadcasted_iota(jnp.int32, (HD, HD), 0)
    ci = lax.broadcasted_iota(jnp.int32, (HD, HD), 1)
    natural = ((ci >> 2) & 1) * 128 + ((ci >> 3) & 7) * 16 + (ci >> 6) * 4 + (ci & 3)
    p2[...] = jnp.where(ri == natural, 1.0, 0.0).astype(BF16)
    tok_send = sems.take()
    tok_recv = sems.many(3)
    toks = [(q_in, tq), (msrc, tm), (og_in, to), (k_in, tk), (vsrc, tv)]
    groups = ((0,), (1, 2), (3, 4))
    group_bytes = (TB * HD * 2, TB * HD * 2 + 8 * HD * 4, TB * HD * 4)

    @pl.when(native)
    def _():
        for g, which in enumerate(groups):
            for i in which:
                keep(toks[i][0], toks[i][1].at[c], tok_recv[g])

    @pl.when(foreign)
    def _():
        for g, which in enumerate(groups):
            for i in which:
                send(toks[i][0], toks[i][1].at[yh], tok_send, tok_recv[g], swapped)

    sib_recv = sems.many(3)

    def tok_forward(g):
        wait_bytes(group_bytes[g], tok_recv[g])
        for i in groups[g]:
            dst = toks[i][1]
            share(dst.at[c], dst.at[c], sib_recv[g], sibling)

    def tok_ready(g):
        wait_bytes(group_bytes[g], sib_recv[g])

    class Gather:
        def __init__(self, buf, stream, r1, r2):
            first, n, axis = stream
            self.buf, self.cols, self.axis = buf, pl.ds(first, n), axis
            self.r1, self.r2 = r1, r2

        def start(self):
            own = self.buf.at[x, z, :, self.cols]
            if self.axis == "z":
                for j in FAR_Z:
                    share(own, own, self.r1, dev(z_=zp(j)))
                self.all1 = self.buf.at[0, 0 : NZ - 1, :, self.cols]
            else:
                for j in FAR_X:
                    share(own, own, self.r1, dev(x_=xp(j)))
                self.all1 = self.buf.at[0, 0 : NX - 1, :, self.cols]

        def mid(self, waited=False):
            if not waited:
                wait_for(self.all1, self.r1)
            if self.axis == "z":
                part = self.buf.at[x, :, :, self.cols]
                for j in FAR_X:
                    share(part, part, self.r2, dev(x_=xp(j)))
            else:
                part = self.buf.at[:, z, :, self.cols]
                for j in FAR_Z:
                    share(part, part, self.r2, dev(z_=zp(j)))

    class Scatter:
        def __init__(self, buf, stream, bufs, owners=None):
            first, n, axis = stream
            self.buf, self.cols, self.axis, self.owners = buf, slice(first, first + n), axis, owners
            self.got1, self.mine, self.got2 = bufs
            self.r1 = sems.take()
            self.s2, self.r2 = owners if owners else (None, sems.take())

        def start(self):
            cols = pl.ds(self.cols.start, self.cols.stop - self.cols.start)
            if self.axis == "z":
                for j in FAR_X:
                    share(self.buf.at[xp(j), :, :, cols], self.got1.at[j - 1], self.r1, dev(x_=xp(j)))
            else:
                for j in FAR_Z:
                    share(self.buf.at[:, zp(j), :, cols], self.got1.at[j - 1], self.r1, dev(z_=zp(j)))

        def mid(self):
            wait_for(self.got1, self.r1)
            count = NZ if self.axis == "z" else NX

            @pl.loop(0, count, unroll=True)
            def _(i):
                if self.axis == "z":
                    total = self.buf[x, i, :, self.cols].astype(F32)
                else:
                    total = self.buf[i, z, :, self.cols].astype(F32)
                for j in range(self.got1.shape[0]):
                    total += self.got1[j, i].astype(F32)
                if self.owners:
                    self.mine[i, 0] = total[0:4].astype(BF16)
                    self.mine[i, 1] = total[4:8].astype(BF16)
                else:
                    self.mine[i] = total.astype(BF16)

            if not self.owners:
                for j in FAR_Z if self.axis == "z" else FAR_X:
                    if self.axis == "z":
                        share(self.mine.at[zp(j)], self.got2.at[j - 1], self.r2, dev(z_=zp(j)))
                    else:
                        share(self.mine.at[xp(j)], self.got2.at[j - 1], self.r2, dev(x_=xp(j)))
                return
            for j in (*FAR_Z, 0) if self.axis == "z" else (*FAR_X, 0):
                for b in range(2):
                    if self.axis == "z":
                        src, to_dev = self.mine.at[zp(j), b], dev(yh_=b, z_=zp(j), c_=yh)
                    else:
                        src, to_dev = self.mine.at[xp(j), b], dev(yh_=b, x_=xp(j), c_=yh)
                    if j > 0:
                        send(src, self.got2.at[c, j], self.s2, self.r2, to_dev)
                        continue
                    here = native & (yh == b)

                    @pl.when(here)
                    def _(src=src, j=j):
                        keep(src, self.got2.at[c, j], self.r2)

                    @pl.when(jnp.logical_not(here))
                    def _(src=src, j=j, to_dev=to_dev):
                        send(src, self.got2.at[c, j], self.s2, self.r2, to_dev)

        def end(self):
            if not self.owners:
                wait_for(self.got2, self.r2)
            if self.owners:
                for hc in range(2):
                    total = fr[hc, :, self.cols]
                    for j in range(self.got2.shape[1]):
                        total += self.got2[hc, j].astype(F32)
                    first = self.cols.start
                    m = first // HALF
                    lo = first - m * HALF + hc * HALF
                    (gg_out, gu_out, gd_out)[m][:, lo : lo + self.cols.stop - first] = total
                return None
            total = self.mine[z if self.axis == "z" else x].astype(F32)
            for j in range(self.got2.shape[0]):
                total += self.got2[j].astype(F32)
            return total

    assert 3 * (NX - 1) * 8 * 128 == 8 * W3
    z1_bytes = 3 * (NZ - 1) * 8 * 256 * 2
    matrix_bytes = (NX - 1) * NZ * 8 * 256 * 2 + (NZ - 1) * NX * 8 * 128 * 2

    def gathers(buf, matrices, x1_shared, z1_shared, all2_shared):
        x1 = sems.take() if x1_shared else None
        z1 = sems.take() if z1_shared else None
        r2 = sems.take() if all2_shared else None
        out, ends = {}, []
        for pair in matrices:
            mine = r2 if all2_shared else sems.take()
            ends.append(mine)
            for s in pair:
                one = z1 if s[2] == "z" else x1
                out[s] = Gather(buf, s, sems.take() if one is None else one, mine)
        return out, x1, z1, ends

    def end_matrix(ends, m):
        wait_bytes(matrix_bytes, ends[m])

    sv_g, sv_x1, _, sv_ends = gathers(sv_all, COARSE, True, False, False)
    in_g, in_x1, in_z1, in_ends = gathers(in_all, COARSE, True, True, True)
    c_g, _, _, c_ends = gathers(c_all, FINE, False, False, False)
    sc1 = {s: Scatter(s1, s, rs1[i]) for i, s in enumerate(STREAMS)}
    own_send = sems.take()
    own_recv = {s: sem for pair, sem in zip(FINE, sems.many(3)) for s in pair}
    sc2 = {s: Scatter(s2, s, rs2[i], (own_send, own_recv[s])) for i, s in enumerate(STREAMS)}

    with jax.named_scope("w_rows"):
        for b in range(2):
            wait_for(stage.at[0, 3:6], w_recv[1][b])

    def eight(first):
        return jnp.concatenate(
            [jnp.concatenate([stage[b, m].astype(F32) for m in range(first, first + 3)], axis=1) for b in range(2)],
            axis=0,
        )

    saved8 = eight(3)
    sv_all[x, z] = saved8.astype(BF16)
    for s in sum(COARSE, ()):
        sv_g[s].start()
    for b in range(2):
        wait_for(stage.at[0, 0:3], w_recv[0][b])
    init8 = eight(0)
    in_all[x, z] = init8.astype(BF16)
    sq_x[x, :, 0:W3] = jnp.sum(init8 * init8, axis=0, keepdims=True)
    sq_x[x, :, W3:] = jnp.sum(saved8 * saved8, axis=0, keepdims=True)
    sq_s1, sq_r1, sq_s2, sq_r2 = sems.many(4)
    for j in range(1, NX):
        send(sq_x.at[x], sq_x.at[x], sq_s1, sq_r1, dev(x_=xp(j)))
    at_end.append((sq_x.at[0 : NX - 1], sq_s1))

    with jax.named_scope("w_tok1"):
        tok_forward(0)
        tok_forward(1)
    with jax.named_scope("w_sv_mid"):
        wait_for(sq_x.at[0 : NX - 1], sq_r1)
        sq_z[z] = sq_x[0] + sq_x[1] + sq_x[2] + sq_x[3]
        for j in FAR_Z:
            send(sq_z.at[z], sq_z.at[z], sq_s2, sq_r2, dev(z_=zp(j)))
        at_end.append((sq_z.at[0 : NZ - 1], sq_s2))
        wait_for(x1_ref, sv_x1)
        for s in [pair[1] for pair in COARSE] + [pair[0] for pair in COARSE]:
            sv_g[s].mid(s[2] == "x")

    def permuted(src, dst):
        dst[...] = dot(src[...].reshape(TT, HD), p2[...]).astype(BF16)

    with jax.named_scope("w_tok2"):
        tok_ready(0)
        tok_ready(1)
    permuted(tq, qp)
    permuted(to, op)
    gains_nat = tm[0, 0:1, :]
    gcol = jnp.concatenate([column(gains_nat[:, 0:TB]), column(gains_nat[:, TB:])], axis=0)
    gp[...] = jnp.sum(p2[...].astype(F32) * gcol, axis=0, keepdims=True)
    with jax.named_scope("w_tok3"):
        tok_forward(2)

    with jax.named_scope("w_sq"):
        wait_for(sq_z.at[0 : NZ - 1], sq_r2)
    total = sq_z[0]
    for j in range(1, NZ):
        total += sq_z[j]
    norms = jnp.sqrt(total + 1e-06)
    norm_i, norm_s = norms[:, 0:W3], norms[:, W3:]
    vecs[0:1, :] = norm_i / norm_s
    vecs[1:2, :] = norm_i / (norm_s * norm_s * norm_s)
    vecs[2:3, :] = 1.0 / (norm_i * norm_s)

    def normalize(m):
        cols = slice(m * HALF, (m + 1) * HALF)
        ratio = vecs[0:1, cols]

        def body(i, rows):
            nrm[rows, cols] = (block(sv_all, i, cols) * ratio).astype(BF16)

        loop16(body)

    c_0, c_1, c_2 = (slice(m * HALF, (m + 1) * HALF) for m in range(3))
    c_01 = slice(0, 2 * HALF)

    with jax.named_scope("w_sv_gate"):
        end_matrix(sv_ends, 0)
    for s in sum(COARSE, ()):
        in_g[s].start()
    normalize(0)
    f_a[...] = dot(qp[...], nrm[:, c_0])
    with jax.named_scope("w_sv_up"):
        end_matrix(sv_ends, 1)
    normalize(1)
    f_b[...] = dot(qp[...], nrm[:, c_1])

    def q_body(i, rows):
        v = f_a[rows, :]
        up = f_b[rows, :]
        s = jax.nn.sigmoid(v)
        a = v * s
        act[rows, :] = a
        ups[rows, :] = up * (s * (1.0 + v * (1.0 - s)))
        qh[rows, :] = (a * up).astype(BF16)

    loop16(q_body)
    with jax.named_scope("w_sv_down"):
        end_matrix(sv_ends, 2)
    normalize(2)
    ap[...] = dot(qh[...], nrm[:, c_2], NT)
    aprs = sems.take()
    share(ap, apr, aprs, sibling)

    gains = gp[...]
    with jax.named_scope("w_ap"):
        wait_for(apr, aprs)
    for b in range(2):
        rows = slice(b * TB, (b + 1) * TB)
        out = ap[rows, :] + apr[rows, :]
        ao[rows, :] = out
        ss[0:1, rows] = row_of(jnp.sum(out * out, axis=1, keepdims=True))
        ss[1:2, rows] = row_of(jnp.sum(out * gains * op[rows, :].astype(F32), axis=1, keepdims=True))
    ss_r = sems.take()
    for j in range(1, 4):
        a, b = plane(j)
        share(ss, sr.at[j - 1], ss_r, dev(yh_=a, yl_=b))
    with jax.named_scope("w_in_mid"):
        wait_for(x1_ref, in_x1)
        wait_bytes(z1_bytes, in_z1)
        for s in sum(COARSE, ()):
            in_g[s].mid(True)
    with jax.named_scope("w_tok4"):
        tok_ready(2)
    permuted(tk, kp)
    permuted(tv, vp)

    with jax.named_scope("w_sums"):
        wait_for(sr, ss_r)
    tot = ss[...] + sr[0] + sr[1] + sr[2]
    full = HEADS * HD
    root_row = jnp.sqrt(tot[0:1, :] / full + 1e-05)
    inv_row = 1.0 / root_row
    fac_row = (tot[1:2, :] / full) / (root_row * root_row * root_row)
    for b in range(2):
        rows = slice(b * TB, (b + 1) * TB)
        inv = column(inv_row[:, rows])
        fac = column(fac_row[:, rows])
        od[rows, :] = (gains * op[rows, :].astype(F32) * inv - ao[rows, :] * fac).astype(BF16)

    def project(m, grad):
        cols = slice(m * HALF, (m + 1) * HALF)
        agr[...] = grad

        def step(i, carry):
            return carry + block(sv_all, i, cols) * agr[pl.ds(pl.multiple_of(i * 16, 16), 16), :]

        part = jnp.sum(lax.fori_loop(0, 16, step, jnp.zeros((16, HALF), F32), unroll=4), axis=0, keepdims=True)
        ratio = vecs[0:1, cols]
        fall = part * vecs[1:2, cols]
        vecs[3:4, cols] = part * vecs[2:3, cols]

        def body(i, rows):
            set_block(s1, i, cols, agr[rows, :] * ratio - block(sv_all, i, cols) * fall)

        loop16(body)

    project(2, dot(od[...], qh[...], TN))
    for s in FINE[2]:
        sc1[s].start()
    f_a[...] = dot(od[...], nrm[:, c_2])

    def d_body(i, rows):
        dh = f_a[rows, :]
        dgu[rows, 0:HALF] = (dh * ups[rows, :]).astype(BF16)
        dgu[rows, HALF : 2 * HALF] = (dh * act[rows, :]).astype(BF16)

    loop16(d_body)
    project(0, dot(qp[...], dgu[:, 0:HALF], TN))
    for s in FINE[0]:
        sc1[s].start()
    project(1, dot(qp[...], dgu[:, HALF : 2 * HALF], TN))
    for s in FINE[1]:
        sc1[s].start()

    give_send, give_recv = sems.many(2)

    class Give:
        def __init__(self, bufs, scale):
            self.part, self.got, self.out, self.back = bufs
            self.scale = scale
            self.r1 = sems.take()
            self.s2, self.r2 = give_send, give_recv

        def first(self, part):
            self.part[...] = part.reshape(2, TB, HD)

        def start(self, part, more=False):
            part = part.reshape(2, TB, HD)
            self.part[...] = self.part[...] + part if more else part
            share(self.part.at[1 - c], self.got, self.r1, sibling)

        def finish(self):
            wait_for(self.got, self.r1)
            total = self.part[c] + self.got[...]
            if self.scale:
                total = total * column(tm[c, 1:2, 0:TB])
            self.out[...] = dot(total.astype(BF16), p2[...], NT).astype(BF16)

            @pl.when(native)
            def _():
                keep(self.out, self.back, self.r2)

            @pl.when(foreign)
            def _():
                send(self.out, self.back, self.s2, self.r2, swapped)

    give_q, give_k, give_v = (Give(rets[i], i == 2) for i in range(3))
    give_q.start(dot(dgu[...], nrm[:, c_01], NT))
    with jax.named_scope("w_sc1_mid"):
        for s in (DOWN_1, GATE_1, DOWN_X, UP_1, GATE_X, UP_X):
            sc1[s].mid()
    with jax.named_scope("w_in_end"):
        wait_bytes(3 * matrix_bytes, in_ends[0])
    ini[...] = in_all[...].reshape(HD, W3)
    f_a[...] = dot(kp[...], ini[:, c_0])
    f_b[...] = dot(kp[...], ini[:, c_1])
    f_c[...] = dot(vp[...], ini[:, c_2])

    def k_body(i, rows):
        v = f_a[rows, :]
        up = f_b[rows, :]
        proj = f_c[rows, :]
        s = jax.nn.sigmoid(v)
        a = v * s
        slope = s * (1.0 + v * (1.0 - s))
        bend = s * (1.0 - s) * (2.0 + v * (1.0 - 2.0 * s))
        k_act[rows, :] = a
        kc1[rows, :] = up * slope
        kc2[rows, :] = proj * slope
        kc3[rows, :] = proj * up * bend
        kh[rows, :] = (a * up).astype(BF16)
        rise[rows, 0:HALF] = (proj * up * slope).astype(BF16)
        rise[rows, HALF : 2 * HALF] = (proj * a).astype(BF16)

    loop16(k_body)
    for s in (DOWN_X, DOWN_1, GATE_1, GATE_X, UP_1, UP_X):
        with jax.named_scope("w_sc1_end"):
            res = sc1[s].end()
        cols = slice(s[0], s[0] + s[1])
        c_all[x, z, :, cols] = res.astype(BF16)
        c_g[s].start()
        fs[0, :, cols] = res[0:4]
        fs[1, :, cols] = res[4:8]

    f_send, f_recv = sems.many(2)
    for hc in range(2):

        @pl.when(c == hc)
        def _(hc=hc):
            @pl.when(native)
            def _():
                keep(fs.at[yh], fr.at[hc], f_recv)

            @pl.when(foreign)
            def _():
                send(fs.at[yh], fr.at[hc], f_send, f_recv, sibling)

            send(fs.at[1 - yh], fr.at[hc], f_send, f_recv, dev(yh_=1 - yh, c_=yh))

    give_q.finish()
    with jax.named_scope("w_c_mid"):
        for s in (DOWN_X, GATE_X, DOWN_1, UP_X, GATE_1, UP_1):
            c_g[s].mid()

    def cot_of(m):
        cols = slice(m * HALF, (m + 1) * HALF)
        cot[:, cols] = c_all[:, :, :, cols].reshape(HD, HALF)
        return cot[:, cols]

    with jax.named_scope("w_c_down"):
        end_matrix(c_ends, 2)
    f_c[...] = dot(vp[...], cot_of(2))
    give_v.first(dot(kh[...], cot[:, c_2], NT))
    with jax.named_scope("w_c_gate"):
        end_matrix(c_ends, 0)
    f_a[...] = dot(kp[...], cot_of(0))
    def up_body(i, rows):
        bk[rows, HALF : 2 * HALF] = (f_a[rows, :] * kc2[rows, :] + f_c[rows, :] * k_act[rows, :]).astype(BF16)

    loop16(up_body)

    def inner(m, grad):
        cols = slice(m * HALF, (m + 1) * HALF)
        extra = vecs[3:4, cols]
        agr[...] = grad

        def body(i, rows):
            set_block(s2, i, cols, agr[rows, :] + ini[rows, cols].astype(F32) * extra)

        loop16(body)

    inner(1, dot(kp[...], bk[:, HALF : 2 * HALF], TN))
    for s in FINE[1]:
        sc2[s].start()
    give_k.first(dot(rise[:, 0:HALF], cot[:, c_0], NT))
    with jax.named_scope("w_c_up"):
        end_matrix(c_ends, 1)
    f_b[...] = dot(kp[...], cot_of(1))

    def b_body(i, rows):
        bg = f_a[rows, :]
        bu = f_b[rows, :]
        c1 = kc1[rows, :]
        bp[rows, :] = (bg * c1 + bu * k_act[rows, :]).astype(BF16)
        bk[rows, 0:HALF] = (bg * kc3[rows, :] + (bu * kc2[rows, :] + f_c[rows, :] * c1)).astype(BF16)

    loop16(b_body)
    inner(2, dot(vp[...], bp[...], TN))
    for s in FINE[2]:
        sc2[s].start()
    inner(0, dot(kp[...], bk[:, 0:HALF], TN))
    for s in FINE[0]:
        sc2[s].start()
    give_v.start(dot(bp[...], ini[:, c_2], NT), True)
    give_k.start(dot(rise[:, HALF:], cot[:, c_1], NT) + dot(bk[...], ini[:, c_01], NT), True)
    with jax.named_scope("w_give_v"):
        give_v.finish()
    with jax.named_scope("w_give_k"):
        give_k.finish()
    with jax.named_scope("w_sc2_mid"):
        for s in (UP_1, DOWN_1, UP_X, GATE_1, DOWN_X, GATE_X):
            sc2[s].mid()
    wait_for(fr, f_recv)

    def rows_out(m):
        wait_bytes(2 * (NZ * 4 * 256 * 2 + NX * 4 * 128 * 2), own_recv[FINE[m][0]])
        for s in FINE[m]:
            sc2[s].end()

    with jax.named_scope("w_sc2_end"):
        rows_out(1)
        rows_out(2)
    with jax.named_scope("w_collect"):
        wait_bytes(3 * TB * HD * 2, give_recv)
        for give, out in ((give_q, gq_out), (give_k, gk_out), (give_v, gv_out)):
            out[...] = give.back[...]
    with jax.named_scope("w_sc2_end"):
        rows_out(0)

    assert sum(sent_bytes) % 4096 == 0 and sum(sent_bytes) // 512 <= SENT_ROWS
    with jax.named_scope("w_sent"):
        wait_for(sent.at[0 : sum(sent_bytes) // 512], shared_sem)
        for ref, sem in at_end:
            wait_for(ref, sem)

        @pl.when(native)
        def _():
            wait_for(stage.at[0], w_send)
            wait_for(fr.at[0], f_send)
            wait_for(own_bytes, own_send)

        @pl.when(foreign)
        def _():
            wait_bytes(2 * 6 * 4 * HALF * 2, w_send)
            wait_bytes(sum(group_bytes), tok_send)
            wait_for(fr, f_send)
            wait_bytes(3 * TB * HD * 2, give_send)
            wait_bytes(3 * 2 * (NZ * 4 * 256 * 2 + NX * 4 * 128 * 2), own_send)


def write_out(*refs):
    sem = refs[-1]
    half = (len(refs) - 1) // 2
    copies = [pltpu.make_async_copy(refs[i], refs[half + i], sem.at[i]) for i in range(half)]
    for cp in copies:
        cp.start()
    for cp in copies:
        cp.wait()


def local(*args):
    (queries, key_rows, value_rows, out_grad, step_sizes, norm_gain, gate_init, up_init, down_init,
     gate_saved, up_saved, down_saved) = args
    ins = [a[0] for a in (queries, key_rows, value_rows, out_grad)]
    ins += [step_sizes, norm_gain]
    ins += [a[0] for a in (gate_init, up_init, down_init, gate_saved, up_saved, down_saved)]
    shapes = [((TB, HD), BF16)] * 3 + [((4, HID), F32)] * 3

    def v(dtype, *shape):
        return pltpu.VMEM(shape, dtype)

    def rs_bufs(owners):
        out = []
        for _, n, axis in STREAMS:
            if axis == "z":
                first, count = v(BF16, NX - 1, NZ, 8, n), NZ
            else:
                first, count = v(BF16, NZ - 1, NX, 8, n), NX
            if owners:
                out += [first, v(BF16, count, 2, 4, n), v(BF16, 2, count, 4, n)]
            else:
                out += [first, v(BF16, count, 8, n), v(BF16, count - 1, 8, n)]
        return out

    ret = [v(F32, 2, TB, HD), v(F32, TB, HD), v(BF16, TB, HD), v(BF16, TB, HD)]
    scratch = [
        pltpu.SemaphoreType.DMA((N_SEMS,)),
        *[v(a.dtype, *a.shape) for a in ins[:6]],
        *[v(BF16, 4, HID)] * 6,
        v(BF16, 2, 6, 4, HALF), v(F32, 8, HD), v(BF16, TB, HD),
        *[v(BF16, 2, TB, HD)] * 4, v(F32, 2, 8, HD),
        *[v(BF16, TT, HD)] * 4, v(F32, 1, HD),
        *[v(BF16, NX, NZ, 8, W3)] * 3,
        v(F32, NZ, 1, 2 * W3), v(F32, NX, 1, 2 * W3), v(BF16, HD, HD),
        v(BF16, HD, W3), v(BF16, HD, W3), v(F32, 8, W3), v(BF16, HD, W3),
        *[v(F32, TT, HALF)] * 5, v(BF16, TT, HALF), v(BF16, TT, 2 * HALF),
        *[v(F32, TT, HD)] * 3, v(F32, 8, TT), v(F32, 3, 8, TT), v(BF16, TT, HD), v(F32, HD, HALF),
        *[v(BF16, NX, NZ, 8, W3)] * 2,
        *rs_bufs(False), *rs_bufs(True),
        *[v(F32, TT, HALF)] * 4, v(BF16, TT, HALF), v(BF16, TT, 2 * HALF), v(BF16, TT, 2 * HALF), v(BF16, TT, HALF),
        *ret * 3,
        v(F32, 2, 4, W3), v(F32, 2, 4, W3), v(F32, SENT_ROWS, 128),
        v(BF16, 8, W3), v(F32, 111, 2, 128),
    ]
    vm = pl.BlockSpec(memory_space=pltpu.VMEM)
    res = pl.pallas_call(
        kernel,
        out_shape=[pltpu.VMEM(s, d) for s, d in shapes],
        in_specs=[pl.BlockSpec(memory_space=pltpu.HBM)] * len(ins),
        out_specs=[vm] * len(shapes),
        scratch_shapes=scratch,
        compiler_params=pltpu.CompilerParams(
            collective_id=0, has_side_effects=True, vmem_limit_bytes=60 * 1024 * 1024
        ),
    )(*[pltpu.with_memory_space_constraint(a, pltpu.HBM) for a in ins])
    res = pl.pallas_call(
        write_out,
        out_shape=[jax.ShapeDtypeStruct(s, d) for s, d in shapes],
        in_specs=[vm] * len(shapes),
        out_specs=[pl.BlockSpec(memory_space=pl.ANY)] * len(shapes),
        scratch_shapes=[pltpu.SemaphoreType.DMA((len(shapes),))],
    )(*[pltpu.with_memory_space_constraint(r, pltpu.VMEM) for r in res])
    return tuple(r[None] for r in res)


def solution(mesh):
    three = P("head", "seq", None)
    return jax.shard_map(
        local,
        mesh=mesh,
        in_specs=(three, three, three, three, P("head", "seq"), P("head", None)) + (three,) * 6,
        out_specs=(three,) * 6,
        check_vma=False,
    )
```

```python
import math

import jax
import jax.numpy as jnp
from jax import lax
from jax.experimental import pallas as pl
from jax.experimental.pallas import tpu as pltpu
from jax.sharding import PartitionSpec as P

HEADS = 4
HD = 256
HID = 768
HALF = HID // 2
W3 = 3 * HALF
NX = 4
NZ = 8
FAR_X = (2, 1, 3)
FAR_Z = (4, 3, 5, 2, 6, 1, 7)
TB = 128
TT = 2 * TB
MESH = pl.DeviceIdType.MESH
F32 = jnp.float32
BF16 = jnp.bfloat16

NN = (((1,), (0,)), ((), ()))
NT = (((1,), (1,)), ((), ()))
TN = (((0,), (0,)), ((), ()))

def streams_of(pieces):
    out = []
    for m in range(3):
        first, mine = m * HALF, []
        for n, axis in pieces:
            mine.append((first, n, axis))
            first += n
        out.append(tuple(mine))
    return tuple(out)


FINE = streams_of(((256, "z"), (128, "x")))
COARSE = streams_of(((256, "z"), (128, "x")))
(GATE_1, GATE_X), (UP_1, UP_X), (DOWN_1, DOWN_X) = FINE
SAVED = COARSE[:2] + (((2 * HALF, HALF, "z"),),)
STREAMS = sum(FINE, ())
N_SEMS = 71
SENT_ROWS = 7232


def dot(a, b, dims=NN):
    return lax.dot_general(a, b, dims, preferred_element_type=F32)


class Sems:
    def __init__(self, ref):
        self.ref = ref
        self.next = 0

    def take(self):
        self.next += 1
        assert self.next <= self.ref.shape[0]
        return self.ref.at[self.next - 1]

    def many(self, count):
        return [self.take() for _ in range(count)]


def wait_for(ref, sem):
    pltpu.make_async_copy(ref, ref, sem).wait()


def loop16(body):
    @pl.loop(0, 16, unroll=4)
    def _(i):
        body(i, pl.ds(pl.multiple_of(i * 16, 16), 16))


def block(buf, i, cols):
    v = buf[lax.div(i, 4), pl.ds(lax.rem(i, 4) * 2, 2), :, cols]
    return v.astype(F32).reshape(16, v.shape[-1])


def set_block(buf, i, cols, value):
    buf[lax.div(i, 4), pl.ds(lax.rem(i, 4) * 2, 2), :, cols] = value.reshape(2, 8, value.shape[-1]).astype(BF16)


def kernel(*refs):
    refs = list(refs)

    def grab(n):
        out = refs[:n]
        del refs[:n]
        return out

    in_hbm = grab(12)
    gq_out, gk_out, gv_out, gg_out, gu_out, gd_out = grab(6)
    (sem_ref,) = grab(1)
    q_in, k_in, v_in, og_in, rate_in, gain_in = in_vmem = grab(6)
    w_in = grab(6)
    stage, msrc, vsrc = grab(3)
    tq, tk, tv, to, tm = grab(5)
    qp, kp, vp, op, gp = grab(5)
    sv_all, in_all, c_all = grab(3)
    sq_z, sq_x, p2, ini, nrm, vecs, cot = grab(7)
    f_a, f_b, f_c, act, ups, qh, dgu = grab(7)
    ap, apr, ao, ss, sr, od, agr = grab(7)
    s1, s2 = grab(2)
    rs1 = [grab(3) for _ in STREAMS]
    rs2 = [grab(3) for _ in STREAMS]
    k_act, kc1, kc2, kc3, kh, rise, bk, bp = grab(8)
    rets = [grab(4) for _ in range(3)]
    fs, fr, sent, x1_ref, own_bytes = grab(5)
    assert not refs

    head = lax.axis_index("head")
    seq = lax.axis_index("seq")
    c = lax.rem(head, 2)
    yl = lax.div(head, 2)
    x = lax.rem(seq, NX)
    z = lax.rem(lax.div(seq, NX), NZ)
    yh = lax.div(seq, NX * NZ)
    native = c == yh
    foreign = jnp.logical_not(native)
    sems = Sems(sem_ref)
    at_end = []

    def dev(yh_=None, z_=None, x_=None, yl_=None, c_=None):
        yh_ = yh if yh_ is None else yh_
        z_ = z if z_ is None else z_
        x_ = x if x_ is None else x_
        yl_ = yl if yl_ is None else yl_
        c_ = c if c_ is None else c_
        return {"head": yl_ * 2 + c_, "seq": (yh_ * NZ + z_) * NX + x_}

    def zp(j):
        return lax.rem(z + j, NZ)

    def xp(j):
        return lax.rem(x + j, NX)

    def plane(j):
        y = lax.rem(yh * 2 + yl + j, 4)
        return lax.div(y, 2), lax.rem(y, 2)

    sibling = dev(c_=1 - c)
    swapped = dev(yh_=c, c_=yh)

    shared_sem = sems.take()
    sent_bytes = []

    def share(src, dst, r_sem, to_dev):
        sent_bytes.append(math.prod(src.shape) * jnp.dtype(src.dtype).itemsize)
        send(src, dst, shared_sem, r_sem, to_dev)

    def send(src, dst, s_sem, r_sem, to_dev):
        pltpu.make_async_remote_copy(
            src_ref=src, dst_ref=dst, send_sem=s_sem, recv_sem=r_sem,
            device_id=to_dev, device_id_type=MESH,
        ).start()

    def keep(src, dst, sem):
        pltpu.make_async_copy(src, dst, sem).start()

    def wait_bytes(count, sem):
        assert count % 4096 == 0
        wait_for(sent.at[0 : count // 512], sem)

    barrier = pltpu.get_barrier_semaphore()
    partners = [dev(z_=zp(j)) for j in range(1, NZ)]
    partners += [dev(x_=xp(j)) for j in range(1, NX)]
    for j in range(1, 4):
        a, b = plane(j)
        partners.append(dev(yh_=a, yl_=b))
    partners.append(sibling)
    partners.append(dev(yh_=1 - yh, c_=1 - c))
    for p in partners:
        pl.semaphore_signal(barrier, inc=1, device_id=p, device_id_type=MESH)
    rows_in, tok_in, rate_sem, gain_sem = sems.many(4)
    for m in range(6):
        keep(in_hbm[6 + m], w_in[m], rows_in)
    for i in (2, 0, 3, 1):
        keep(in_hbm[i], in_vmem[i], tok_in)
    keep(in_hbm[4], rate_in, rate_sem)
    keep(in_hbm[5], gain_in, gain_sem)
    with jax.named_scope("barrier"):
        pl.semaphore_wait(barrier, len(partners))

    w_send = sems.take()
    w_recv = (sems.many(2), sems.many(2))
    wait_bytes(6 * 4 * HID * 2, rows_in)

    def rows_of(m, half):
        return w_in[m].at[:, pl.ds(half * HALF, HALF)]

    @pl.when(native)
    def _():
        for b in range(2):
            for hf in range(2):

                @pl.when((yh == b) & (c == hf))
                def _(b=b, hf=hf):
                    for m in (3, 4, 5, 0, 1, 2):
                        send(rows_of(m, 1 - hf), stage.at[b, m], w_send, w_recv[m // 3][b], sibling)
                    for m in (3, 4, 5, 0, 1, 2):
                        keep(rows_of(m, hf), stage.at[b, m], w_recv[m // 3][b])

    @pl.when(foreign)
    def _():
        for b in range(2):

            @pl.when(yh == b)
            def _(b=b):
                for m in (3, 4, 5, 0, 1, 2):
                    for hf in range(2):
                        send(rows_of(m, hf), stage.at[b, m], w_send, w_recv[m // 3][b], dev(yh_=c, c_=hf))

    eye = lax.broadcasted_iota(jnp.int32, (TB, TB), 0) == lax.broadcasted_iota(jnp.int32, (TB, TB), 1)

    def column(row):
        return jnp.sum(jnp.where(eye, jnp.broadcast_to(row, (TB, TB)), 0.0), axis=1, keepdims=True)

    def row_of(col):
        return jnp.sum(jnp.where(eye, jnp.broadcast_to(col, (TB, TB)), 0.0), axis=0, keepdims=True)

    wait_bytes(4 * TB * HD * 2, tok_in)
    wait_for(rate_in, rate_sem)
    wait_for(gain_in, gain_sem)
    msrc[...] = jnp.zeros_like(msrc)
    msrc[0:1, :] = gain_in[...]
    msrc[1:2, 0:TB] = rate_in[...]
    vsrc[...] = (column(rate_in[...]) * v_in[...].astype(F32)).astype(BF16)
    ri = lax.broadcasted_iota(jnp.int32, (HD, HD), 0)
    ci = lax.broadcasted_iota(jnp.int32, (HD, HD), 1)
    natural = ((ci >> 2) & 1) * 128 + ((ci >> 3) & 7) * 16 + (ci >> 6) * 4 + (ci & 3)
    p2[...] = jnp.where(ri == natural, 1.0, 0.0).astype(BF16)
    tok_send = sems.take()
    tok_recv = sems.many(3)
    toks = [(q_in, tq), (msrc, tm), (og_in, to), (k_in, tk), (vsrc, tv)]
    groups = ((0,), (1, 2), (3, 4))
    group_bytes = (TB * HD * 2, TB * HD * 2 + 8 * HD * 4, TB * HD * 4)

    @pl.when(native)
    def _():
        for g, which in enumerate(groups):
            for i in which:
                keep(toks[i][0], toks[i][1].at[c], tok_recv[g])

    @pl.when(foreign)
    def _():
        for g, which in enumerate(groups):
            for i in which:
                send(toks[i][0], toks[i][1].at[yh], tok_send, tok_recv[g], swapped)

    sib_recv = sems.many(3)

    def tok_forward(g):
        wait_bytes(group_bytes[g], tok_recv[g])
        for i in groups[g]:
            dst = toks[i][1]
            share(dst.at[c], dst.at[c], sib_recv[g], sibling)

    def tok_ready(g):
        wait_bytes(group_bytes[g], sib_recv[g])

    class Gather:
        def __init__(self, buf, stream, r1, r2):
            first, n, axis = stream
            self.buf, self.cols, self.axis = buf, pl.ds(first, n), axis
            self.r1, self.r2 = r1, r2

        def start(self):
            own = self.buf.at[x, z, :, self.cols]
            if self.axis == "z":
                for j in FAR_Z:
                    share(own, own, self.r1, dev(z_=zp(j)))
                self.all1 = self.buf.at[0, 0 : NZ - 1, :, self.cols]
            else:
                for j in FAR_X:
                    share(own, own, self.r1, dev(x_=xp(j)))
                self.all1 = self.buf.at[0, 0 : NX - 1, :, self.cols]

        def mid(self, waited=False):
            if not waited:
                wait_for(self.all1, self.r1)
            if self.axis == "z":
                part = self.buf.at[x, :, :, self.cols]
                for j in FAR_X:
                    share(part, part, self.r2, dev(x_=xp(j)))
            else:
                part = self.buf.at[:, z, :, self.cols]
                for j in FAR_Z:
                    share(part, part, self.r2, dev(z_=zp(j)))

    class Scatter:
        def __init__(self, buf, stream, bufs, owners=None):
            first, n, axis = stream
            self.buf, self.cols, self.axis, self.owners = buf, slice(first, first + n), axis, owners
            self.got1, self.mine, self.got2 = bufs
            self.r1 = sems.take()
            self.s2, self.r2 = owners if owners else (None, sems.take())

        def start(self):
            cols = pl.ds(self.cols.start, self.cols.stop - self.cols.start)
            if self.axis == "z":
                for j in FAR_X:
                    share(self.buf.at[xp(j), :, :, cols], self.got1.at[j - 1], self.r1, dev(x_=xp(j)))
            else:
                for j in FAR_Z:
                    share(self.buf.at[:, zp(j), :, cols], self.got1.at[j - 1], self.r1, dev(z_=zp(j)))

        def mid(self):
            wait_for(self.got1, self.r1)
            count = NZ if self.axis == "z" else NX

            @pl.loop(0, count, unroll=True)
            def _(i):
                if self.axis == "z":
                    total = self.buf[x, i, :, self.cols].astype(F32)
                else:
                    total = self.buf[i, z, :, self.cols].astype(F32)
                for j in range(self.got1.shape[0]):
                    total += self.got1[j, i].astype(F32)
                if self.owners:
                    self.mine[i, 0] = total[0:4].astype(BF16)
                    self.mine[i, 1] = total[4:8].astype(BF16)
                else:
                    self.mine[i] = total.astype(BF16)

            if not self.owners:
                for j in FAR_Z if self.axis == "z" else FAR_X:
                    if self.axis == "z":
                        share(self.mine.at[zp(j)], self.got2.at[j - 1], self.r2, dev(z_=zp(j)))
                    else:
                        share(self.mine.at[xp(j)], self.got2.at[j - 1], self.r2, dev(x_=xp(j)))
                return
            for j in (*FAR_Z, 0) if self.axis == "z" else (*FAR_X, 0):
                for b in range(2):
                    if self.axis == "z":
                        src, to_dev = self.mine.at[zp(j), b], dev(yh_=b, z_=zp(j), c_=yh)
                    else:
                        src, to_dev = self.mine.at[xp(j), b], dev(yh_=b, x_=xp(j), c_=yh)
                    if j > 0:
                        send(src, self.got2.at[c, j], self.s2, self.r2, to_dev)
                        continue
                    here = native & (yh == b)

                    @pl.when(here)
                    def _(src=src, j=j):
                        keep(src, self.got2.at[c, j], self.r2)

                    @pl.when(jnp.logical_not(here))
                    def _(src=src, j=j, to_dev=to_dev):
                        send(src, self.got2.at[c, j], self.s2, self.r2, to_dev)

        def end(self):
            if not self.owners:
                wait_for(self.got2, self.r2)
            if self.owners:
                for hc in range(2):
                    total = fr[hc, :, self.cols]
                    for j in range(self.got2.shape[1]):
                        total += self.got2[hc, j].astype(F32)
                    first = self.cols.start
                    m = first // HALF
                    lo = first - m * HALF + hc * HALF
                    (gg_out, gu_out, gd_out)[m][:, lo : lo + self.cols.stop - first] = total
                return None
            total = self.mine[z if self.axis == "z" else x].astype(F32)
            for j in range(self.got2.shape[0]):
                total += self.got2[j].astype(F32)
            return total

    assert 3 * (NX - 1) * 8 * 128 == 8 * W3
    z1_bytes = 3 * (NZ - 1) * 8 * 256 * 2
    matrix_bytes = (NX - 1) * NZ * 8 * 256 * 2 + (NZ - 1) * NX * 8 * 128 * 2

    def gathers(buf, matrices, x1_shared, z1_shared, all2_shared):
        x1 = sems.take() if x1_shared else None
        z1 = sems.take() if z1_shared else None
        r2 = sems.take() if all2_shared else None
        out, ends = {}, []
        for pair in matrices:
            mine = r2 if all2_shared else sems.take()
            ends.append(mine)
            for s in pair:
                one = z1 if s[2] == "z" else x1
                out[s] = Gather(buf, s, sems.take() if one is None else one, mine)
        return out, x1, z1, ends

    def end_matrix(ends, m):
        wait_bytes(matrix_bytes, ends[m])

    sv_g, sv_x1, _, sv_ends = gathers(sv_all, SAVED, True, False, False)
    in_g, in_x1, in_z1, in_ends = gathers(in_all, COARSE, True, True, True)
    c_g, _, _, c_ends = gathers(c_all, FINE, False, False, False)
    sc1 = {s: Scatter(s1, s, rs1[i]) for i, s in enumerate(STREAMS)}
    own_send = sems.take()
    own_recv = {s: sem for pair, sem in zip(FINE, sems.many(3)) for s in pair}
    sc2 = {s: Scatter(s2, s, rs2[i], (own_send, own_recv[s])) for i, s in enumerate(STREAMS)}

    with jax.named_scope("w_rows"):
        for b in range(2):
            wait_for(stage.at[0, 3:6], w_recv[1][b])

    def eight(first):
        return jnp.concatenate(
            [jnp.concatenate([stage[b, m].astype(F32) for m in range(first, first + 3)], axis=1) for b in range(2)],
            axis=0,
        )

    saved8 = eight(3)
    sv_all[x, z] = saved8.astype(BF16)
    for s in sum(SAVED, ()):
        sv_g[s].start()
    for b in range(2):
        wait_for(stage.at[0, 0:3], w_recv[0][b])
    init8 = eight(0)
    in_all[x, z] = init8.astype(BF16)
    sq_x[x, :, 0:W3] = jnp.sum(init8 * init8, axis=0, keepdims=True)
    sq_x[x, :, W3:] = jnp.sum(saved8 * saved8, axis=0, keepdims=True)
    sq_s1, sq_r1, sq_s2, sq_r2 = sems.many(4)
    for j in range(1, NX):
        send(sq_x.at[x], sq_x.at[x], sq_s1, sq_r1, dev(x_=xp(j)))
    at_end.append((sq_x.at[0 : NX - 1], sq_s1))

    with jax.named_scope("w_tok1"):
        tok_forward(0)
        tok_forward(1)
    with jax.named_scope("w_sv_mid"):
        wait_for(sq_x.at[0 : NX - 1], sq_r1)
        sq_z[z] = sq_x[0] + sq_x[1] + sq_x[2] + sq_x[3]
        for j in FAR_Z:
            send(sq_z.at[z], sq_z.at[z], sq_s2, sq_r2, dev(z_=zp(j)))
        at_end.append((sq_z.at[0 : NZ - 1], sq_s2))
        wait_bytes(2 * (NX - 1) * 8 * 128 * 2, sv_x1)
        for s in [pair[1] for pair in SAVED[:2]] + [pair[0] for pair in SAVED]:
            sv_g[s].mid(s[2] == "x")

    def permuted(src, dst):
        dst[...] = dot(src[...].reshape(TT, HD), p2[...]).astype(BF16)

    with jax.named_scope("w_tok2"):
        tok_ready(0)
        tok_ready(1)
    permuted(tq, qp)
    permuted(to, op)
    gains_nat = tm[0, 0:1, :]
    gcol = jnp.concatenate([column(gains_nat[:, 0:TB]), column(gains_nat[:, TB:])], axis=0)
    gp[...] = jnp.sum(p2[...].astype(F32) * gcol, axis=0, keepdims=True)
    with jax.named_scope("w_tok3"):
        tok_forward(2)

    with jax.named_scope("w_sq"):
        wait_for(sq_z.at[0 : NZ - 1], sq_r2)
    total = sq_z[0]
    for j in range(1, NZ):
        total += sq_z[j]
    norms = jnp.sqrt(total + 1e-06)
    norm_i, norm_s = norms[:, 0:W3], norms[:, W3:]
    vecs[0:1, :] = norm_i / norm_s
    vecs[1:2, :] = norm_i / (norm_s * norm_s * norm_s)
    vecs[2:3, :] = 1.0 / (norm_i * norm_s)

    def normalize(m):
        cols = slice(m * HALF, (m + 1) * HALF)
        ratio = vecs[0:1, cols]

        def body(i, rows):
            nrm[rows, cols] = (block(sv_all, i, cols) * ratio).astype(BF16)

        loop16(body)

    c_0, c_1, c_2 = (slice(m * HALF, (m + 1) * HALF) for m in range(3))
    c_01 = slice(0, 2 * HALF)

    with jax.named_scope("w_sv_gate"):
        end_matrix(sv_ends, 0)
    for s in sum(COARSE, ()):
        in_g[s].start()
    normalize(0)
    f_a[...] = dot(qp[...], nrm[:, c_0])
    with jax.named_scope("w_sv_up"):
        end_matrix(sv_ends, 1)
    normalize(1)
    f_b[...] = dot(qp[...], nrm[:, c_1])

    def q_body(i, rows):
        v = f_a[rows, :]
        up = f_b[rows, :]
        s = jax.nn.sigmoid(v)
        a = v * s
        act[rows, :] = a
        ups[rows, :] = up * (s * (1.0 + v * (1.0 - s)))
        qh[rows, :] = (a * up).astype(BF16)

    loop16(q_body)
    with jax.named_scope("w_sv_down"):
        wait_bytes((NX - 1) * NZ * 8 * HALF * 2, sv_ends[2])
    normalize(2)
    ap[...] = dot(qh[...], nrm[:, c_2], NT)
    aprs = sems.take()
    share(ap, apr, aprs, sibling)

    gains = gp[...]
    with jax.named_scope("w_ap"):
        wait_for(apr, aprs)
    for b in range(2):
        rows = slice(b * TB, (b + 1) * TB)
        out = ap[rows, :] + apr[rows, :]
        ao[rows, :] = out
        ss[0:1, rows] = row_of(jnp.sum(out * out, axis=1, keepdims=True))
        ss[1:2, rows] = row_of(jnp.sum(out * gains * op[rows, :].astype(F32), axis=1, keepdims=True))
    ss_r = sems.take()
    for j in range(1, 4):
        a, b = plane(j)
        share(ss, sr.at[j - 1], ss_r, dev(yh_=a, yl_=b))
    with jax.named_scope("w_in_mid"):
        wait_for(x1_ref, in_x1)
        wait_bytes(z1_bytes, in_z1)
        for s in sum(COARSE, ()):
            in_g[s].mid(True)
    with jax.named_scope("w_tok4"):
        tok_ready(2)
    permuted(tk, kp)
    permuted(tv, vp)

    with jax.named_scope("w_sums"):
        wait_for(sr, ss_r)
    tot = ss[...] + sr[0] + sr[1] + sr[2]
    full = HEADS * HD
    root_row = jnp.sqrt(tot[0:1, :] / full + 1e-05)
    inv_row = 1.0 / root_row
    fac_row = (tot[1:2, :] / full) / (root_row * root_row * root_row)
    for b in range(2):
        rows = slice(b * TB, (b + 1) * TB)
        inv = column(inv_row[:, rows])
        fac = column(fac_row[:, rows])
        od[rows, :] = (gains * op[rows, :].astype(F32) * inv - ao[rows, :] * fac).astype(BF16)

    def project(m, grad):
        cols = slice(m * HALF, (m + 1) * HALF)
        agr[...] = grad

        def step(i, carry):
            return carry + block(sv_all, i, cols) * agr[pl.ds(pl.multiple_of(i * 16, 16), 16), :]

        part = jnp.sum(lax.fori_loop(0, 16, step, jnp.zeros((16, HALF), F32), unroll=4), axis=0, keepdims=True)
        ratio = vecs[0:1, cols]
        fall = part * vecs[1:2, cols]
        vecs[3:4, cols] = part * vecs[2:3, cols]

        def body(i, rows):
            set_block(s1, i, cols, agr[rows, :] * ratio - block(sv_all, i, cols) * fall)

        loop16(body)

    project(2, dot(od[...], qh[...], TN))
    for s in FINE[2]:
        sc1[s].start()
    f_a[...] = dot(od[...], nrm[:, c_2])

    def d_body(i, rows):
        dh = f_a[rows, :]
        dgu[rows, 0:HALF] = (dh * ups[rows, :]).astype(BF16)
        dgu[rows, HALF : 2 * HALF] = (dh * act[rows, :]).astype(BF16)

    loop16(d_body)
    project(0, dot(qp[...], dgu[:, 0:HALF], TN))
    for s in FINE[0]:
        sc1[s].start()
    project(1, dot(qp[...], dgu[:, HALF : 2 * HALF], TN))
    for s in FINE[1]:
        sc1[s].start()

    give_send, give_recv = sems.many(2)

    class Give:
        def __init__(self, bufs, scale):
            self.part, self.got, self.out, self.back = bufs
            self.scale = scale
            self.r1 = sems.take()
            self.s2, self.r2 = give_send, give_recv

        def first(self, part):
            self.part[...] = part.reshape(2, TB, HD)

        def start(self, part, more=False):
            part = part.reshape(2, TB, HD)
            self.part[...] = self.part[...] + part if more else part
            share(self.part.at[1 - c], self.got, self.r1, sibling)

        def finish(self):
            wait_for(self.got, self.r1)
            total = self.part[c] + self.got[...]
            if self.scale:
                total = total * column(tm[c, 1:2, 0:TB])
            self.out[...] = dot(total.astype(BF16), p2[...], NT).astype(BF16)

            @pl.when(native)
            def _():
                keep(self.out, self.back, self.r2)

            @pl.when(foreign)
            def _():
                send(self.out, self.back, self.s2, self.r2, swapped)

    give_q, give_k, give_v = (Give(rets[i], i == 2) for i in range(3))
    give_q.start(dot(dgu[...], nrm[:, c_01], NT))
    with jax.named_scope("w_sc1_mid"):
        for s in (DOWN_1, GATE_1, DOWN_X, UP_1, GATE_X, UP_X):
            sc1[s].mid()
    with jax.named_scope("w_in_end"):
        wait_bytes(3 * matrix_bytes, in_ends[0])
    ini[...] = in_all[...].reshape(HD, W3)
    f_a[...] = dot(kp[...], ini[:, c_0])
    f_b[...] = dot(kp[...], ini[:, c_1])
    f_c[...] = dot(vp[...], ini[:, c_2])

    def k_body(i, rows):
        v = f_a[rows, :]
        up = f_b[rows, :]
        proj = f_c[rows, :]
        s = jax.nn.sigmoid(v)
        a = v * s
        slope = s * (1.0 + v * (1.0 - s))
        bend = s * (1.0 - s) * (2.0 + v * (1.0 - 2.0 * s))
        k_act[rows, :] = a
        kc1[rows, :] = up * slope
        kc2[rows, :] = proj * slope
        kc3[rows, :] = proj * up * bend
        kh[rows, :] = (a * up).astype(BF16)
        rise[rows, 0:HALF] = (proj * up * slope).astype(BF16)
        rise[rows, HALF : 2 * HALF] = (proj * a).astype(BF16)

    loop16(k_body)
    for s in (DOWN_X, DOWN_1, GATE_1, GATE_X, UP_1, UP_X):
        with jax.named_scope("w_sc1_end"):
            res = sc1[s].end()
        cols = slice(s[0], s[0] + s[1])
        c_all[x, z, :, cols] = res.astype(BF16)
        c_g[s].start()
        fs[0, :, cols] = res[0:4]
        fs[1, :, cols] = res[4:8]

    f_send, f_recv = sems.many(2)
    for hc in range(2):

        @pl.when(c == hc)
        def _(hc=hc):
            @pl.when(native)
            def _():
                keep(fs.at[yh], fr.at[hc], f_recv)

            @pl.when(foreign)
            def _():
                send(fs.at[yh], fr.at[hc], f_send, f_recv, sibling)

            send(fs.at[1 - yh], fr.at[hc], f_send, f_recv, dev(yh_=1 - yh, c_=yh))

    give_q.finish()
    with jax.named_scope("w_c_mid"):
        for s in (DOWN_X, GATE_X, DOWN_1, UP_X, GATE_1, UP_1):
            c_g[s].mid()

    def cot_of(m):
        cols = slice(m * HALF, (m + 1) * HALF)
        cot[:, cols] = c_all[:, :, :, cols].reshape(HD, HALF)
        return cot[:, cols]

    with jax.named_scope("w_c_down"):
        end_matrix(c_ends, 2)
    f_c[...] = dot(vp[...], cot_of(2))
    give_v.first(dot(kh[...], cot[:, c_2], NT))
    with jax.named_scope("w_c_gate"):
        end_matrix(c_ends, 0)
    f_a[...] = dot(kp[...], cot_of(0))
    def up_body(i, rows):
        bk[rows, HALF : 2 * HALF] = (f_a[rows, :] * kc2[rows, :] + f_c[rows, :] * k_act[rows, :]).astype(BF16)

    loop16(up_body)

    def inner(m, grad):
        cols = slice(m * HALF, (m + 1) * HALF)
        extra = vecs[3:4, cols]
        agr[...] = grad

        def body(i, rows):
            set_block(s2, i, cols, agr[rows, :] + ini[rows, cols].astype(F32) * extra)

        loop16(body)

    inner(1, dot(kp[...], bk[:, HALF : 2 * HALF], TN))
    for s in FINE[1]:
        sc2[s].start()
    give_k.first(dot(rise[:, 0:HALF], cot[:, c_0], NT))
    with jax.named_scope("w_c_up"):
        end_matrix(c_ends, 1)
    f_b[...] = dot(kp[...], cot_of(1))

    def b_body(i, rows):
        bg = f_a[rows, :]
        bu = f_b[rows, :]
        c1 = kc1[rows, :]
        bp[rows, :] = (bg * c1 + bu * k_act[rows, :]).astype(BF16)
        bk[rows, 0:HALF] = (bg * kc3[rows, :] + (bu * kc2[rows, :] + f_c[rows, :] * c1)).astype(BF16)

    loop16(b_body)
    inner(2, dot(vp[...], bp[...], TN))
    for s in FINE[2]:
        sc2[s].start()
    inner(0, dot(kp[...], bk[:, 0:HALF], TN))
    for s in FINE[0]:
        sc2[s].start()
    give_v.start(dot(bp[...], ini[:, c_2], NT), True)
    give_k.start(dot(rise[:, HALF:], cot[:, c_1], NT) + dot(bk[...], ini[:, c_01], NT), True)
    with jax.named_scope("w_give_v"):
        give_v.finish()
    with jax.named_scope("w_give_k"):
        give_k.finish()
    with jax.named_scope("w_sc2_mid"):
        for s in (UP_1, DOWN_1, UP_X, GATE_1, DOWN_X, GATE_X):
            sc2[s].mid()
    wait_for(fr, f_recv)

    def rows_out(m):
        wait_bytes(2 * (NZ * 4 * 256 * 2 + NX * 4 * 128 * 2), own_recv[FINE[m][0]])
        for s in FINE[m]:
            sc2[s].end()

    with jax.named_scope("w_sc2_end"):
        rows_out(1)
        rows_out(2)
    with jax.named_scope("w_collect"):
        wait_bytes(3 * TB * HD * 2, give_recv)
        for give, out in ((give_q, gq_out), (give_k, gk_out), (give_v, gv_out)):
            out[...] = give.back[...]
    with jax.named_scope("w_sc2_end"):
        rows_out(0)

    assert sum(sent_bytes) % 4096 == 0 and sum(sent_bytes) // 512 <= SENT_ROWS
    with jax.named_scope("w_sent"):
        wait_for(sent.at[0 : sum(sent_bytes) // 512], shared_sem)
        for ref, sem in at_end:
            wait_for(ref, sem)

        @pl.when(native)
        def _():
            wait_for(stage.at[0], w_send)
            wait_for(fr.at[0], f_send)
            wait_for(own_bytes, own_send)

        @pl.when(foreign)
        def _():
            wait_bytes(2 * 6 * 4 * HALF * 2, w_send)
            wait_bytes(sum(group_bytes), tok_send)
            wait_for(fr, f_send)
            wait_bytes(3 * TB * HD * 2, give_send)
            wait_bytes(3 * 2 * (NZ * 4 * 256 * 2 + NX * 4 * 128 * 2), own_send)


def write_out(*refs):
    sem = refs[-1]
    half = (len(refs) - 1) // 2
    copies = [pltpu.make_async_copy(refs[i], refs[half + i], sem.at[i]) for i in range(half)]
    for cp in copies:
        cp.start()
    for cp in copies:
        cp.wait()


def local(*args):
    (queries, key_rows, value_rows, out_grad, step_sizes, norm_gain, gate_init, up_init, down_init,
     gate_saved, up_saved, down_saved) = args
    ins = [a[0] for a in (queries, key_rows, value_rows, out_grad)]
    ins += [step_sizes, norm_gain]
    ins += [a[0] for a in (gate_init, up_init, down_init, gate_saved, up_saved, down_saved)]
    shapes = [((TB, HD), BF16)] * 3 + [((4, HID), F32)] * 3

    def v(dtype, *shape):
        return pltpu.VMEM(shape, dtype)

    def rs_bufs(owners):
        out = []
        for _, n, axis in STREAMS:
            if axis == "z":
                first, count = v(BF16, NX - 1, NZ, 8, n), NZ
            else:
                first, count = v(BF16, NZ - 1, NX, 8, n), NX
            if owners:
                out += [first, v(BF16, count, 2, 4, n), v(BF16, 2, count, 4, n)]
            else:
                out += [first, v(BF16, count, 8, n), v(BF16, count - 1, 8, n)]
        return out

    ret = [v(F32, 2, TB, HD), v(F32, TB, HD), v(BF16, TB, HD), v(BF16, TB, HD)]
    scratch = [
        pltpu.SemaphoreType.DMA((N_SEMS,)),
        *[v(a.dtype, *a.shape) for a in ins[:6]],
        *[v(BF16, 4, HID)] * 6,
        v(BF16, 2, 6, 4, HALF), v(F32, 8, HD), v(BF16, TB, HD),
        *[v(BF16, 2, TB, HD)] * 4, v(F32, 2, 8, HD),
        *[v(BF16, TT, HD)] * 4, v(F32, 1, HD),
        *[v(BF16, NX, NZ, 8, W3)] * 3,
        v(F32, NZ, 1, 2 * W3), v(F32, NX, 1, 2 * W3), v(BF16, HD, HD),
        v(BF16, HD, W3), v(BF16, HD, W3), v(F32, 8, W3), v(BF16, HD, W3),
        *[v(F32, TT, HALF)] * 5, v(BF16, TT, HALF), v(BF16, TT, 2 * HALF),
        *[v(F32, TT, HD)] * 3, v(F32, 8, TT), v(F32, 3, 8, TT), v(BF16, TT, HD), v(F32, HD, HALF),
        *[v(BF16, NX, NZ, 8, W3)] * 2,
        *rs_bufs(False), *rs_bufs(True),
        *[v(F32, TT, HALF)] * 4, v(BF16, TT, HALF), v(BF16, TT, 2 * HALF), v(BF16, TT, 2 * HALF), v(BF16, TT, HALF),
        *ret * 3,
        v(F32, 2, 4, W3), v(F32, 2, 4, W3), v(F32, SENT_ROWS, 128),
        v(BF16, 8, W3), v(F32, 111, 2, 128),
    ]
    vm = pl.BlockSpec(memory_space=pltpu.VMEM)
    res = pl.pallas_call(
        kernel,
        out_shape=[pltpu.VMEM(s, d) for s, d in shapes],
        in_specs=[pl.BlockSpec(memory_space=pltpu.HBM)] * len(ins),
        out_specs=[vm] * len(shapes),
        scratch_shapes=scratch,
        compiler_params=pltpu.CompilerParams(
            collective_id=0, has_side_effects=True, vmem_limit_bytes=60 * 1024 * 1024
        ),
    )(*[pltpu.with_memory_space_constraint(a, pltpu.HBM) for a in ins])
    res = pl.pallas_call(
        write_out,
        out_shape=[jax.ShapeDtypeStruct(s, d) for s, d in shapes],
        in_specs=[vm] * len(shapes),
        out_specs=[pl.BlockSpec(memory_space=pl.ANY)] * len(shapes),
        scratch_shapes=[pltpu.SemaphoreType.DMA((len(shapes),))],
    )(*[pltpu.with_memory_space_constraint(r, pltpu.VMEM) for r in res])
    return tuple(r[None] for r in res)


def solution(mesh):
    three = P("head", "seq", None)
    return jax.shard_map(
        local,
        mesh=mesh,
        in_specs=(three, three, three, three, P("head", "seq"), P("head", None)) + (three,) * 6,
        out_specs=(three,) * 6,
        check_vma=False,
    )
```
